32 devices in a mesh: gx: 4 (over z), gy: 4 (over x, core), ma: 2 (over y).
Axes of the slice: x: 2, y: 2, z: 4, core: 2. Of those that a mesh axis runs over, the one named last changes fastest.
Arguments:
- right_side: float32 [128, 128, 4, 256], P('gx', 'gy', None, 'ma'), may hold values from -6 to 6
- start_field: float32 [128, 128, 4, 256], P('gx', 'gy', None, 'ma'), may hold values from -1.8 to 1.8
- coefficients: float32 [3, 128, 128, 4], P(None, 'gx', 'gy'), may hold values from -0.8 to 3, as said below
- couplings: float32 [3, 256, 256], replicated, may hold values from -0.25 to 2.25, as said below
Outputs:
- solution_field: float32 [128, 128, 4, 256], P('gx', 'gy', None, 'ma')
- residual: float32 [128, 128, 4, 256], P('gx', 'gy', None, 'ma')
The draws below stay inside these ranges and needn't reach their ends.
Inputs may be any that keep to these rules, and one draw needn't show every extreme that they name: coefficients[0] lies between 1 and 3, coefficients[1] and coefficients[2] between -0.8 and 0.8. couplings[0] is 2 on its diagonal plus entries of size about 256 ** -0.5; couplings[1] and couplings[2] have entries of size about 256 ** -0.5.
All inputs are finite; a program needn't handle non-finite values.
Results may differ from the reference program's by a relative error of at most 0.00016.
Values sent between devices are 32-bit elements; how exact they have to be, the bound alone decides.
No kernel may reach another device: no remote copies, remote signals or barrier semaphores. Data moves between devices by JAX's collectives and lax.ppermute only.
A program may use at most 128 MiB of HBM per device.

```python
import jax
import jax.numpy as jnp
from jax import lax

P_SIZE = 256
NZ = 4
NX = 128
NY = 128


def draw_coefficients(key, part):
    key_mean, key_one, key_two = jax.random.split(key, 3)
    shape = (NX, NY, NZ)
    mean_field = jax.random.uniform(key_mean, shape, jnp.float32, 1.0, 3.0)
    first_field = jax.random.uniform(key_one, shape, jnp.float32, -0.8, 0.8)
    second_field = jax.random.uniform(key_two, shape, jnp.float32, -0.8, 0.8)
    return jnp.stack([mean_field, first_field, second_field], axis=0)


def draw_couplings(key, part):
    shape = (3, P_SIZE, P_SIZE)
    entries = jnp.clip(jax.random.normal(key, shape, jnp.float32), -4.0, 4.0)
    entries = entries / jnp.sqrt(jnp.float32(P_SIZE))
    diagonal = 2.0 * jnp.eye(P_SIZE, dtype=jnp.float32)
    return entries + jnp.stack([diagonal, jnp.zeros_like(diagonal), jnp.zeros_like(diagonal)], axis=0)


def level_of(own_key, dims, cuts, least, high):
    loudness, own = 1.0, jax.random.fold_in(own_key, 6)
    for axis_at, parts in cuts:
        steps = jnp.exp(jax.random.uniform(jax.random.fold_in(own, axis_at), (parts,), jnp.float32, least / len(cuts), high / len(cuts)))
        loudness = loudness * jnp.repeat(steps, dims[axis_at] // parts).reshape([-1 if axis == axis_at else 1 for axis in range(len(dims))])
    return loudness


def noise(stream_key, shape, width, limit, cuts=(), kind=jnp.bfloat16):
    result = jax.random.normal(stream_key, shape, jnp.float32) * width
    if len(cuts) > 0:
        result = level_of(stream_key, shape, cuts, -0.22, 0.18) * result
    return jnp.clip(result, min=-limit, max=limit).astype(kind)


def setup_inputs(seed: int = 0) -> dict:
    arg_keys = jax.random.split(jax.random.key(seed), 5)
    return {
        "right_side": noise(arg_keys[0], (NX, NY, NZ, P_SIZE), 1.0, 6.0, ((0, 4), (1, 4), (3, 2)), jnp.float32),
        "start_field": noise(arg_keys[1], (NX, NY, NZ, P_SIZE), 0.3, 1.8, ((0, 4), (1, 4), (3, 2)), jnp.float32),
        "coefficients": draw_coefficients(jax.random.fold_in(arg_keys[4], 71), 0),
        "couplings": draw_couplings(jax.random.fold_in(arg_keys[4], 71), 0),
    }


step_size = 0.02


def moved(array, offset_x, offset_y, offset_z):
    size_x, size_y, size_z = array.shape[0], array.shape[1], array.shape[2]
    return array[1 + offset_x:size_x - 1 + offset_x, 1 + offset_y:size_y - 1 + offset_y, 1 + offset_z:size_z - 1 + offset_z]


def stencil(field_pad, coef_pad):
    center = moved(field_pad, 0, 0, 0)
    coef_center = moved(coef_pad, 0, 0, 0)
    total = jnp.zeros(center.shape, jnp.float32)
    for offsets in ((1, 0, 0), (-1, 0, 0), (0, 1, 0), (0, -1, 0), (0, 0, 1), (0, 0, -1)):
        neighbour = moved(field_pad, offsets[0], offsets[1], offsets[2])
        face = 0.5 * (coef_center + moved(coef_pad, offsets[0], offsets[1], offsets[2]))
        total = total + face[..., None] * (center - neighbour)
    return total


def pad_grid(array):
    widths = [(1, 1), (0, 0), (1, 1)] + [(0, 0)] * (array.ndim - 3)
    padded = jnp.pad(array, widths)
    return jnp.concatenate([padded[:, -1:], padded, padded[:, :1]], axis=1)


def operator(field, coef_pads, couplings):
    field_pad = pad_grid(field)
    total = jnp.zeros((field.shape[0] * field.shape[1] * field.shape[2], P_SIZE), jnp.float32)
    for index in range(3):
        applied = stencil(field_pad, coef_pads[index]).reshape(-1, P_SIZE)
        total = total + jnp.dot(applied, couplings[index].T, precision=lax.Precision.HIGHEST, preferred_element_type=jnp.float32)
    return total.reshape(field.shape)


def reference(right_side, start_field, coefficients, couplings):
    coef_pads = [pad_grid(coefficients[index]) for index in range(3)]
    first = start_field + step_size * (right_side - operator(start_field, coef_pads, couplings))
    residual = right_side - operator(first, coef_pads, couplings)
    solution_field = first + step_size * residual
    return solution_field, residual
```

```python
import functools

import jax
import jax.numpy as jnp
from jax import lax
from jax.experimental import pallas as pl
from jax.experimental.pallas import tpu as pltpu
from jax.sharding import PartitionSpec as P

step_size = 0.02
lanes = 128
group = 2
pad = 8
vmem_bytes = 28 * 1024 * 1024
f32 = jnp.float32
bf16 = jnp.bfloat16
whole = pl.BlockSpec(memory_space=pltpu.VMEM)
anywhere = pl.BlockSpec(memory_space=pl.ANY)


def call(body, out_shapes, scratch, flops=0, size=0, in_specs=None, out_specs=None, aliases=None, name=None):
    return pl.pallas_call(
        body,
        out_shape=[jax.ShapeDtypeStruct(shape, kind) for shape, kind in out_shapes],
        in_specs=in_specs,
        out_specs=out_specs if out_specs is not None else [whole] * len(out_shapes),
        scratch_shapes=scratch,
        input_output_aliases=aliases or {},
        cost_estimate=pl.CostEstimate(flops=flops, bytes_accessed=size, transcendentals=0),
        compiler_params=pltpu.CompilerParams(vmem_limit_bytes=vmem_bytes),
        name=name,
    )


def sent(array, axis, step, periodic):
    count = lax.axis_size(axis)
    pairs = [(i, (i + step) % count) for i in range(count) if periodic or 0 <= i + step < count]
    return lax.ppermute(array, axis, pairs)


def weights_body(half_ref, couplings_ref, own_hi, own_lo, other_hi, other_lo, turned):
    half = half_ref[0]
    modes = own_hi.shape[1] // 2
    for field in range(3):
        mine = couplings_ref[field, pl.ds(pl.multiple_of(half * modes, modes), modes), :]
        theirs = couplings_ref[field, pl.ds(pl.multiple_of((1 - half) * modes, modes), modes), :]
        turned[:, :modes] = mine.T
        turned[:, modes:] = theirs.T
        own = turned[pl.ds(pl.multiple_of(half * modes, modes), modes), :]
        other = turned[pl.ds(pl.multiple_of((1 - half) * modes, modes), modes), :modes]
        rows = pl.ds(field * modes, modes)
        top = own.astype(bf16)
        own_hi[rows, :] = top
        own_lo[rows, :] = (own - top.astype(f32)).astype(bf16)
        top = other.astype(bf16)
        other_hi[rows, :] = top
        other_lo[rows, :] = (other - top.astype(f32)).astype(bf16)


def neighbours(padded, plane, start, size, depth):
    row = pad + start
    z = lax.broadcasted_iota(jnp.int32, (size, lanes), 0) % depth
    middle = plane + 1
    here = padded[middle, row : row + size, :]
    low_z = jnp.where(z == 0, 0.0, padded[middle, row - 1 : row - 1 + size, :])
    high_z = jnp.where(z == depth - 1, 0.0, padded[middle, row + 1 : row + 1 + size, :])
    return here, (
        padded[plane + 2, row : row + size, :],
        padded[plane, row : row + size, :],
        padded[middle, row + depth : row + depth + size, :],
        padded[middle, row - depth : row - depth + size, :],
        high_z,
        low_z,
    )


def fill_strips(padded, low, high, first, count, depth, source=0):
    rows = padded.shape[1] - 2 * pad

    def one(i, _):
        padded[first + i + 1, pad - depth : pad, :] = low[source + i]
        padded[first + i + 1, pad + rows : pad + rows + depth, :] = high[source + i]
        return 0

    lax.fori_loop(0, count, one, 0)


def faces_body(depth, coef, low_x, high_x, low_y, high_y, faces, padded, sem):
    count, rows = coef.shape[0], coef.shape[1]
    copy = pltpu.make_async_copy(coef, padded.at[pl.ds(1, count), pl.ds(pad, rows), :], sem)
    copy.start()
    padded[0, pad : pad + rows, :] = low_x[...]
    padded[count + 1, pad : pad + rows, :] = high_x[...]
    fill_strips(padded, low_y, high_y, 0, count, depth)
    copy.wait()
    size = 32

    def one(plane, _):
        lane = lax.broadcasted_iota(jnp.int32, (size, lanes), 1)
        for start in range(0, rows, size):
            here, beside = neighbours(padded, plane, start, size, depth)
            chosen = beside[5]
            for direction in range(4, -1, -1):
                chosen = jnp.where(lane < 3 * (direction + 1), beside[direction], chosen)
            faces[plane, start : start + size, :] = 0.5 * (here + chosen)
        return 0

    lax.fori_loop(0, count, one, 0)


def products(padded, faces, plane_of, face_of, step, depth, upper, lower, hi, lo):
    size = 32
    rows = padded.shape[1] - 2 * pad
    for j in range(group):
        plane = plane_of(step * group + j)
        face_plane = face_of(step * group + j)
        for start in range(0, rows, size):
            here, beside = neighbours(padded, plane, start, size, depth)
            face = faces[face_plane, start : start + size, :]
            moved = [here - value for value in beside]
            for field in range(3):
                total = face[:, field : field + 1] * moved[0]
                for direction in range(1, 6):
                    at = 3 * direction + field
                    total = total + face[:, at : at + 1] * moved[direction]
                top = total.astype(bf16)
                where = slice(j * rows + start, j * rows + start + size), slice(field * lanes, (field + 1) * lanes)
                upper[where] = top
                lower[where] = (total - top.astype(f32)).astype(bf16)
    big, small = upper[...], lower[...]
    out = jnp.dot(big, hi[...], preferred_element_type=f32)
    out = out + jnp.dot(big, lo[...], preferred_element_type=f32)
    return out + jnp.dot(small, hi[...], preferred_element_type=f32)


def first_body(depth, begin, count, sent_from, field, right, low_x, high_x, low_y, high_y, faces, hi, lo, rest, part, padded, upper, lower, sem):
    planes, rows = field.shape[0], field.shape[1]
    copy = pltpu.make_async_copy(field, padded.at[pl.ds(1, planes), pl.ds(pad, rows), :], sem)
    copy.start()
    padded[0, pad : pad + rows, :] = low_x[...]
    padded[planes + 1, pad : pad + rows, :] = high_x[...]
    fill_strips(padded, low_y, high_y, 0, planes, depth)
    copy.wait()

    def one(step, _):
        place = lambda i: begin + i
        out = products(padded, faces, place, place, step, depth, upper, lower, hi, lo)
        for j in range(group):
            at = step * group + j
            mine = out[j * rows : (j + 1) * rows]
            rest[at] = right[begin + at] - mine[:, :lanes]

            @pl.when(at >= sent_from)
            def _():
                part[at - sent_from] = mine[:, lanes:]

        return 0

    lax.fori_loop(0, count // group, one, 0)


def middle_body(depth, taken, other, low_y, high_y, faces, rest_a, rest_b, came, hi, lo, residual, low, high, edge, padded, upper, lower, sem):
    held, rows = other.shape[0], other.shape[1]
    copy = pltpu.make_async_copy(other, padded.at[pl.ds(0, held), pl.ds(pad, rows), :], sem)
    copy.start()
    fill_strips(padded, low_y, high_y, -1, held, depth)

    def near(i, _):
        value = rest_a[i] - came[i]
        residual[i] = value
        low[i] = value[:depth]
        high[i] = value[rows - depth :]
        return 0

    lax.fori_loop(0, taken, near, 0)
    edge[...] = residual[0]
    copy.wait()
    count = held - 2

    def one(step, _):
        out = products(padded, faces, lambda i: i, lambda i: taken + i, step, depth, upper, lower, hi, lo)
        for j in range(group):
            at = step * group + j
            value = rest_b[at] - out[j * rows : (j + 1) * rows]
            residual[taken + at] = value
            low[taken + at] = value[:depth]
            high[taken + at] = value[rows - depth :]
        return 0

    lax.fori_loop(0, count // group, one, 0)


def last_rows_body(depth, skip, rest_b, came, residual, low, high, edge):
    rows = came.shape[1]
    count = came.shape[0]

    def one(i, _):
        value = rest_b[skip + i] - came[i]
        residual[i] = value
        low[i] = value[:depth]
        high[i] = value[rows - depth :]
        return 0

    lax.fori_loop(0, count, one, 0)
    edge[...] = residual[count - 1]


def finish(out, residual, start):
    later = residual - step_size * out
    return later, start + step_size * (residual + later)


def second_body(depth, begin, count, residual, start, low_y, high_y, faces, hi, lo, later, fields, part, padded, upper, lower, sem):
    planes, rows = residual.shape[0], residual.shape[1]
    copy = pltpu.make_async_copy(residual, padded.at[pl.ds(1, planes), pl.ds(pad, rows), :], sem)
    copy.start()
    fill_strips(padded, low_y, high_y, 0, planes, depth)
    copy.wait()

    def one(step, _):
        place = lambda i: begin + i
        out = products(padded, faces, place, place, step, depth, upper, lower, hi, lo)
        for j in range(group):
            at = step * group + j
            mine = out[j * rows : (j + 1) * rows]
            here = padded[begin + at + 1, pad : pad + rows, :]
            later[begin + at], fields[begin + at] = finish(mine[:, :lanes], here, start[begin + at])
            part[at] = mine[:, lanes:]
        return 0

    lax.fori_loop(0, count // group, one, 0)


def third_body(depth, first, residual_a, residual_b, start, low_x, high_x, low_a, high_a, low_b, high_b, faces, hi, lo, later_in, fields_in, later, fields, part, padded, upper, lower, staged, sem):
    near, far = residual_a.shape[0], residual_b.shape[0]
    rows = residual_a.shape[1]
    planes = near + far
    copies = [
        pltpu.make_async_copy(residual_a, padded.at[pl.ds(1, near), pl.ds(pad, rows), :], sem.at[0]),
        pltpu.make_async_copy(residual_b, padded.at[pl.ds(1 + near, far), pl.ds(pad, rows), :], sem.at[1]),
    ]
    for copy in copies:
        copy.start()
    padded[0, pad : pad + rows, :] = low_x[...]
    padded[planes + 1, pad : pad + rows, :] = high_x[...]
    fill_strips(padded, low_a, high_a, 0, near, depth)
    fill_strips(padded, low_b, high_b, near, far, depth)
    for copy in copies:
        copy.wait()
    count = planes - first + 1
    place = lambda i: lax.rem(first + i, planes)

    def one(step, _):
        out = products(padded, faces, place, place, step, depth, upper, lower, hi, lo)
        for j in range(group):
            at = step * group + j
            mine = out[j * rows : (j + 1) * rows]
            here = padded[place(at) + 1, pad : pad + rows, :]
            staged[0, at], staged[1, at] = finish(mine[:, :lanes], here, start[place(at)])
            part[at] = mine[:, lanes:]
        return 0

    lax.fori_loop(0, count // group, one, 0)
    outward = []
    for which, target in ((0, later), (1, fields)):
        outward.append(pltpu.make_async_copy(staged.at[which, pl.ds(0, count - 1)], target.at[pl.ds(first, count - 1)], sem.at[2 * which]))
        outward.append(pltpu.make_async_copy(staged.at[which, pl.ds(count - 1, 1)], target.at[pl.ds(0, 1)], sem.at[2 * which + 1]))
    for copy in outward:
        copy.start()
    for copy in outward:
        copy.wait()


def last_body(came, later_in, fields_in, later, fields):
    later[...] = later_in[...] - step_size * came[...]
    fields[...] = fields_in[...] - (step_size * step_size) * came[...]


def add_last(came, later, fields, first):
    count = came.shape[0]
    planes = later.shape[0]
    block = (1,) + later.shape[1:]
    moving = pl.BlockSpec(block, lambda i: (lax.rem(first + i, planes), 0, 0))
    return pl.pallas_call(
        last_body,
        grid=(count,),
        out_shape=[jax.ShapeDtypeStruct(later.shape, f32)] * 2,
        in_specs=[pl.BlockSpec(block, lambda i: (i, 0, 0)), moving, moving],
        out_specs=[moving, moving],
        input_output_aliases={1: 0, 2: 1},
        cost_estimate=pl.CostEstimate(flops=4 * came.size, bytes_accessed=20 * came.size, transcendentals=0),
        name="last",
    )(came, later, fields)


def shards(right_side, start_field, coefficients, couplings):
    nx, ny, depth, modes = start_field.shape
    rows = ny * depth
    flat = (nx, rows, modes)
    start = start_field.reshape(flat)
    right = right_side.reshape(flat)
    begin = (9 * nx) // 32
    end = nx - begin
    taken = begin + 1
    ready = end - 1
    plane = (rows, modes)

    raw = sent(lax.slice_in_dim(start_field, begin, end, axis=0), "ma", 1, True)

    half = lax.axis_index("ma").astype(jnp.int32).reshape(1)
    width = 3 * modes
    own_hi, own_lo, other_hi, other_lo = call(
        weights_body,
        [((width, 2 * modes), bf16)] * 2 + [((width, modes), bf16)] * 2,
        [pltpu.VMEM((2 * modes, 2 * modes), f32)],
        in_specs=[pl.BlockSpec(memory_space=pltpu.SMEM), whole],
        size=couplings.size * 4,
        name="weights",
    )(half, couplings)

    choose = jnp.tile(jnp.eye(3, dtype=f32), (1, 6))
    choose = jnp.pad(choose, ((0, 0), (0, lanes - 18)))
    coef = jnp.einsum("kxyz,kl->xyzl", coefficients, choose, precision=lax.Precision.HIGHEST, preferred_element_type=f32)

    both = jnp.stack([start_field, coef])
    low_x = sent(both[:, nx - 1], "gx", 1, False)
    high_x = sent(both[:, 0], "gx", -1, False)
    low_y = sent(both[:, :, ny - 1], "gy", 1, True)
    high_y = sent(both[:, :, 0], "gy", -1, True)
    low_x, high_x = low_x.reshape((2,) + plane), high_x.reshape((2,) + plane)

    padded = pltpu.VMEM((nx + 2, rows + 2 * pad, lanes), f32)
    products_scratch = [pltpu.VMEM((group * rows, width), bf16)] * 2
    flops_of = lambda count, out: 2 * 3 * count * rows * width * out
    size_of = lambda count: 4 * count * rows * lanes
    (faces,) = call(
        functools.partial(faces_body, depth),
        [(flat, f32)],
        [padded, pltpu.SemaphoreType.DMA],
        in_specs=[anywhere] + [whole] * 4,
        size=2 * size_of(nx),
        name="faces",
    )(coef.reshape(flat), low_x[1], high_x[1], low_y[1], high_y[1])

    def first(begin, count, sent_from, kind):
        return call(
            functools.partial(first_body, depth, begin, count, sent_from),
            [((count,) + plane, f32), ((count - sent_from,) + plane, f32)],
            [padded] + products_scratch + [pltpu.SemaphoreType.DMA],
            in_specs=[anywhere] + [whole] * 8,
            flops=flops_of(count, 2 * modes),
            size=3 * size_of(count),
            name=kind,
        )(start, right, low_x[0], high_x[0], low_y[0], high_y[0], faces, own_hi, own_lo)

    back = (lambda array: array)
    rest_a, part_a = first(0, taken, 0, "first_a")
    came_a = sent(part_a, "ma", 1, True)
    rest_b, part_b = first(taken, nx - taken, ready - taken, "first_b")
    came_b = sent(part_b, "ma", 1, True)

    raw_low = sent(raw[:, ny - 1], "gy", 1, True)
    raw_high = sent(raw[:, 0], "gy", -1, True)
    held = end - begin
    raw = raw.reshape((held,) + plane)
    strip = lambda count: ((count, depth, modes), f32)
    near, low_a, high_a, edge_first = call(
        functools.partial(middle_body, depth, taken),
        [((ready,) + plane, f32), strip(ready), strip(ready), (plane, f32)],
        [pltpu.VMEM((held, rows + 2 * pad, lanes), f32)] + products_scratch + [pltpu.SemaphoreType.DMA],
        in_specs=[anywhere] + [whole] * 8,
        flops=flops_of(held - 2, modes),
        size=3 * size_of(ready),
        name="middle",
    )(raw, raw_low, raw_high, faces, rest_a, rest_b, came_a, other_hi, other_lo)
    next_low_a = sent(high_a, "gy", 1, True)
    next_high_a = sent(low_a, "gy", -1, True)
    next_high_x = sent(edge_first, "gx", -1, False)

    whole_fields = [(flat, f32)] * 2
    count = ready - 2
    later, fields, part_c = call(
        functools.partial(second_body, depth, 1, count),
        whole_fields + [((count,) + plane, f32)],
        [padded] + products_scratch + [pltpu.SemaphoreType.DMA],
        in_specs=[anywhere] + [whole] * 6,
        flops=flops_of(count, 2 * modes),
        size=5 * size_of(count),
        name="second",
    )(near, start, next_low_a, next_high_a, faces, own_hi, own_lo)
    came_c = sent(part_c, "ma", 1, True)

    remaining = nx - ready
    far, low_b, high_b, edge_last = call(
        functools.partial(last_rows_body, depth, ready - taken),
        [((remaining,) + plane, f32), strip(remaining), strip(remaining), (plane, f32)],
        [],
        in_specs=[whole] * 2,
        size=3 * size_of(remaining),
        name="far",
    )(rest_b, came_b)
    next_low_b = sent(high_b, "gy", 1, True)
    next_high_b = sent(low_b, "gy", -1, True)
    next_low_x = sent(edge_last, "gx", 1, False)

    done = ready - 1
    count = nx - done + 1
    later, fields, part_d = call(
        functools.partial(third_body, depth, done),
        whole_fields + [((count,) + plane, f32)],
        [padded] + products_scratch + [pltpu.VMEM((2, count) + plane, f32), pltpu.SemaphoreType.DMA((4,))],
        in_specs=[anywhere] * 2 + [whole] * 10 + [anywhere] * 2,
        out_specs=[anywhere] * 2 + [whole],
        flops=flops_of(count, 2 * modes),
        size=5 * size_of(count),
        aliases={12: 0, 13: 1},
        name="third",
    )(near, far, start, next_low_x, next_high_x, next_low_a, next_high_a, next_low_b, next_high_b, faces, own_hi, own_lo, later, fields)
    came_d = sent(part_d, "ma", 1, True)

    later, fields = add_last(came_c, later, fields, 1)
    later, fields = add_last(came_d, later, fields, done)
    return (fields.reshape(start_field.shape), later.reshape(start_field.shape))


def solution(mesh):
    placed = (P("gx", "gy", None, "ma"), P("gx", "gy", None, "ma"), P(None, "gx", "gy", None), P())
    return jax.shard_map(
        shards,
        mesh=mesh,
        in_specs=placed,
        out_specs=(P("gx", "gy", None, "ma"), P("gx", "gy", None, "ma")),
        check_vma=False,
    )
```

```python
import functools

import jax
import jax.numpy as jnp
from jax import lax
from jax.experimental import pallas as pl
from jax.experimental.pallas import tpu as pltpu
from jax.sharding import PartitionSpec as P

step_size = 0.02
lanes = 128
group = 2
pad = 8
vmem_bytes = 12 * 1024 * 1024
f32 = jnp.float32
bf16 = jnp.bfloat16
whole = pl.BlockSpec(memory_space=pltpu.VMEM)
anywhere = pl.BlockSpec(memory_space=pl.ANY)


def call(body, out_shapes, scratch, work=1.0, in_specs=None, out_specs=None, aliases=None, name=None):
    return pl.pallas_call(
        body,
        out_shape=[jax.ShapeDtypeStruct(shape, kind) for shape, kind in out_shapes],
        in_specs=in_specs,
        out_specs=out_specs if out_specs is not None else [whole] * len(out_shapes),
        scratch_shapes=scratch,
        input_output_aliases=aliases or {},
        cost_estimate=pl.CostEstimate(flops=int(work * 1e9), bytes_accessed=int(work * 2e6), transcendentals=0),
        compiler_params=pltpu.CompilerParams(vmem_limit_bytes=vmem_bytes),
        name=name,
    )


def sent(array, axis, step, periodic):
    count = lax.axis_size(axis)
    pairs = [(i, (i + step) % count) for i in range(count) if periodic or 0 <= i + step < count]
    return lax.ppermute(array, axis, pairs)


def weights_body(couplings_ref, own_hi, own_lo, other_hi, other_lo, turned):
    half = lax.axis_index("ma")
    modes = own_hi.shape[1] // 2
    for field in range(3):
        mine = couplings_ref[field, pl.ds(pl.multiple_of(half * modes, modes), modes), :]
        theirs = couplings_ref[field, pl.ds(pl.multiple_of((1 - half) * modes, modes), modes), :]
        turned[:, :modes] = mine.T
        turned[:, modes:] = theirs.T
        own = turned[pl.ds(pl.multiple_of(half * modes, modes), modes), :]
        other = turned[pl.ds(pl.multiple_of((1 - half) * modes, modes), modes), :modes]
        rows = pl.ds(field * modes, modes)
        top = own.astype(bf16)
        own_hi[rows, :] = top
        own_lo[rows, :] = (own - top.astype(f32)).astype(bf16)
        top = other.astype(bf16)
        other_hi[rows, :] = top
        other_lo[rows, :] = (other - top.astype(f32)).astype(bf16)


def layers_body(depth, field, coef, first_x, last_x, first_y, last_y, held, sem):
    planes, rows = field.shape[0], field.shape[1]
    copy = pltpu.make_async_copy(field, held, sem)
    copy.start()
    for out in (first_x, last_x, first_y, last_y):
        out[rows : rows + coef.shape[0]] = coef[...]
        out[rows + coef.shape[0] :] = jnp.zeros((out.shape[0] - rows - coef.shape[0], lanes), f32)
    copy.wait()
    first_x[:rows] = held[0]
    last_x[:rows] = held[planes - 1]
    for plane in range(planes):
        first_y[plane * depth : (plane + 1) * depth] = held[plane, :depth]
        last_y[plane * depth : (plane + 1) * depth] = held[plane, rows - depth :]


def halves_body(coef, halves, square):
    count, rows = coef.shape[0], coef.shape[1]
    square[:count] = 0.5 * coef[...]
    square[count:] = jnp.zeros((lanes - count, rows), f32)
    columns = square[...].T
    planes = count // 3
    for plane in range(planes):
        for field in range(3):
            at = field * planes + plane
            halves[field, plane + 1, pad : pad + rows, :] = jnp.broadcast_to(columns[:, at : at + 1], (rows, lanes))


def around(ref, middle, row, size, depth):
    z = lax.broadcasted_iota(jnp.int32, (size, lanes), 0) % depth
    low = jnp.where(z != 0, ref[middle, row - 1 : row - 1 + size, :], 0.0)
    high = jnp.where(z != depth - 1, ref[middle, row + 1 : row + 1 + size, :], 0.0)
    beside = ref[middle, row - depth : row - depth + size, :] + ref[middle, row + depth : row + depth + size, :]
    return (ref[middle - 1, row : row + size, :] + ref[middle + 1, row : row + size, :]) + (beside + (low + high))


def diagonal_body(depth, low_x, high_x, low_y, high_y, halves_in, halves, diagonal):
    planes, rows = diagonal.shape[1], diagonal.shape[2]
    spread = lambda column, height: jnp.broadcast_to(column, (height, lanes))
    before = (0.5 * low_x[rows:]).T
    after = (0.5 * high_x[rows:]).T
    for field in range(3):
        at = field * planes + planes - 1
        halves[field, 0, pad : pad + rows, :] = spread(before[:, at : at + 1], rows)
        at = field * planes
        halves[field, planes + 1, pad : pad + rows, :] = spread(after[:, at : at + 1], rows)
    below = (0.5 * low_y[rows:]).T[rows - depth :]
    above = (0.5 * high_y[rows:]).T[:depth]
    for plane in range(planes):
        for field in range(3):
            at = field * planes + plane
            halves[field, plane + 1, pad - depth : pad, :] = spread(below[:, at : at + 1], depth)
            halves[field, plane + 1, pad + rows : pad + rows + depth, :] = spread(above[:, at : at + 1], depth)
    size = 32

    def one(plane, _):
        for start in range(0, rows, size):
            row = pad + start
            for field in range(3):
                here = halves[field, plane + 1, row : row + size, :]
                diagonal[field, plane, start : start + size, :] = 6.0 * here + around(halves.at[field], plane + 1, row, size, depth)
        return 0

    lax.fori_loop(0, planes, one, 0)


def weigh(padded, halves, weighed, local, first, count):
    size = (padded.shape[1]) // 3

    def one(i, _):
        for start in range(0, padded.shape[1], size):
            value = padded[local + i, start : start + size, :]
            for field in range(3):
                weighed[field, local + i, start : start + size, :] = halves[field, first + i, start : start + size, :] * value
        return 0

    lax.fori_loop(0, count, one, 0)


def stencil(padded, halves, diagonal, weighed, middle, plane, at, depth, upper, lower):
    size = 32
    rows = padded.shape[1] - 2 * pad
    for start in range(0, rows, size):
        row = pad + start
        here = padded[middle, row : row + size, :]
        total = around(padded, middle, row, size, depth)
        for field in range(3):
            value = diagonal[field, plane, start : start + size, :] * here - halves[field, plane + 1, row : row + size, :] * total
            value = value - around(weighed.at[field], middle, row, size, depth)
            where = slice(at + start, at + start + size), slice(field * lanes, (field + 1) * lanes)
            top = value.astype(bf16)
            upper[where] = top
            lower[where] = (value - top.astype(f32)).astype(bf16)


def operate(depth, count, place, scratch, halves, diagonal, hi, lo, emit):
    padded, weighed, upper_a, lower_a, upper_b, lower_b = scratch
    rows = padded.shape[1] - 2 * pad

    def fill(at, upper, lower):
        for j in range(group):
            middle, plane = place(at + j)
            stencil(padded, halves, diagonal, weighed, middle, plane, j * rows, depth, upper, lower)

    def flush(at, upper, lower):
        big, small = upper[...], lower[...]
        out = jnp.dot(big, hi[...], preferred_element_type=f32)
        out = out + jnp.dot(big, lo[...], preferred_element_type=f32)
        out = out + jnp.dot(small, hi[...], preferred_element_type=f32)
        for j in range(group):
            emit(at + j, out[j * rows : (j + 1) * rows])

    groups = count // group
    fill(0, upper_a, lower_a)

    def one(i, _):
        at = 2 * group * i
        flush(at, upper_a, lower_a)
        fill(at + group, upper_b, lower_b)
        flush(at + group, upper_b, lower_b)
        fill(at + 2 * group, upper_a, lower_a)
        return 0

    lax.fori_loop(0, (groups - 1) // 2, one, 0)
    if groups % 2:
        flush(count - group, upper_a, lower_a)
    else:
        at = count - 2 * group
        flush(at, upper_a, lower_a)
        fill(at + group, upper_b, lower_b)
        flush(at + group, upper_b, lower_b)


def strips(padded, local, count, depth, low, high, source, stacked):
    rows = padded.shape[1] - 2 * pad
    for i in range(count):
        at = slice((source + i) * depth, (source + i + 1) * depth) if stacked else source + i
        padded[local + i, pad - depth : pad, :] = low[at]
        padded[local + i, pad + rows : pad + rows + depth, :] = high[at]


def loads(pieces, padded, sem):
    rows = padded.shape[1] - 2 * pad
    copies = []
    for number, (source, start, count, local) in enumerate(pieces):
        target = padded.at[pl.ds(local, count), pl.ds(pad, rows), :]
        copies.append(pltpu.make_async_copy(source.at[pl.ds(start, count)], target, sem.at[number]))
        copies[-1].start()
    return copies


def scratch_for(locals_, rows, width):
    padded = pltpu.VMEM((locals_, rows + 2 * pad, lanes), f32)
    weighed = pltpu.VMEM((3, locals_, rows + 2 * pad, lanes), f32)
    return [padded, weighed] + [pltpu.VMEM((group * rows, width), bf16)] * 4 + [pltpu.SemaphoreType.DMA((4,))]


def first_body(depth, begin, count, sent_from, field, right, low_x, high_x, low_y, high_y, halves, diagonal, hi, lo, rest, part, *scratch):
    padded, weighed, sem = scratch[0], scratch[1], scratch[-1]
    planes, rows = field.shape[0], field.shape[1]
    low, high = max(begin - 1, 0), min(begin + count + 1, planes)
    copies = loads([(field, low, high - low, low - begin + 1)], padded, sem)
    if begin == 0:
        padded[0, pad : pad + rows, :] = low_x[:rows]
    if begin + count == planes:
        padded[count + 1, pad : pad + rows, :] = high_x[:rows]
    strips(padded, 1, count, depth, low_y, high_y, begin, True)
    for copy in copies:
        copy.wait()
    weigh(padded, halves, weighed, 0, begin, count + 2)

    def emit(at, out):
        rest[at] = right[begin + at] - out[:, :lanes]

        @pl.when(at >= sent_from)
        def _():
            part[at - sent_from] = out[:, lanes:]

    operate(depth, count, lambda i: (i + 1, begin + i), scratch[:-1], halves, diagonal, hi, lo, emit)


def sides_body(depth, planes, first, last):
    rows = planes.shape[1]
    first[...] = planes[:, :depth, :]
    last[...] = planes[:, rows - depth :, :]


def middle_body(depth, taken, other, low_y, high_y, halves, diagonal, rest, hi, lo, residual, low, high, *scratch):
    padded, weighed, sem = scratch[0], scratch[1], scratch[-1]
    held, rows = other.shape[0], other.shape[1]
    count = held - 2
    copies = loads([(other, 0, held, 0)], padded, sem)
    strips(padded, 1, count, depth, low_y, high_y, 1, False)
    for copy in copies:
        copy.wait()
    weigh(padded, halves, weighed, 0, taken, held)

    def emit(at, out):
        value = rest[at] - out
        residual[taken + at] = value
        low[taken + at] = value[:depth]
        high[taken + at] = value[rows - depth :]

    operate(depth, count, lambda i: (i + 1, taken + i), scratch[:-1], halves, diagonal, hi, lo, emit)


def near_body(depth, rest, came, residual_in, low_in, high_in, residual, low, high, edge):
    count, rows = came.shape[0], came.shape[1]

    def one(i, _):
        value = rest[i] - came[i]
        residual[i] = value
        low[i] = value[:depth]
        high[i] = value[rows - depth :]
        return 0

    lax.fori_loop(0, count, one, 0)
    edge[...] = residual[0]


def far_body(depth, skip, rest, came, residual, low, high, edge):
    count, rows = came.shape[0], came.shape[1]

    def one(i, _):
        value = rest[skip + i] - came[i]
        residual[i] = value
        low[i] = value[:depth]
        high[i] = value[rows - depth :]
        return 0

    lax.fori_loop(0, count, one, 0)
    edge[...] = residual[count - 1]


def finish(out, residual, start):
    later = residual - step_size * out
    return later, start + step_size * (residual + later)


def second_body(depth, begin, count, residual, start, low_y, high_y, halves, diagonal, hi, lo, later, fields, part, *scratch):
    padded, weighed, sem = scratch[0], scratch[1], scratch[-1]
    rows = residual.shape[1]
    copies = loads([(residual, begin - 1, count + 2, 0)], padded, sem)
    strips(padded, 1, count, depth, low_y, high_y, begin, False)
    for copy in copies:
        copy.wait()
    weigh(padded, halves, weighed, 0, begin, count + 2)

    def emit(at, out):
        here = padded[at + 1, pad : pad + rows, :]
        later[at], fields[at] = finish(out[:, :lanes], here, start[begin + at])
        part[at] = out[:, lanes:]

    operate(depth, count, lambda i: (i + 1, begin + i), scratch[:-1], halves, diagonal, hi, lo, emit)


def third_body(depth, first, near, far, start, low_x, high_x, low_a, high_a, low_b, high_b, halves, diagonal, hi, lo, later, fields, part, *scratch):
    padded, weighed, sem = scratch[0], scratch[1], scratch[-1]
    ready, remaining = near.shape[0], far.shape[0]
    rows = near.shape[1]
    planes = ready + remaining
    run = planes - first
    copies = loads([(near, first - 1, ready - first + 1, 0), (far, 0, remaining, ready - first + 1), (near, 0, 2, run + 3)], padded, sem)
    padded[run + 1, pad : pad + rows, :] = high_x[...]
    padded[run + 2, pad : pad + rows, :] = low_x[...]
    strips(padded, 1, ready - first, depth, low_a, high_a, first, False)
    strips(padded, 1 + ready - first, remaining, depth, low_b, high_b, 0, False)
    strips(padded, run + 3, 1, depth, low_a, high_a, 0, False)
    for copy in copies:
        copy.wait()
    weigh(padded, halves, weighed, 0, first, run + 2)
    weigh(padded, halves, weighed, run + 2, 0, 3)

    def place(i):
        wrapped = jnp.where(i >= run, 1, 0)
        return i + 1 + 2 * wrapped, first + i - planes * wrapped

    def emit(at, out):
        middle, plane = place(at)
        here = padded[middle, pad : pad + rows, :]
        later[at], fields[at] = finish(out[:, :lanes], here, start[plane])
        part[at] = out[:, lanes:]

    operate(depth, run + 1, place, scratch[:-1], halves, diagonal, hi, lo, emit)


def last_body(first, later_part, fields_part, came, *refs):
    later, fields, staged, sem = refs[-4:]
    count = came.shape[0]
    planes = later.shape[0]
    piece = 4
    copies = []
    for begin in range(0, count, piece):
        for at in range(begin, begin + piece):
            staged[0, at] = later_part[at] - step_size * came[at]
            staged[1, at] = fields_part[at] - (step_size * step_size) * came[at]
        end = begin + piece
        wrap = max(begin, min(end, planes - first))
        for which, target in ((0, later), (1, fields)):
            for low, high in ((begin, wrap), (wrap, end)):
                if high > low:
                    goal = (first + low) % planes
                    copy = pltpu.make_async_copy(
                        staged.at[which, pl.ds(low, high - low)], target.at[pl.ds(goal, high - low)], sem.at[len(copies)]
                    )
                    copy.start()
                    copies.append(copy)
    for copy in copies:
        copy.wait()


def add_last(first, shape, later_part, fields_part, came, before):
    count = came.shape[0]
    return call(
        functools.partial(last_body, first),
        [(shape, f32)] * 2,
        [pltpu.VMEM((2,) + came.shape, f32), pltpu.SemaphoreType.DMA((count + 4,))],
        in_specs=[whole] * 3 + [anywhere] * len(before),
        out_specs=[anywhere] * 2,
        aliases={3: 0, 4: 1} if before else {},
        work=0.2,
        name="last",
    )(later_part, fields_part, came, *before)


def shards(right_side, start_field, coefficients, couplings):
    nx, ny, depth, modes = start_field.shape
    rows = ny * depth
    plane = (rows, modes)
    flat = (nx,) + plane
    start = start_field.reshape(flat)
    right = right_side.reshape(flat)
    begin = (9 * nx) // 32
    end = nx - begin
    held = end - begin
    taken = begin + 1
    ready = end - 1
    done = ready - 1
    width = 3 * modes

    raw = sent(lax.slice_in_dim(start, begin, end, axis=0), "ma", 1, True)

    coef = coefficients.reshape(3 * nx, rows)
    layer = ((rows + lanes, lanes), f32)
    first_x, last_x, first_y, last_y = call(
        functools.partial(layers_body, depth),
        [layer] * 4,
        [pltpu.VMEM(flat, f32), pltpu.SemaphoreType.DMA],
        in_specs=[anywhere, whole],
        name="layers",
    )(start, coef)
    low_y = sent(last_y, "gy", 1, True)
    high_y = sent(first_y, "gy", -1, True)
    low_x = sent(last_x, "gx", 1, False)
    high_x = sent(first_x, "gx", -1, False)

    own_hi, own_lo, other_hi, other_lo = call(
        weights_body,
        [((width, 2 * modes), bf16)] * 2 + [((width, modes), bf16)] * 2,
        [pltpu.VMEM((2 * modes, 2 * modes), f32)],
        in_specs=[whole],
        name="weights",
    )(couplings)

    halves_shape = (3, nx + 2, rows + 2 * pad, lanes)
    (halves,) = call(halves_body, [(halves_shape, f32)], [pltpu.VMEM((lanes, rows), f32)], in_specs=[whole], name="halves")(coef)
    halves, diagonal = call(
        functools.partial(diagonal_body, depth),
        [(halves_shape, f32), ((3,) + flat, f32)],
        [],
        in_specs=[whole] * 5,
        aliases={4: 0},
        name="diagonal",
    )(low_x, high_x, low_y, high_y, halves)

    def first(begin, count, sent_from, name):
        return call(
            functools.partial(first_body, depth, begin, count, sent_from),
            [((count,) + plane, f32), ((count - sent_from,) + plane, f32)],
            scratch_for(count + 2, rows, width),
            in_specs=[anywhere] + [whole] * 9,
            work=count / 10,
            name=name,
        )(start, right, low_x, high_x, low_y, high_y, halves, diagonal, own_hi, own_lo)

    rest_a, part_a = first(0, taken, 0, "first_a")
    came_a = sent(part_a, "ma", 1, True)
    rest_b, part_b = first(taken, nx - taken, ready - taken, "first_b")
    came_b = sent(part_b, "ma", 1, True)

    strip = lambda count: ((count, depth, modes), f32)
    raw_first, raw_last = call(
        functools.partial(sides_body, depth), [strip(held)] * 2, [], in_specs=[whole], work=0.1, name="sides"
    )(raw)
    raw_low = sent(raw_last, "gy", 1, True)
    raw_high = sent(raw_first, "gy", -1, True)
    near_shapes = [((ready,) + plane, f32), strip(ready), strip(ready)]
    near, low_a, high_a = call(
        functools.partial(middle_body, depth, taken),
        near_shapes,
        scratch_for(held, rows, width),
        in_specs=[anywhere] + [whole] * 7,
        work=(held - 2) / 12,
        name="middle",
    )(raw, raw_low, raw_high, halves, diagonal, rest_b, other_hi, other_lo)
    near, low_a, high_a, edge_first = call(
        functools.partial(near_body, depth),
        near_shapes + [(plane, f32)],
        [],
        in_specs=[whole] * 5,
        aliases={2: 0, 3: 1, 4: 2},
        work=0.2,
        name="near",
    )(rest_a, came_a, near, low_a, high_a)
    next_low_a = sent(high_a, "gy", 1, True)
    next_high_a = sent(low_a, "gy", -1, True)
    next_high_x = sent(edge_first, "gx", -1, False)

    count = ready - 2
    later_c, fields_c, part_c = call(
        functools.partial(second_body, depth, 1, count),
        [((count,) + plane, f32)] * 3,
        scratch_for(count + 2, rows, width),
        in_specs=[anywhere] + [whole] * 7,
        work=count / 10,
        name="second",
    )(near, start, next_low_a, next_high_a, halves, diagonal, own_hi, own_lo)
    came_c = sent(part_c, "ma", 1, True)

    remaining = nx - ready
    far, low_b, high_b, edge_last = call(
        functools.partial(far_body, depth, ready - taken),
        [((remaining,) + plane, f32), strip(remaining), strip(remaining), (plane, f32)],
        [],
        in_specs=[whole] * 2,
        work=0.2,
        name="far",
    )(rest_b, came_b)
    next_low_b = sent(high_b, "gy", 1, True)
    next_high_b = sent(low_b, "gy", -1, True)
    next_low_x = sent(edge_last, "gx", 1, False)

    count = nx - done + 1
    later_d, fields_d, part_d = call(
        functools.partial(third_body, depth, done),
        [((count,) + plane, f32)] * 3,
        scratch_for(count + 4, rows, width),
        in_specs=[anywhere] * 2 + [whole] * 11,
        work=count / 10,
        name="third",
    )(near, far, start, next_low_x, next_high_x, next_low_a, next_high_a, next_low_b, next_high_b, halves, diagonal, own_hi, own_lo)
    came_d = sent(part_d, "ma", 1, True)

    outs = add_last(1, flat, later_c, fields_c, came_c, ())
    later, fields = add_last(done, flat, later_d, fields_d, came_d, outs)
    return (fields.reshape(start_field.shape), later.reshape(start_field.shape))


def solution(mesh):
    placed = (P("gx", "gy", None, "ma"), P("gx", "gy", None, "ma"), P(None, "gx", "gy", None), P())
    return jax.shard_map(
        shards,
        mesh=mesh,
        in_specs=placed,
        out_specs=(P("gx", "gy", None, "ma"), P("gx", "gy", None, "ma")),
        check_vma=False,
    )
```

```python
import functools

import jax
import jax.numpy as jnp
from jax import lax
from jax.experimental import pallas as pl
from jax.experimental.pallas import tpu as pltpu
from jax.sharding import PartitionSpec as P

step_size = 0.02
lanes = 128
group = 2
pad = 8
vmem_bytes = 12 * 1024 * 1024
f32 = jnp.float32
bf16 = jnp.bfloat16
whole = pl.BlockSpec(memory_space=pltpu.VMEM)
anywhere = pl.BlockSpec(memory_space=pl.ANY)


def call(body, out_shapes, scratch, work=1.0, vmem=vmem_bytes, in_specs=None, out_specs=None, aliases=None, name=None):
    return pl.pallas_call(
        body,
        out_shape=[jax.ShapeDtypeStruct(shape, kind) for shape, kind in out_shapes],
        in_specs=in_specs,
        out_specs=out_specs if out_specs is not None else [whole] * len(out_shapes),
        scratch_shapes=scratch,
        input_output_aliases=aliases or {},
        cost_estimate=pl.CostEstimate(flops=int(work * 1e9), bytes_accessed=int(work * 2e6), transcendentals=0),
        compiler_params=pltpu.CompilerParams(vmem_limit_bytes=vmem),
        name=name,
    )


def sent(array, axis, step, periodic):
    count = lax.axis_size(axis)
    pairs = [(i, (i + step) % count) for i in range(count) if periodic or 0 <= i + step < count]
    return lax.ppermute(array, axis, pairs)


def weights_body(couplings_ref, own_hi, own_lo, other_hi, other_lo, turned):
    half = lax.axis_index("ma")
    modes = own_hi.shape[1] // 2
    for field in range(3):
        mine = couplings_ref[field, pl.ds(pl.multiple_of(half * modes, modes), modes), :]
        theirs = couplings_ref[field, pl.ds(pl.multiple_of((1 - half) * modes, modes), modes), :]
        turned[:, :modes] = mine.T
        turned[:, modes:] = theirs.T
        own = turned[pl.ds(pl.multiple_of(half * modes, modes), modes), :]
        other = turned[pl.ds(pl.multiple_of((1 - half) * modes, modes), modes), :modes]
        rows = pl.ds(field * modes, modes)
        top = own.astype(bf16)
        own_hi[rows, :] = top
        own_lo[rows, :] = (own - top.astype(f32)).astype(bf16)
        top = other.astype(bf16)
        other_hi[rows, :] = top
        other_lo[rows, :] = (other - top.astype(f32)).astype(bf16)


def chosen_body(begin, field, out, sem):
    copy = pltpu.make_async_copy(field.at[pl.ds(begin, out.shape[0])], out, sem)
    copy.start()
    copy.wait()


def layers_body(depth, field, coef, first_x, last_x, first_y, last_y, held, sem):
    planes, rows = field.shape[0], field.shape[1]
    copy = pltpu.make_async_copy(field, held, sem)
    copy.start()
    for out in (first_x, last_x, first_y, last_y):
        out[rows : rows + coef.shape[0]] = coef[...]
        out[rows + coef.shape[0] :] = jnp.zeros((out.shape[0] - rows - coef.shape[0], lanes), f32)
    copy.wait()
    first_x[:rows] = held[0]
    last_x[:rows] = held[planes - 1]
    for plane in range(planes):
        first_y[plane * depth : (plane + 1) * depth] = held[plane, :depth]
        last_y[plane * depth : (plane + 1) * depth] = held[plane, rows - depth :]


def halves_body(coef, halves, square):
    count, rows = coef.shape[0], coef.shape[1]
    square[:count] = 0.5 * coef[...]
    square[count:] = jnp.zeros((lanes - count, rows), f32)
    columns = square[...].T
    planes = count // 3
    for plane in range(planes):
        for field in range(3):
            at = field * planes + plane
            halves[field, plane + 1, pad : pad + rows, :] = jnp.broadcast_to(columns[:, at : at + 1], (rows, lanes))


def around(ref, middle, row, size, depth):
    z = lax.broadcasted_iota(jnp.int32, (size, lanes), 0) % depth
    low = jnp.where(z != 0, ref[middle, row - 1 : row - 1 + size, :], 0.0)
    high = jnp.where(z != depth - 1, ref[middle, row + 1 : row + 1 + size, :], 0.0)
    beside = ref[middle, row - depth : row - depth + size, :] + ref[middle, row + depth : row + depth + size, :]
    return (ref[middle - 1, row : row + size, :] + ref[middle + 1, row : row + size, :]) + (beside + (low + high))


def diagonal_body(depth, low_x, high_x, low_y, high_y, halves_in, halves, diagonal):
    planes, rows = diagonal.shape[1], diagonal.shape[2]
    spread = lambda column, height: jnp.broadcast_to(column, (height, lanes))
    before = (0.5 * low_x[rows:]).T
    after = (0.5 * high_x[rows:]).T
    for field in range(3):
        at = field * planes + planes - 1
        halves[field, 0, pad : pad + rows, :] = spread(before[:, at : at + 1], rows)
        at = field * planes
        halves[field, planes + 1, pad : pad + rows, :] = spread(after[:, at : at + 1], rows)
    below = (0.5 * low_y[rows:]).T[rows - depth :]
    above = (0.5 * high_y[rows:]).T[:depth]
    for plane in range(planes):
        for field in range(3):
            at = field * planes + plane
            halves[field, plane + 1, pad - depth : pad, :] = spread(below[:, at : at + 1], depth)
            halves[field, plane + 1, pad + rows : pad + rows + depth, :] = spread(above[:, at : at + 1], depth)
    size = 32

    def one(plane, _):
        for start in range(0, rows, size):
            row = pad + start
            for field in range(3):
                here = halves[field, plane + 1, row : row + size, :]
                diagonal[field, plane, start : start + size, :] = 6.0 * here + around(halves.at[field], plane + 1, row, size, depth)
        return 0

    lax.fori_loop(0, planes, one, 0)


def weigh(padded, halves, weighed, local, first, count):
    size = (padded.shape[1]) // 3

    def one(i, _):
        for start in range(0, padded.shape[1], size):
            value = padded[local + i, start : start + size, :]
            for field in range(3):
                weighed[field, local + i, start : start + size, :] = halves[field, first + i, start : start + size, :] * value
        return 0

    lax.fori_loop(0, count, one, 0)


def stencil(padded, halves, diagonal, weighed, middle, plane, at, depth, upper, lower):
    size = 32
    rows = padded.shape[1] - 2 * pad
    for start in range(0, rows, size):
        row = pad + start
        here = padded[middle, row : row + size, :]
        total = around(padded, middle, row, size, depth)
        for field in range(3):
            value = diagonal[field, plane, start : start + size, :] * here - halves[field, plane + 1, row : row + size, :] * total
            value = value - around(weighed.at[field], middle, row, size, depth)
            where = slice(at + start, at + start + size), slice(field * lanes, (field + 1) * lanes)
            top = value.astype(bf16)
            upper[where] = top
            lower[where] = (value - top.astype(f32)).astype(bf16)


def operate(depth, count, place, scratch, halves, diagonal, hi, lo, emit):
    padded, weighed, upper_a, lower_a, upper_b, lower_b = scratch
    rows = padded.shape[1] - 2 * pad

    def fill(at, upper, lower):
        for j in range(group):
            middle, plane = place(at + j)
            stencil(padded, halves, diagonal, weighed, middle, plane, j * rows, depth, upper, lower)

    def flush(at, upper, lower):
        big, small = upper[...], lower[...]
        out = jnp.dot(big, hi[...], preferred_element_type=f32)
        out = out + jnp.dot(big, lo[...], preferred_element_type=f32)
        out = out + jnp.dot(small, hi[...], preferred_element_type=f32)
        for j in range(group):
            emit(at + j, out[j * rows : (j + 1) * rows])

    groups = -(-count // group)
    begin = lambda number: jnp.minimum(number * group, count - group)
    fill(0, upper_a, lower_a)

    def one(i, _):
        flush(begin(2 * i), upper_a, lower_a)
        fill(begin(2 * i + 1), upper_b, lower_b)
        flush(begin(2 * i + 1), upper_b, lower_b)
        fill(begin(2 * i + 2), upper_a, lower_a)
        return 0

    lax.fori_loop(0, (groups - 1) // 2, one, 0)
    if groups % 2:
        flush(count - group, upper_a, lower_a)
    else:
        flush(begin(groups - 2), upper_a, lower_a)
        fill(count - group, upper_b, lower_b)
        flush(count - group, upper_b, lower_b)


def strips(padded, local, count, depth, low, high, source, stacked):
    rows = padded.shape[1] - 2 * pad
    for i in range(count):
        at = slice((source + i) * depth, (source + i + 1) * depth) if stacked else source + i
        padded[local + i, pad - depth : pad, :] = low[at]
        padded[local + i, pad + rows : pad + rows + depth, :] = high[at]


def loads(pieces, padded, sem):
    rows = padded.shape[1] - 2 * pad
    copies = []
    for number, (source, start, count, local) in enumerate(pieces):
        target = padded.at[pl.ds(local, count), pl.ds(pad, rows), :]
        copies.append(pltpu.make_async_copy(source.at[pl.ds(start, count)], target, sem.at[number]))
        copies[-1].start()
    return copies


def scratch_for(locals_, rows, width):
    padded = pltpu.VMEM((locals_, rows + 2 * pad, lanes), f32)
    weighed = pltpu.VMEM((3, locals_, rows + 2 * pad, lanes), f32)
    return [padded, weighed] + [pltpu.VMEM((group * rows, width), bf16)] * 4 + [pltpu.SemaphoreType.DMA((4,))]


def first_body(depth, begin, count, sent_from, field, right, low_x, high_x, low_y, high_y, halves, diagonal, hi, lo, rest, part, *scratch):
    padded, weighed, sem = scratch[0], scratch[1], scratch[-1]
    planes, rows = field.shape[0], field.shape[1]
    low, high = max(begin - 1, 0), min(begin + count + 1, planes)
    copies = loads([(field, low, high - low, low - begin + 1)], padded, sem)
    if begin == 0:
        padded[0, pad : pad + rows, :] = low_x[:rows]
    if begin + count == planes:
        padded[count + 1, pad : pad + rows, :] = high_x[:rows]
    strips(padded, 1, count, depth, low_y, high_y, begin, True)
    for copy in copies:
        copy.wait()
    weigh(padded, halves, weighed, 0, begin, count + 2)

    def emit(at, out):
        rest[at] = right[begin + at] - out[:, :lanes]

        @pl.when(at >= sent_from)
        def _():
            part[at - sent_from] = out[:, lanes:]

    operate(depth, count, lambda i: (i + 1, begin + i), scratch[:-1], halves, diagonal, hi, lo, emit)


def sides_body(depth, planes, first, last):
    rows = planes.shape[1]
    first[...] = planes[:, :depth, :]
    last[...] = planes[:, rows - depth :, :]


def middle_body(depth, taken, other, low_y, high_y, halves, diagonal, rest, hi, lo, residual, low, high, *scratch):
    padded, weighed, sem = scratch[0], scratch[1], scratch[-1]
    held, rows = other.shape[0], other.shape[1]
    count = held - 2
    copies = loads([(other, 0, held, 0)], padded, sem)
    strips(padded, 1, count, depth, low_y, high_y, 1, False)
    for copy in copies:
        copy.wait()
    weigh(padded, halves, weighed, 0, taken, held)

    def emit(at, out):
        value = rest[at] - out
        residual[taken + at] = value
        low[taken + at] = value[:depth]
        high[taken + at] = value[rows - depth :]

    operate(depth, count, lambda i: (i + 1, taken + i), scratch[:-1], halves, diagonal, hi, lo, emit)


def near_body(depth, rest, came, residual_in, low_in, high_in, residual, low, high, edge):
    count, rows = came.shape[0], came.shape[1]

    def one(i, _):
        value = rest[i] - came[i]
        residual[i] = value
        low[i] = value[:depth]
        high[i] = value[rows - depth :]
        return 0

    lax.fori_loop(0, count, one, 0)
    edge[...] = residual[0]


def far_body(depth, skip, rest, came, after, residual, low, high, edge):
    count, rows = came.shape[0], came.shape[1]

    def one(i, _):
        value = rest[skip + i] - came[i]
        residual[i] = value
        low[i] = value[:depth]
        high[i] = value[rows - depth :]
        return 0

    lax.fori_loop(0, count, one, 0)
    edge[...] = residual[count - 1]


def finish(out, residual, start):
    later = residual - step_size * out
    return later, start + step_size * (residual + later)


def second_body(depth, begin, count, residual, start, low_y, high_y, halves, diagonal, hi, lo, later, fields, part, *scratch):
    padded, weighed, sem = scratch[0], scratch[1], scratch[-1]
    rows = residual.shape[1]
    copies = loads([(residual, begin - 1, count + 2, 0)], padded, sem)
    strips(padded, 1, count, depth, low_y, high_y, begin, False)
    for copy in copies:
        copy.wait()
    weigh(padded, halves, weighed, 0, begin, count + 2)

    def emit(at, out):
        here = padded[at + 1, pad : pad + rows, :]
        later[at], fields[at] = finish(out[:, :lanes], here, start[begin + at])
        part[at] = out[:, lanes:]

    operate(depth, count, lambda i: (i + 1, begin + i), scratch[:-1], halves, diagonal, hi, lo, emit)


def third_body(depth, first, near, far, start, low_x, high_x, low_a, high_a, low_b, high_b, halves, diagonal, hi, lo, *refs):
    later, fields, part, final_later, final_fields, final_part = refs[:6]
    scratch = refs[6:]
    split = part.shape[0]
    padded, weighed, sem = scratch[0], scratch[1], scratch[-1]
    ready, remaining = near.shape[0], far.shape[0]
    rows = near.shape[1]
    planes = ready + remaining
    run = planes - first
    copies = loads([(near, first - 1, ready - first + 1, 0), (far, 0, remaining, ready - first + 1), (near, 0, 2, run + 3)], padded, sem)
    padded[run + 1, pad : pad + rows, :] = high_x[...]
    padded[run + 2, pad : pad + rows, :] = low_x[...]
    strips(padded, 1, ready - first, depth, low_a, high_a, first, False)
    strips(padded, 1 + ready - first, remaining, depth, low_b, high_b, 0, False)
    strips(padded, run + 3, 1, depth, low_a, high_a, 0, False)
    for copy in copies:
        copy.wait()
    weigh(padded, halves, weighed, 0, first, run + 2)
    weigh(padded, halves, weighed, run + 2, 0, 3)

    def place(i):
        wrapped = jnp.where(i >= run, 1, 0)
        return i + 1 + 2 * wrapped, first + i - planes * wrapped

    def emit(at, out):
        middle, plane = place(at)
        here = padded[middle, pad : pad + rows, :]
        one, two = finish(out[:, :lanes], here, start[plane])

        @pl.when(at < split)
        def _():
            later[at], fields[at], part[at] = one, two, out[:, lanes:]

        @pl.when(at >= split)
        def _():
            final_later[at - split], final_fields[at - split], final_part[at - split] = one, two, out[:, lanes:]

    operate(depth, run + 1, place, scratch[:-1], halves, diagonal, hi, lo, emit)


def last_body(first, later_part, fields_part, came, *refs):
    later, fields, staged, sem = refs[-4:]
    count = came.shape[0]
    planes = later.shape[0]
    piece = 2
    copies = []
    for begin in range(0, count, piece):
        end = min(begin + piece, count)
        for at in range(begin, end):
            staged[0, at] = later_part[at] - step_size * came[at]
            staged[1, at] = fields_part[at] - (step_size * step_size) * came[at]
        wrap = max(begin, min(end, planes - first))
        for which, target in ((0, later), (1, fields)):
            for low, high in ((begin, wrap), (wrap, end)):
                if high > low:
                    goal = (first + low) % planes
                    copy = pltpu.make_async_copy(
                        staged.at[which, pl.ds(low, high - low)], target.at[pl.ds(goal, high - low)], sem.at[len(copies)]
                    )
                    copy.start()
                    copies.append(copy)
    for copy in copies:
        copy.wait()


def add_last(first, shape, later_part, fields_part, came, before):
    count = came.shape[0]
    return call(
        functools.partial(last_body, first),
        [(shape, f32)] * 2,
        [pltpu.VMEM((2,) + came.shape, f32), pltpu.SemaphoreType.DMA((2 * count + 4,))],
        in_specs=[whole] * 3 + [anywhere] * len(before),
        out_specs=[anywhere] * 2,
        aliases={3: 0, 4: 1} if before else {},
        work=0.2,
        name="last",
    )(later_part, fields_part, came, *before)


def shards(right_side, start_field, coefficients, couplings):
    nx, ny, depth, modes = start_field.shape
    rows = ny * depth
    plane = (rows, modes)
    flat = (nx,) + plane
    start = start_field.reshape(flat)
    right = right_side.reshape(flat)
    begin = nx // 4
    end = nx - begin
    held = end - begin
    taken = begin + 1
    ready = end - 1
    done = ready - 1
    width = 3 * modes

    (chosen,) = call(
        functools.partial(chosen_body, begin),
        [((held,) + plane, f32)],
        [pltpu.SemaphoreType.DMA],
        in_specs=[pl.BlockSpec(memory_space=pltpu.HBM)],
        out_specs=[anywhere],
        vmem=60 * 1024 * 1024,
        name="chosen",
    )(start)
    raw = sent(chosen, "ma", 1, True)

    coef = coefficients.reshape(3 * nx, rows)
    layer = ((rows + lanes, lanes), f32)
    first_x, last_x, first_y, last_y = call(
        functools.partial(layers_body, depth),
        [layer] * 4,
        [pltpu.VMEM(flat, f32), pltpu.SemaphoreType.DMA],
        in_specs=[anywhere, whole],
        name="layers",
    )(start, coef)
    low_y = sent(last_y, "gy", 1, True)
    high_y = sent(first_y, "gy", -1, True)
    low_x = sent(last_x, "gx", 1, False)
    high_x = sent(first_x, "gx", -1, False)

    own_hi, own_lo, other_hi, other_lo = call(
        weights_body,
        [((width, 2 * modes), bf16)] * 2 + [((width, modes), bf16)] * 2,
        [pltpu.VMEM((2 * modes, 2 * modes), f32)],
        in_specs=[whole],
        name="weights",
    )(couplings)

    halves_shape = (3, nx + 2, rows + 2 * pad, lanes)
    (halves,) = call(halves_body, [(halves_shape, f32)], [pltpu.VMEM((lanes, rows), f32)], in_specs=[whole], name="halves")(coef)
    halves, diagonal = call(
        functools.partial(diagonal_body, depth),
        [(halves_shape, f32), ((3,) + flat, f32)],
        [],
        in_specs=[whole] * 5,
        aliases={4: 0},
        name="diagonal",
    )(low_x, high_x, low_y, high_y, halves)

    def first(begin, count, sent_from, name):
        return call(
            functools.partial(first_body, depth, begin, count, sent_from),
            [((count,) + plane, f32), ((count - sent_from,) + plane, f32)],
            scratch_for(count + 2, rows, width),
            in_specs=[anywhere] + [whole] * 9,
            work=count / 10,
            name=name,
        )(start, right, low_x, high_x, low_y, high_y, halves, diagonal, own_hi, own_lo)

    rest_a, part_a = first(0, taken, 0, "first_a")
    came_a = sent(part_a, "ma", 1, True)
    rest_b, part_b = first(taken, nx - taken, ready - taken, "first_b")
    came_b = sent(part_b, "ma", 1, True)

    strip = lambda count: ((count, depth, modes), f32)
    raw_first, raw_last = call(
        functools.partial(sides_body, depth), [strip(held)] * 2, [], in_specs=[whole], work=0.1, name="sides"
    )(raw)
    raw_low = sent(raw_last, "gy", 1, True)
    raw_high = sent(raw_first, "gy", -1, True)
    near_shapes = [((ready,) + plane, f32), strip(ready), strip(ready)]
    near, low_a, high_a = call(
        functools.partial(middle_body, depth, taken),
        near_shapes,
        scratch_for(held, rows, width),
        in_specs=[anywhere] + [whole] * 7,
        work=(held - 2) / 12,
        name="middle",
    )(raw, raw_low, raw_high, halves, diagonal, rest_b, other_hi, other_lo)
    near, low_a, high_a, edge_first = call(
        functools.partial(near_body, depth),
        near_shapes + [(plane, f32)],
        [],
        in_specs=[whole] * 5,
        aliases={2: 0, 3: 1, 4: 2},
        work=0.2,
        name="near",
    )(rest_a, came_a, near, low_a, high_a)
    next_low_a = sent(high_a, "gy", 1, True)
    next_high_a = sent(low_a, "gy", -1, True)
    next_high_x = sent(edge_first, "gx", -1, False)

    count = ready - 2
    later_c, fields_c, part_c = call(
        functools.partial(second_body, depth, 1, count),
        [((count,) + plane, f32)] * 3,
        scratch_for(count + 2, rows, width),
        in_specs=[anywhere] + [whole] * 7,
        work=count / 10,
        name="second",
    )(near, start, next_low_a, next_high_a, halves, diagonal, own_hi, own_lo)
    came_c = sent(part_c, "ma", 1, True)

    remaining = nx - ready
    far, low_b, high_b, edge_last = call(
        functools.partial(far_body, depth, ready - taken),
        [((remaining,) + plane, f32), strip(remaining), strip(remaining), (plane, f32)],
        [],
        in_specs=[whole] * 2 + [anywhere],
        work=0.2,
        name="far",
    )(rest_b, came_b, part_c)
    next_low_b = sent(high_b, "gy", 1, True)
    next_high_b = sent(low_b, "gy", -1, True)
    next_low_x = sent(edge_last, "gx", 1, False)

    count = nx - done + 1
    final = 4
    later_d, fields_d, part_d, later_e, fields_e, part_e = call(
        functools.partial(third_body, depth, done),
        [((count - final,) + plane, f32)] * 3 + [((final,) + plane, f32)] * 3,
        scratch_for(count + 4, rows, width),
        in_specs=[anywhere] * 2 + [whole] * 11,
        work=6.0,
        name="third",
    )(near, far, start, next_low_x, next_high_x, next_low_a, next_high_a, next_low_b, next_high_b, halves, diagonal, own_hi, own_lo)
    came_d = sent(part_d, "ma", 1, True)
    came_e = sent(part_e, "ma", 1, True)

    outs = add_last(1, flat, later_c, fields_c, came_c, ())
    outs = add_last(done, flat, later_d, fields_d, came_d, outs)
    later, fields = add_last(done + count - final, flat, later_e, fields_e, came_e, outs)
    return (fields.reshape(start_field.shape), later.reshape(start_field.shape))


def solution(mesh):
    placed = (P("gx", "gy", None, "ma"), P("gx", "gy", None, "ma"), P(None, "gx", "gy", None), P())
    return jax.shard_map(
        shards,
        mesh=mesh,
        in_specs=placed,
        out_specs=(P("gx", "gy", None, "ma"), P("gx", "gy", None, "ma")),
        check_vma=False,
    )
```

```python
import functools

import jax
import jax.numpy as jnp
from jax import lax
from jax.experimental import pallas as pl
from jax.experimental.pallas import tpu as pltpu
from jax.sharding import PartitionSpec as P

step_size = 0.02
lanes = 128
group = 2
pad = 8
vmem_bytes = 12 * 1024 * 1024
f32 = jnp.float32
bf16 = jnp.bfloat16
whole = pl.BlockSpec(memory_space=pltpu.VMEM)
anywhere = pl.BlockSpec(memory_space=pl.ANY)


def call(body, out_shapes, scratch, work=1.0, vmem=vmem_bytes, in_specs=None, out_specs=None, aliases=None, name=None):
    return pl.pallas_call(
        body,
        out_shape=[jax.ShapeDtypeStruct(shape, kind) for shape, kind in out_shapes],
        in_specs=in_specs,
        out_specs=out_specs if out_specs is not None else [whole] * len(out_shapes),
        scratch_shapes=scratch,
        input_output_aliases=aliases or {},
        cost_estimate=pl.CostEstimate(flops=int(work * 1e9), bytes_accessed=int(work * 2e6), transcendentals=0),
        compiler_params=pltpu.CompilerParams(vmem_limit_bytes=vmem),
        name=name,
    )


def sent(array, axis, step, periodic):
    count = lax.axis_size(axis)
    pairs = [(i, (i + step) % count) for i in range(count) if periodic or 0 <= i + step < count]
    return lax.ppermute(array, axis, pairs)


def weights_body(couplings_ref, own_hi, own_lo, other_hi, other_lo, turned):
    half = lax.axis_index("ma")
    modes = own_hi.shape[1] // 2
    for field in range(3):
        mine = couplings_ref[field, pl.ds(pl.multiple_of(half * modes, modes), modes), :]
        theirs = couplings_ref[field, pl.ds(pl.multiple_of((1 - half) * modes, modes), modes), :]
        turned[:, :modes] = mine.T
        turned[:, modes:] = theirs.T
        own = turned[pl.ds(pl.multiple_of(half * modes, modes), modes), :]
        other = turned[pl.ds(pl.multiple_of((1 - half) * modes, modes), modes), :modes]
        rows = pl.ds(field * modes, modes)
        top = own.astype(bf16)
        own_hi[rows, :] = top
        own_lo[rows, :] = (own - top.astype(f32)).astype(bf16)
        top = other.astype(bf16)
        other_hi[rows, :] = top
        other_lo[rows, :] = (other - top.astype(f32)).astype(bf16)


def chosen_body(begin, field, out, sem):
    copy = pltpu.make_async_copy(field.at[pl.ds(begin, out.shape[0])], out, sem)
    copy.start()
    copy.wait()


def layers_body(depth, field, coef, first_x, last_x, first_y, last_y, held, sem):
    planes, rows = field.shape[0], field.shape[1]
    copy = pltpu.make_async_copy(field, held, sem)
    copy.start()
    for out in (first_x, last_x, first_y, last_y):
        out[rows : rows + coef.shape[0]] = coef[...]
        out[rows + coef.shape[0] :] = jnp.zeros((out.shape[0] - rows - coef.shape[0], lanes), f32)
    copy.wait()
    first_x[:rows] = held[0]
    last_x[:rows] = held[planes - 1]
    for plane in range(planes):
        first_y[plane * depth : (plane + 1) * depth] = held[plane, :depth]
        last_y[plane * depth : (plane + 1) * depth] = held[plane, rows - depth :]


def halves_body(coef, halves, square):
    count, rows = coef.shape[0], coef.shape[1]
    square[:count] = 0.5 * coef[...]
    square[count:] = jnp.zeros((lanes - count, rows), f32)
    columns = square[...].T
    planes = count // 3
    for plane in range(planes):
        for field in range(3):
            at = field * planes + plane
            halves[field, plane + 1, pad : pad + rows, :] = jnp.broadcast_to(columns[:, at : at + 1], (rows, lanes))


def around(ref, middle, row, size, depth):
    z = lax.broadcasted_iota(jnp.int32, (size, lanes), 0) % depth
    low = jnp.where(z != 0, ref[middle, row - 1 : row - 1 + size, :], 0.0)
    high = jnp.where(z != depth - 1, ref[middle, row + 1 : row + 1 + size, :], 0.0)
    beside = ref[middle, row - depth : row - depth + size, :] + ref[middle, row + depth : row + depth + size, :]
    return (ref[middle - 1, row : row + size, :] + ref[middle + 1, row : row + size, :]) + (beside + (low + high))


def diagonal_body(depth, low_x, high_x, low_y, high_y, halves_in, halves, diagonal):
    planes, rows = diagonal.shape[1], diagonal.shape[2]
    spread = lambda column, height: jnp.broadcast_to(column, (height, lanes))
    before = (0.5 * low_x[rows:]).T
    after = (0.5 * high_x[rows:]).T
    for field in range(3):
        at = field * planes + planes - 1
        halves[field, 0, pad : pad + rows, :] = spread(before[:, at : at + 1], rows)
        at = field * planes
        halves[field, planes + 1, pad : pad + rows, :] = spread(after[:, at : at + 1], rows)
    below = (0.5 * low_y[rows:]).T[rows - depth :]
    above = (0.5 * high_y[rows:]).T[:depth]
    for plane in range(planes):
        for field in range(3):
            at = field * planes + plane
            halves[field, plane + 1, pad - depth : pad, :] = spread(below[:, at : at + 1], depth)
            halves[field, plane + 1, pad + rows : pad + rows + depth, :] = spread(above[:, at : at + 1], depth)
    size = 32

    def one(plane, _):
        for start in range(0, rows, size):
            row = pad + start
            for field in range(3):
                here = halves[field, plane + 1, row : row + size, :]
                diagonal[field, plane, start : start + size, :] = 6.0 * here + around(halves.at[field], plane + 1, row, size, depth)
        return 0

    lax.fori_loop(0, planes, one, 0)


def weigh(padded, halves, weighed, local, first, count):
    size = (padded.shape[1]) // 3

    def one(i, _):
        for start in range(0, padded.shape[1], size):
            value = padded[local + i, start : start + size, :]
            for field in range(3):
                weighed[field, local + i, start : start + size, :] = halves[field, first + i, start : start + size, :] * value
        return 0

    lax.fori_loop(0, count, one, 0)


def stencil(padded, halves, diagonal, weighed, middle, plane, at, depth, upper, lower):
    size = 32
    rows = padded.shape[1] - 2 * pad
    for start in range(0, rows, size):
        row = pad + start
        here = padded[middle, row : row + size, :]
        total = around(padded, middle, row, size, depth)
        for field in range(3):
            value = diagonal[field, plane, start : start + size, :] * here - halves[field, plane + 1, row : row + size, :] * total
            value = value - around(weighed.at[field], middle, row, size, depth)
            where = slice(at + start, at + start + size), slice(field * lanes, (field + 1) * lanes)
            top = value.astype(bf16)
            upper[where] = top
            lower[where] = (value - top.astype(f32)).astype(bf16)


def operate(depth, count, place, scratch, halves, diagonal, hi, lo, emit):
    padded, weighed, upper_a, lower_a, upper_b, lower_b = scratch
    rows = padded.shape[1] - 2 * pad

    def fill(at, upper, lower):
        for j in range(group):
            middle, plane = place(at + j)
            stencil(padded, halves, diagonal, weighed, middle, plane, j * rows, depth, upper, lower)

    def flush(at, upper, lower):
        big, small = upper[...], lower[...]
        out = jnp.dot(big, hi[...], preferred_element_type=f32)
        out = out + jnp.dot(big, lo[...], preferred_element_type=f32)
        out = out + jnp.dot(small, hi[...], preferred_element_type=f32)
        for j in range(group):
            emit(at + j, out[j * rows : (j + 1) * rows])

    groups = -(-count // group)
    begin = lambda number: jnp.minimum(number * group, count - group)
    fill(0, upper_a, lower_a)

    def one(i, _):
        flush(begin(2 * i), upper_a, lower_a)
        fill(begin(2 * i + 1), upper_b, lower_b)
        flush(begin(2 * i + 1), upper_b, lower_b)
        fill(begin(2 * i + 2), upper_a, lower_a)
        return 0

    lax.fori_loop(0, (groups - 1) // 2, one, 0)
    if groups % 2:
        flush(count - group, upper_a, lower_a)
    else:
        flush(begin(groups - 2), upper_a, lower_a)
        fill(count - group, upper_b, lower_b)
        flush(count - group, upper_b, lower_b)


def strips(padded, local, count, depth, low, high, source, stacked):
    rows = padded.shape[1] - 2 * pad
    for i in range(count):
        at = slice((source + i) * depth, (source + i + 1) * depth) if stacked else source + i
        padded[local + i, pad - depth : pad, :] = low[at]
        padded[local + i, pad + rows : pad + rows + depth, :] = high[at]


def loads(pieces, padded, sem):
    rows = padded.shape[1] - 2 * pad
    copies = []
    for number, (source, start, count, local) in enumerate(pieces):
        target = padded.at[pl.ds(local, count), pl.ds(pad, rows), :]
        copies.append(pltpu.make_async_copy(source.at[pl.ds(start, count)], target, sem.at[number]))
        copies[-1].start()
    return copies


def scratch_for(locals_, rows, width):
    padded = pltpu.VMEM((locals_, rows + 2 * pad, lanes), f32)
    weighed = pltpu.VMEM((3, locals_, rows + 2 * pad, lanes), f32)
    return [padded, weighed] + [pltpu.VMEM((group * rows, width), bf16)] * 4 + [pltpu.SemaphoreType.DMA((4,))]


def first_body(depth, begin, count, sends, field, right, low_x, high_x, low_y, high_y, halves, diagonal, hi, lo, rest, *refs):
    scratch = refs[1:] if sends else refs
    padded, weighed, sem = scratch[0], scratch[1], scratch[-1]
    planes, rows = field.shape[0], field.shape[1]
    low, high = max(begin - 1, 0), min(begin + count + 1, planes)
    copies = loads([(field, low, high - low, low - begin + 1)], padded, sem)
    if begin == 0:
        padded[0, pad : pad + rows, :] = low_x[:rows]
    if begin + count == planes:
        padded[count + 1, pad : pad + rows, :] = high_x[:rows]
    strips(padded, 1, count, depth, low_y, high_y, begin, True)
    for copy in copies:
        copy.wait()
    weigh(padded, halves, weighed, 0, begin, count + 2)

    def emit(at, out):
        rest[at] = right[begin + at] - out[:, :lanes]
        if sends:
            refs[0][at] = out[:, lanes:]

    used = pl.ds(0, 2 * lanes if sends else lanes)
    operate(depth, count, lambda i: (i + 1, begin + i), scratch[:-1], halves, diagonal, hi.at[:, used], lo.at[:, used], emit)


def sides_body(depth, planes, first, last):
    rows = planes.shape[1]
    first[...] = planes[:, :depth, :]
    last[...] = planes[:, rows - depth :, :]


def middle_body(depth, taken, other, low_y, high_y, halves, diagonal, rest, hi, lo, residual, low, high, *scratch):
    padded, weighed, sem = scratch[0], scratch[1], scratch[-1]
    held, rows = other.shape[0], other.shape[1]
    count = held - 2
    copies = loads([(other, 0, held, 0)], padded, sem)
    strips(padded, 1, count, depth, low_y, high_y, 1, False)
    for copy in copies:
        copy.wait()
    weigh(padded, halves, weighed, 0, taken, held)

    def emit(at, out):
        value = rest[at] - out
        residual[taken + at] = value
        low[taken + at] = value[:depth]
        high[taken + at] = value[rows - depth :]

    operate(depth, count, lambda i: (i + 1, taken + i), scratch[:-1], halves, diagonal, hi, lo, emit)


def near_body(depth, rest, came, residual_in, low_in, high_in, residual, low, high, edge):
    count, rows = came.shape[0], came.shape[1]

    def one(i, _):
        value = rest[i] - came[i]
        residual[i] = value
        low[i] = value[:depth]
        high[i] = value[rows - depth :]
        return 0

    lax.fori_loop(0, count, one, 0)
    edge[...] = residual[0]


def far_body(depth, rest, came, after, residual, low, high, edge):
    count, rows = came.shape[0], came.shape[1]

    def one(i, _):
        value = rest[i] - came[i]
        residual[i] = value
        low[i] = value[:depth]
        high[i] = value[rows - depth :]
        return 0

    lax.fori_loop(0, count, one, 0)
    edge[...] = residual[count - 1]


def finish(out, residual, start):
    later = residual - step_size * out
    return later, start + step_size * (residual + later)


def second_body(depth, begin, count, residual, start, low_y, high_y, halves, diagonal, hi, lo, later, fields, part, *scratch):
    padded, weighed, sem = scratch[0], scratch[1], scratch[-1]
    rows = residual.shape[1]
    copies = loads([(residual, begin - 1, count + 2, 0)], padded, sem)
    strips(padded, 1, count, depth, low_y, high_y, begin, False)
    for copy in copies:
        copy.wait()
    weigh(padded, halves, weighed, 0, begin, count + 2)

    def emit(at, out):
        here = padded[at + 1, pad : pad + rows, :]
        later[at], fields[at] = finish(out[:, :lanes], here, start[begin + at])
        part[at] = out[:, lanes:]

    operate(depth, count, lambda i: (i + 1, begin + i), scratch[:-1], halves, diagonal, hi, lo, emit)


def third_body(depth, first, near, far, start, low_x, high_x, low_a, high_a, low_b, high_b, halves, diagonal, hi, lo, *refs):
    later, fields, part, final_later, final_fields, final_part = refs[:6]
    scratch = refs[6:]
    split = part.shape[0]
    padded, weighed, sem = scratch[0], scratch[1], scratch[-1]
    ready, remaining = near.shape[0], far.shape[0]
    rows = near.shape[1]
    planes = ready + remaining
    run = planes - first
    copies = loads([(near, first - 1, ready - first + 1, 0), (far, 0, remaining, ready - first + 1), (near, 0, 2, run + 3)], padded, sem)
    padded[run + 1, pad : pad + rows, :] = high_x[...]
    padded[run + 2, pad : pad + rows, :] = low_x[...]
    strips(padded, 1, ready - first, depth, low_a, high_a, first, False)
    strips(padded, 1 + ready - first, remaining, depth, low_b, high_b, 0, False)
    strips(padded, run + 3, 1, depth, low_a, high_a, 0, False)
    for copy in copies:
        copy.wait()
    weigh(padded, halves, weighed, 0, first, run + 2)
    weigh(padded, halves, weighed, run + 2, 0, 3)

    def place(i):
        wrapped = jnp.where(i >= run, 1, 0)
        return i + 1 + 2 * wrapped, first + i - planes * wrapped

    def emit(at, out):
        middle, plane = place(at)
        here = padded[middle, pad : pad + rows, :]
        one, two = finish(out[:, :lanes], here, start[plane])

        @pl.when(at < split)
        def _():
            later[at], fields[at], part[at] = one, two, out[:, lanes:]

        @pl.when(at >= split)
        def _():
            final_later[at - split], final_fields[at - split], final_part[at - split] = one, two, out[:, lanes:]

    operate(depth, run + 1, place, scratch[:-1], halves, diagonal, hi, lo, emit)


def last_body(first, later_part, fields_part, came, *refs):
    later, fields, staged, sem = refs[-4:]
    count = came.shape[0]
    planes = later.shape[0]
    piece = 2
    copies = []
    for begin in range(0, count, piece):
        end = min(begin + piece, count)
        for at in range(begin, end):
            staged[0, at] = later_part[at] - step_size * came[at]
            staged[1, at] = fields_part[at] - (step_size * step_size) * came[at]
        wrap = max(begin, min(end, planes - first))
        for which, target in ((0, later), (1, fields)):
            for low, high in ((begin, wrap), (wrap, end)):
                if high > low:
                    goal = (first + low) % planes
                    copy = pltpu.make_async_copy(
                        staged.at[which, pl.ds(low, high - low)], target.at[pl.ds(goal, high - low)], sem.at[len(copies)]
                    )
                    copy.start()
                    copies.append(copy)
    for copy in copies:
        copy.wait()


def add_last(first, shape, later_part, fields_part, came, before):
    count = came.shape[0]
    return call(
        functools.partial(last_body, first),
        [(shape, f32)] * 2,
        [pltpu.VMEM((2,) + came.shape, f32), pltpu.SemaphoreType.DMA((2 * count + 4,))],
        in_specs=[whole] * 3 + [anywhere] * len(before),
        out_specs=[anywhere] * 2,
        aliases={3: 0, 4: 1} if before else {},
        work=0.2,
        name="last",
    )(later_part, fields_part, came, *before)


def shards(right_side, start_field, coefficients, couplings):
    nx, ny, depth, modes = start_field.shape
    rows = ny * depth
    plane = (rows, modes)
    flat = (nx,) + plane
    start = start_field.reshape(flat)
    right = right_side.reshape(flat)
    begin = nx // 4
    end = nx - begin - nx // 32
    held = end - begin
    taken = begin + 1
    ready = end - 1
    done = ready - 1
    width = 3 * modes

    (chosen,) = call(
        functools.partial(chosen_body, begin),
        [((held,) + plane, f32)],
        [pltpu.SemaphoreType.DMA],
        in_specs=[pl.BlockSpec(memory_space=pltpu.HBM)],
        vmem=60 * 1024 * 1024,
        name="chosen",
    )(start)
    raw = sent(chosen, "ma", 1, True)

    coef = coefficients.reshape(3 * nx, rows)
    layer = ((rows + lanes, lanes), f32)
    first_x, last_x, first_y, last_y = call(
        functools.partial(layers_body, depth),
        [layer] * 4,
        [pltpu.VMEM(flat, f32), pltpu.SemaphoreType.DMA],
        in_specs=[anywhere, whole],
        name="layers",
    )(start, coef)
    low_y = sent(last_y, "gy", 1, True)
    high_y = sent(first_y, "gy", -1, True)
    low_x = sent(last_x, "gx", 1, False)
    high_x = sent(first_x, "gx", -1, False)

    own_hi, own_lo, other_hi, other_lo = call(
        weights_body,
        [((width, 2 * modes), bf16)] * 2 + [((width, modes), bf16)] * 2,
        [pltpu.VMEM((2 * modes, 2 * modes), f32)],
        in_specs=[whole],
        name="weights",
    )(couplings)

    halves_shape = (3, nx + 2, rows + 2 * pad, lanes)
    (halves,) = call(halves_body, [(halves_shape, f32)], [pltpu.VMEM((lanes, rows), f32)], in_specs=[whole], name="halves")(coef)
    halves, diagonal = call(
        functools.partial(diagonal_body, depth),
        [(halves_shape, f32), ((3,) + flat, f32)],
        [],
        in_specs=[whole] * 5,
        aliases={4: 0},
        name="diagonal",
    )(low_x, high_x, low_y, high_y, halves)

    def first(begin, count, sends, name):
        return call(
            functools.partial(first_body, depth, begin, count, sends),
            [((count,) + plane, f32)] * (2 if sends else 1),
            scratch_for(count + 2, rows, width),
            in_specs=[anywhere] + [whole] * 9,
            work=count / 10,
            name=name,
        )(start, right, low_x, high_x, low_y, high_y, halves, diagonal, own_hi, own_lo)

    rest_a, part_a = first(0, taken, True, "first_a")
    came_a = sent(part_a, "ma", 1, True)
    rest_b, part_b = first(ready, nx - ready, True, "first_b")
    came_b = sent(part_b, "ma", 1, True)
    (rest_c,) = first(taken, ready - taken, False, "first_c")

    strip = lambda count: ((count, depth, modes), f32)
    raw_first, raw_last = call(
        functools.partial(sides_body, depth), [strip(held)] * 2, [], in_specs=[whole], work=0.1, name="sides"
    )(raw)
    raw_low = sent(raw_last, "gy", 1, True)
    raw_high = sent(raw_first, "gy", -1, True)
    near_shapes = [((ready,) + plane, f32), strip(ready), strip(ready)]
    near, low_a, high_a = call(
        functools.partial(middle_body, depth, taken),
        near_shapes,
        scratch_for(held, rows, width),
        in_specs=[anywhere] + [whole] * 7,
        work=(held - 2) / 12,
        name="middle",
    )(raw, raw_low, raw_high, halves, diagonal, rest_c, other_hi, other_lo)
    near, low_a, high_a, edge_first = call(
        functools.partial(near_body, depth),
        near_shapes + [(plane, f32)],
        [],
        in_specs=[whole] * 5,
        aliases={2: 0, 3: 1, 4: 2},
        work=0.2,
        name="near",
    )(rest_a, came_a, near, low_a, high_a)
    next_low_a = sent(high_a, "gy", 1, True)
    next_high_a = sent(low_a, "gy", -1, True)
    next_high_x = sent(edge_first, "gx", -1, False)

    count = ready - 2
    later_c, fields_c, part_c = call(
        functools.partial(second_body, depth, 1, count),
        [((count,) + plane, f32)] * 3,
        scratch_for(count + 2, rows, width),
        in_specs=[anywhere] + [whole] * 7,
        work=count / 10,
        name="second",
    )(near, start, next_low_a, next_high_a, halves, diagonal, own_hi, own_lo)
    came_c = sent(part_c, "ma", 1, True)

    remaining = nx - ready
    far, low_b, high_b, edge_last = call(
        functools.partial(far_body, depth),
        [((remaining,) + plane, f32), strip(remaining), strip(remaining), (plane, f32)],
        [],
        in_specs=[whole] * 2 + [anywhere],
        work=0.2,
        name="far",
    )(rest_b, came_b, part_c)
    next_low_b = sent(high_b, "gy", 1, True)
    next_high_b = sent(low_b, "gy", -1, True)
    next_low_x = sent(edge_last, "gx", 1, False)

    count = nx - done + 1
    final = 4
    later_d, fields_d, part_d, later_e, fields_e, part_e = call(
        functools.partial(third_body, depth, done),
        [((count - final,) + plane, f32)] * 3 + [((final,) + plane, f32)] * 3,
        scratch_for(count + 4, rows, width),
        in_specs=[anywhere] * 2 + [whole] * 11,
        work=6.0,
        name="third",
    )(near, far, start, next_low_x, next_high_x, next_low_a, next_high_a, next_low_b, next_high_b, halves, diagonal, own_hi, own_lo)
    came_d = sent(part_d, "ma", 1, True)
    came_e = sent(part_e, "ma", 1, True)

    outs = add_last(1, flat, later_c, fields_c, came_c, ())
    outs = add_last(done, flat, later_d, fields_d, came_d, outs)
    later, fields = add_last(done + count - final, flat, later_e, fields_e, came_e, outs)
    return (fields.reshape(start_field.shape), later.reshape(start_field.shape))


def solution(mesh):
    placed = (P("gx", "gy", None, "ma"), P("gx", "gy", None, "ma"), P(None, "gx", "gy", None), P())
    return jax.shard_map(
        shards,
        mesh=mesh,
        in_specs=placed,
        out_specs=(P("gx", "gy", None, "ma"), P("gx", "gy", None, "ma")),
        check_vma=False,
    )
```

```python
import functools

import jax
import jax.numpy as jnp
from jax import lax
from jax.experimental import pallas as pl
from jax.experimental.pallas import tpu as pltpu
from jax.sharding import PartitionSpec as P

step_size = 0.02
lanes = 128
group = 2
pad = 8
vmem_bytes = 12 * 1024 * 1024
most_bytes = 60 * 1024 * 1024
f32 = jnp.float32
bf16 = jnp.bfloat16
whole = pl.BlockSpec(memory_space=pltpu.VMEM)
anywhere = pl.BlockSpec(memory_space=pl.ANY)


def call(body, out_shapes, scratch, work=1.0, vmem=vmem_bytes, in_specs=None, out_specs=None, aliases=None, name=None):
    return pl.pallas_call(
        body,
        out_shape=[jax.ShapeDtypeStruct(shape, kind) for shape, kind in out_shapes],
        in_specs=in_specs,
        out_specs=out_specs if out_specs is not None else [whole] * len(out_shapes),
        scratch_shapes=scratch,
        input_output_aliases=aliases or {},
        cost_estimate=pl.CostEstimate(flops=int(work * 1e6), bytes_accessed=int(work * 2e3), transcendentals=0),
        compiler_params=pltpu.CompilerParams(vmem_limit_bytes=vmem),
        name=name,
    )


def sent(array, axis, step, periodic):
    count = lax.axis_size(axis)
    pairs = [(i, (i + step) % count) for i in range(count) if periodic or 0 <= i + step < count]
    return lax.ppermute(array, axis, pairs)


def weights_body(couplings_ref, own_hi, own_lo, other_hi, other_lo, turned):
    half = lax.axis_index("ma")
    modes = own_hi.shape[1] // 2
    for field in range(3):
        mine = couplings_ref[field, pl.ds(pl.multiple_of(half * modes, modes), modes), :]
        theirs = couplings_ref[field, pl.ds(pl.multiple_of((1 - half) * modes, modes), modes), :]
        turned[:, :modes] = mine.T
        turned[:, modes:] = theirs.T
        own = turned[pl.ds(pl.multiple_of(half * modes, modes), modes), :]
        other = turned[pl.ds(pl.multiple_of((1 - half) * modes, modes), modes), :modes]
        rows = pl.ds(field * modes, modes)
        top = own.astype(bf16)
        own_hi[rows, :] = top
        own_lo[rows, :] = (own - top.astype(f32)).astype(bf16)
        top = other.astype(bf16)
        other_hi[rows, :] = top
        other_lo[rows, :] = (other - top.astype(f32)).astype(bf16)


def chosen_body(begin, field, *refs):
    out, sem = refs[-2:]
    copy = pltpu.make_async_copy(field.at[pl.ds(begin, out.shape[0])], out, sem)
    copy.start()
    copy.wait()


def layers_body(depth, field, coef, first_x, last_x, first_y, last_y, held, sem):
    planes, rows = field.shape[0], field.shape[1]
    copy = pltpu.make_async_copy(field, held, sem)
    copy.start()
    for out in (first_x, last_x, first_y, last_y):
        out[rows : rows + coef.shape[0]] = coef[...]
        out[rows + coef.shape[0] :] = jnp.zeros((out.shape[0] - rows - coef.shape[0], lanes), f32)
    copy.wait()
    first_x[:rows] = held[0]
    last_x[:rows] = held[planes - 1]
    for plane in range(planes):
        first_y[plane * depth : (plane + 1) * depth] = held[plane, :depth]
        last_y[plane * depth : (plane + 1) * depth] = held[plane, rows - depth :]


def halves_body(coef, halves, square):
    count, rows = coef.shape[0], coef.shape[1]
    square[:count] = 0.5 * coef[...]
    square[count:] = jnp.zeros((lanes - count, rows), f32)
    columns = square[...].T
    planes = count // 3
    for plane in range(planes):
        for field in range(3):
            at = field * planes + plane
            halves[field, plane + 1, pad : pad + rows, :] = jnp.broadcast_to(columns[:, at : at + 1], (rows, lanes))


def around(ref, middle, row, size, depth):
    z = lax.broadcasted_iota(jnp.int32, (size, lanes), 0) % depth
    low = jnp.where(z != 0, ref[middle, row - 1 : row - 1 + size, :], 0.0)
    high = jnp.where(z != depth - 1, ref[middle, row + 1 : row + 1 + size, :], 0.0)
    beside = ref[middle, row - depth : row - depth + size, :] + ref[middle, row + depth : row + depth + size, :]
    return (ref[middle - 1, row : row + size, :] + ref[middle + 1, row : row + size, :]) + (beside + (low + high))


def diagonal_body(depth, low_x, high_x, low_y, high_y, halves_in, halves, diagonal):
    planes, rows = diagonal.shape[1], diagonal.shape[2]
    spread = lambda column, height: jnp.broadcast_to(column, (height, lanes))
    before = (0.5 * low_x[rows:]).T
    after = (0.5 * high_x[rows:]).T
    for field in range(3):
        at = field * planes + planes - 1
        halves[field, 0, pad : pad + rows, :] = spread(before[:, at : at + 1], rows)
        at = field * planes
        halves[field, planes + 1, pad : pad + rows, :] = spread(after[:, at : at + 1], rows)
    below = (0.5 * low_y[rows:]).T[rows - depth :]
    above = (0.5 * high_y[rows:]).T[:depth]
    for plane in range(planes):
        for field in range(3):
            at = field * planes + plane
            halves[field, plane + 1, pad - depth : pad, :] = spread(below[:, at : at + 1], depth)
            halves[field, plane + 1, pad + rows : pad + rows + depth, :] = spread(above[:, at : at + 1], depth)
    size = 32

    def one(plane, _):
        for start in range(0, rows, size):
            row = pad + start
            for field in range(3):
                here = halves[field, plane + 1, row : row + size, :]
                diagonal[field, plane, start : start + size, :] = 6.0 * here + around(halves.at[field], plane + 1, row, size, depth)
        return 0

    lax.fori_loop(0, planes, one, 0)


def weigh(padded, halves, weighed, local, first, count):
    size = (padded.shape[1]) // 3

    def one(i, _):
        for start in range(0, padded.shape[1], size):
            value = padded[local + i, start : start + size, :]
            for field in range(3):
                weighed[field, local + i, start : start + size, :] = halves[field, first + i, start : start + size, :] * value
        return 0

    lax.fori_loop(0, count, one, 0)


def stencil(padded, halves, diagonal, weighed, middle, plane, at, depth, upper, lower):
    size = 32
    rows = padded.shape[1] - 2 * pad
    for start in range(0, rows, size):
        row = pad + start
        here = padded[middle, row : row + size, :]
        total = around(padded, middle, row, size, depth)
        for field in range(3):
            value = diagonal[field, plane, start : start + size, :] * here - halves[field, plane + 1, row : row + size, :] * total
            value = value - around(weighed.at[field], middle, row, size, depth)
            where = slice(at + start, at + start + size), slice(field * lanes, (field + 1) * lanes)
            top = value.astype(bf16)
            upper[where] = top
            lower[where] = (value - top.astype(f32)).astype(bf16)


def operate(depth, count, place, scratch, halves, diagonal, hi, lo, emit):
    padded, weighed, upper_a, lower_a, upper_b, lower_b = scratch
    rows = padded.shape[1] - 2 * pad

    def fill(at, upper, lower):
        for j in range(group):
            middle, plane = place(at + j)
            stencil(padded, halves, diagonal, weighed, middle, plane, j * rows, depth, upper, lower)

    def flush(at, upper, lower):
        big, small = upper[...], lower[...]
        out = jnp.dot(big, hi[...], preferred_element_type=f32)
        out = out + jnp.dot(big, lo[...], preferred_element_type=f32)
        out = out + jnp.dot(small, hi[...], preferred_element_type=f32)
        for j in range(group):
            emit(at + j, out[j * rows : (j + 1) * rows])

    groups = -(-count // group)
    begin = lambda number: jnp.minimum(number * group, count - group)
    fill(0, upper_a, lower_a)

    def one(i, _):
        flush(begin(2 * i), upper_a, lower_a)
        fill(begin(2 * i + 1), upper_b, lower_b)
        flush(begin(2 * i + 1), upper_b, lower_b)
        fill(begin(2 * i + 2), upper_a, lower_a)
        return 0

    lax.fori_loop(0, (groups - 1) // 2, one, 0)
    if groups % 2:
        flush(count - group, upper_a, lower_a)
    else:
        flush(begin(groups - 2), upper_a, lower_a)
        fill(count - group, upper_b, lower_b)
        flush(count - group, upper_b, lower_b)


def strips(padded, local, count, depth, low, high, source, stacked):
    rows = padded.shape[1] - 2 * pad
    for i in range(count):
        at = slice((source + i) * depth, (source + i + 1) * depth) if stacked else source + i
        padded[local + i, pad - depth : pad, :] = low[at]
        padded[local + i, pad + rows : pad + rows + depth, :] = high[at]


def scratch_for(locals_, rows, width):
    padded = pltpu.VMEM((locals_, rows + 2 * pad, lanes), f32)
    weighed = pltpu.VMEM((3, locals_, rows + 2 * pad, lanes), f32)
    return [padded, weighed] + [pltpu.VMEM((group * rows, width), bf16)] * 4 + [pltpu.SemaphoreType.DMA((8,))]


class Run:
    def __init__(self, local, plane, count):
        self.local, self.plane, self.count = local, plane, count


def planes_body(depth, names, outs, pieces, edges, layers, runs, sends, emit, *refs):
    named = dict(zip(names + outs, refs))
    scratch = refs[len(names) + len(outs) :]
    padded, weighed, sem = scratch[0], scratch[1], scratch[-1]
    rows = padded.shape[1] - 2 * pad
    halves, diagonal = named["halves"], named["diagonal"]
    copies = []
    for number, (source, first, count, local) in enumerate(pieces):
        target = padded.at[pl.ds(local, count), pl.ds(pad, rows), :]
        copies.append(pltpu.make_async_copy(named[source].at[pl.ds(first, count)], target, sem.at[number]))
        copies[-1].start()
    for source, local in edges:
        padded[local, pad : pad + rows, :] = named[source][:rows]
    for low, high, first, count, local, stacked in layers:
        strips(padded, local, count, depth, named[low], named[high], first, stacked)
    for copy in copies:
        copy.wait()
    for run in runs:
        weigh(padded, halves, weighed, run.local - 1, run.plane, run.count + 2)
    total = sum(run.count for run in runs)

    def place(i):
        local, plane = i + runs[0].local, i + runs[0].plane
        if len(runs) > 1:
            later = i >= runs[0].count
            local = jnp.where(later, i - runs[0].count + runs[1].local, local)
            plane = jnp.where(later, i - runs[0].count + runs[1].plane, plane)
        return local, plane

    def put(i, out):
        local, plane = place(i)
        emit(named, i, plane, out, padded, local, rows)

    used = pl.ds(0, 2 * lanes if sends else lanes)
    operate(depth, total, place, scratch[:-1], halves, diagonal, named["hi"].at[:, used], named["lo"].at[:, used], put)


def own_emit(named, i, plane, out, padded, local, rows):
    named["rest"][i] = named["right"][plane] - out


def middle_emit(depth, named, i, plane, out, padded, local, rows):
    value = named["rest"][i] - out
    named["residual"][i] = value
    named["low"][i] = value[:depth]
    named["high"][i] = value[rows - depth :]
    if "last" in named:

        @pl.when(i == 0)
        def _():
            named["last"][...] = value

        @pl.when(i == 1)
        def _():
            named["first"][...] = value


def second_emit(split, named, i, plane, out, padded, local, rows):
    here = padded[local, pad : pad + rows, :]
    later = here - step_size * out[:, :lanes]
    fields = named["start"][plane] + step_size * (here + later)
    values = (later, fields, out[:, lanes:])
    if split is None:
        for name, value in zip(("later", "fields", "part"), values):
            named[name][i] = value
    else:

        @pl.when(i < split)
        def _():
            for name, value in zip(("later", "fields", "part"), values):
                named[name][i] = value

        @pl.when(i >= split)
        def _():
            for name, value in zip(("later2", "fields2", "part2"), values):
                named[name][i - split] = value


def over_planes(name, depth, width, operands, outs, pieces, edges, layers, runs, sends, emit, work, ties=()):
    locals_ = max(run.local + run.count + 1 for run in runs)
    operands = dict(operands)
    copied = {piece[0] for piece in pieces} - {edge[0] for edge in edges}
    names = list(operands) + ["tie" + str(number) for number in range(len(ties))]
    rows = operands["diagonal"].shape[2]
    return call(
        functools.partial(planes_body, depth, tuple(names), tuple(outs), pieces, edges, layers, runs, sends, emit),
        [(shape, f32) for shape in outs.values()],
        scratch_for(locals_, rows, width),
        in_specs=[anywhere if key in copied or key.startswith("tie") else whole for key in names],
        work=work,
        name=name,
    )(*operands.values(), *ties)


def sides_body(depth, *refs):
    first, last = refs[-2:]
    planes = refs[0]
    rows = planes.shape[1]
    first[...] = planes[:, :depth, :]
    last[...] = planes[:, rows - depth :, :]


def sides_and_plane_body(depth, which, *refs):
    first, last, plane = refs[-3:]
    planes = refs[0]
    rows = planes.shape[1]
    first[...] = planes[:, :depth, :]
    last[...] = planes[:, rows - depth :, :]
    plane[...] = planes[which]


def last_body(first, later_part, fields_part, came, *refs):
    later, fields, staged, sem = refs[-4:]
    count = came.shape[0]
    planes = later.shape[0]
    piece = 2
    copies = []
    for begin in range(0, count, piece):
        end = min(begin + piece, count)
        for at in range(begin, end):
            staged[0, at] = later_part[at] - step_size * came[at]
            staged[1, at] = fields_part[at] - (step_size * step_size) * came[at]
        wrap = max(begin, min(end, planes - first))
        for which, target in ((0, later), (1, fields)):
            for low, high in ((begin, wrap), (wrap, end)):
                if high > low:
                    goal = (first + low) % planes
                    copy = pltpu.make_async_copy(
                        staged.at[which, pl.ds(low, high - low)], target.at[pl.ds(goal, high - low)], sem.at[len(copies)]
                    )
                    copy.start()
                    copies.append(copy)
    for copy in copies:
        copy.wait()


def add_last(first, shape, later_part, fields_part, came, before):
    count = came.shape[0]
    return call(
        functools.partial(last_body, first),
        [(shape, f32)] * 2,
        [pltpu.VMEM((2,) + came.shape, f32), pltpu.SemaphoreType.DMA((2 * count + 4,))],
        in_specs=[whole] * 3 + [anywhere] * len(before),
        out_specs=[anywhere] * 2,
        aliases={3: 0, 4: 1} if before else {},
        work=0.2,
        name="last",
    )(later_part, fields_part, came, *before)


def shards(right_side, start_field, coefficients, couplings):
    nx, ny, depth, modes = start_field.shape
    rows = ny * depth
    plane = (rows, modes)
    flat = (nx,) + plane
    start = start_field.reshape(flat)
    right = right_side.reshape(flat)
    low, high = nx // 4, (11 * nx) // 16
    width = 3 * modes
    strip = lambda count: ((count, depth, modes), f32)

    def chosen(begin, count, name, *ties):
        (out,) = call(
            functools.partial(chosen_body, begin),
            [((count,) + plane, f32)],
            [pltpu.SemaphoreType.DMA],
            in_specs=[anywhere] * (1 + len(ties)),
            vmem=vmem_bytes if ties else most_bytes,
            name=name,
        )(start, *ties)
        return sent(out, "ma", 1, True)

    raw_1 = chosen(low, high - low, "chosen_1")

    coef = coefficients.reshape(3 * nx, rows)
    layer = ((rows + lanes, lanes), f32)
    first_x, last_x, first_y, last_y = call(
        functools.partial(layers_body, depth),
        [layer] * 4,
        [pltpu.VMEM(flat, f32), pltpu.SemaphoreType.DMA],
        in_specs=[anywhere, whole],
        vmem=most_bytes,
        name="layers",
    )(start, coef)
    low_y = sent(last_y, "gy", 1, True)
    high_y = sent(first_y, "gy", -1, True)
    low_x = sent(last_x, "gx", 1, False)
    high_x = sent(first_x, "gx", -1, False)

    own_hi, own_lo, other_hi, other_lo = call(
        weights_body,
        [((width, 2 * modes), bf16)] * 2 + [((width, modes), bf16)] * 2,
        [pltpu.VMEM((2 * modes, 2 * modes), f32)],
        in_specs=[whole],
        name="weights",
    )(couplings)

    halves_shape = (3, nx + 2, rows + 2 * pad, lanes)
    (halves,) = call(halves_body, [(halves_shape, f32)], [pltpu.VMEM((lanes, rows), f32)], in_specs=[whole], name="halves")(coef)
    halves, diagonal = call(
        functools.partial(diagonal_body, depth),
        [(halves_shape, f32), ((3,) + flat, f32)],
        [],
        in_specs=[whole] * 5,
        aliases={4: 0},
        name="diagonal",
    )(low_x, high_x, low_y, high_y, halves)
    shared = {"halves": halves, "diagonal": diagonal}
    mine = {**shared, "hi": own_hi, "lo": own_lo}
    theirs = {**shared, "hi": other_hi, "lo": other_lo}
    raw_2 = chosen(high, nx - high, "chosen_2", own_hi, diagonal)

    n1, n2, n3 = high - low - 2, nx - high, low + 2
    ring = [Run(1, nx - 1, 1), Run(4, 0, low + 1)]

    def own(name, count, pieces, edges, layers, runs, ties=()):
        operands = {**mine, "start": start, "right": right, "low_y": low_y, "high_y": high_y, "low_x": low_x, "high_x": high_x}
        outs = {"rest": (count,) + plane}
        return over_planes(name, depth, width, operands, outs, pieces, edges, layers, runs, False, own_emit, count / 10, ties)[0]

    rest_1 = own(
        "own_1", n1, [("start", low, n1 + 2, 0)], [], [("low_y", "high_y", low + 1, n1, 1, True)], [Run(1, low + 1, n1)]
    )
    raw_3 = chosen(0, low, "chosen_3", rest_1)

    def sides(chunk, which, name, *ties):
        count = chunk.shape[0]
        body = functools.partial(sides_body, depth) if which is None else functools.partial(sides_and_plane_body, depth, which)
        return call(
            body,
            [strip(count)] * 2 + ([] if which is None else [(plane, f32)]),
            [],
            in_specs=[whole] + [anywhere] * len(ties),
            work=0.1,
            name=name,
        )(chunk, *ties)

    def exchanged(first, last):
        return sent(last, "gy", 1, True), sent(first, "gy", -1, True)

    def middle(name, count, operands, pieces, edges, layers, runs, with_edges, ties=()):
        outs = {"residual": (count,) + plane, "low": (count, depth, modes), "high": (count, depth, modes)}
        if with_edges:
            outs.update({"last": plane, "first": plane})
        emit = functools.partial(middle_emit, depth)
        return over_planes(name, depth, width, {**theirs, **operands}, outs, pieces, edges, layers, runs, False, emit, count / 10, ties)

    def second(name, counts, operands, pieces, edges, layers, runs, ties=(), work=1.0):
        outs = {}
        for number, count in enumerate(counts):
            mark = "" if number == 0 else "2"
            outs.update({key + mark: (count,) + plane for key in ("later", "fields", "part")})
        emit = functools.partial(second_emit, counts[0] if len(counts) > 1 else None)
        operands = {**mine, "start": start, **operands}
        return over_planes(name, depth, width, operands, outs, pieces, edges, layers, runs, True, emit, work, ties)

    raw_low_1, raw_high_1 = exchanged(*sides(raw_1, None, "sides_1"))
    residual_1, first_1, last_1 = middle(
        "middle_1",
        n1,
        {"rest": rest_1, "raw_1": raw_1, "low_1": raw_low_1, "high_1": raw_high_1},
        [("raw_1", 0, n1 + 2, 0)],
        [],
        [("low_1", "high_1", 1, n1, 1, False)],
        [Run(1, low + 1, n1)],
        False,
    )
    low_1, high_1 = exchanged(first_1, last_1)
    rest_2 = own(
        "own_2",
        n2,
        [("start", high - 2, n2 + 2, 0)],
        [],
        [("low_y", "high_y", high - 1, n2, 1, True)],
        [Run(1, high - 1, n2)],
        (first_1,),
    )
    later_1, fields_1, part_1 = second(
        "second_1",
        [n1 - 2],
        {"residual_1": residual_1, "low_1": low_1, "high_1": high_1},
        [("residual_1", 0, n1, 0)],
        [],
        [("low_1", "high_1", 1, n1 - 2, 1, False)],
        [Run(1, low + 2, n1 - 2)],
        (rest_2,),
    )
    came_1 = sent(part_1, "ma", 1, True)

    sides_2 = sides(raw_2, nx - high - 1, "sides_2", part_1)
    raw_low_2, raw_high_2 = exchanged(sides_2[0], sides_2[1])
    raw_low_x = sent(sides_2[2], "gx", 1, False)
    rest_3 = own(
        "own_3",
        n3,
        [("start", nx - 2, 2, 0), ("start", 0, low + 2, 4)],
        [("high_x", 2), ("low_x", 3)],
        [("low_y", "high_y", nx - 1, 1, 1, True), ("low_y", "high_y", 0, low + 1, 4, True)],
        ring,
        (sides_2[0],),
    )
    residual_2, first_2, last_2 = middle(
        "middle_2",
        n2,
        {"rest": rest_2, "raw_1": raw_1, "raw_2": raw_2, "low_1": raw_low_1, "high_1": raw_high_1, "low_2": raw_low_2, "high_2": raw_high_2},
        [("raw_1", high - low - 2, 2, 0), ("raw_2", 0, n2, 2)],
        [],
        [("low_1", "high_1", high - low - 1, 1, 1, False), ("low_2", "high_2", 0, n2 - 1, 2, False)],
        [Run(1, high - 1, n2)],
        False,
        (rest_3,),
    )
    low_2, high_2 = exchanged(first_2, last_2)

    sides_3 = sides(raw_3, 0, "sides_3", first_2)
    raw_low_3, raw_high_3 = exchanged(sides_3[0], sides_3[1])
    raw_high_x = sent(sides_3[2], "gx", -1, False)
    later_2, fields_2, part_2 = second(
        "second_2",
        [n2],
        {"residual_1": residual_1, "residual_2": residual_2, "low_1": low_1, "high_1": high_1, "low_2": low_2, "high_2": high_2},
        [("residual_1", n1 - 2, 2, 0), ("residual_2", 0, n2, 2)],
        [],
        [("low_1", "high_1", n1 - 1, 1, 1, False), ("low_2", "high_2", 0, n2 - 1, 2, False)],
        [Run(1, high - 2, n2)],
        (sides_3[0], raw_low_x),
    )
    came_2 = sent(part_2, "ma", 1, True)
    residual_3, first_3, last_3, edge_last, edge_first = middle(
        "middle_3",
        n3,
        {
            "rest": rest_3,
            "raw_1": raw_1,
            "raw_2": raw_2,
            "raw_3": raw_3,
            "low_x": raw_low_x,
            "high_x": raw_high_x,
            "low_1": raw_low_1,
            "high_1": raw_high_1,
            "low_2": raw_low_2,
            "high_2": raw_high_2,
            "low_3": raw_low_3,
            "high_3": raw_high_3,
        },
        [("raw_2", n2 - 2, 2, 0), ("raw_3", 0, low, 4), ("raw_1", 0, 2, 4 + low)],
        [("high_x", 2), ("low_x", 3)],
        [("low_2", "high_2", n2 - 1, 1, 1, False), ("low_3", "high_3", 0, low, 4, False), ("low_1", "high_1", 0, 1, 4 + low, False)],
        ring,
        True,
        (part_2,),
    )
    low_3, high_3 = exchanged(first_3, last_3)
    next_low_x = sent(edge_last, "gx", 1, False)
    next_high_x = sent(edge_first, "gx", -1, False)
    final = 4
    count = low + 4
    later_3, fields_3, part_3, later_4, fields_4, part_4 = second(
        "second_3",
        [count - final, final],
        {
            "residual_1": residual_1,
            "residual_2": residual_2,
            "residual_3": residual_3,
            "low_x": next_low_x,
            "high_x": next_high_x,
            "low_1": low_1,
            "high_1": high_1,
            "low_2": low_2,
            "high_2": high_2,
            "low_3": low_3,
            "high_3": high_3,
        },
        [("residual_2", n2 - 2, 2, 0), ("residual_3", 0, 1, 2), ("residual_3", 1, low + 1, 5), ("residual_1", 0, 2, 6 + low)],
        [("high_x", 3), ("low_x", 4)],
        [
            ("low_2", "high_2", n2 - 1, 1, 1, False),
            ("low_3", "high_3", 0, 1, 2, False),
            ("low_3", "high_3", 1, low + 1, 5, False),
            ("low_1", "high_1", 0, 1, 6 + low, False),
        ],
        [Run(1, nx - 2, 2), Run(5, 0, low + 2)],
        (came_1,),
        1.0,
    )
    came_3 = sent(part_3, "ma", 1, True)
    came_4 = sent(part_4, "ma", 1, True)

    outs = add_last(low + 2, flat, later_1, fields_1, came_1, ())
    outs = add_last(high - 2, flat, later_2, fields_2, came_2, outs)
    outs = add_last(nx - 2, flat, later_3, fields_3, came_3, outs)
    later, fields = add_last(low + 2 - final, flat, later_4, fields_4, came_4, outs)
    return (fields.reshape(start_field.shape), later.reshape(start_field.shape))


def solution(mesh):
    placed = (P("gx", "gy", None, "ma"), P("gx", "gy", None, "ma"), P(None, "gx", "gy", None), P())
    return jax.shard_map(
        shards,
        mesh=mesh,
        in_specs=placed,
        out_specs=(P("gx", "gy", None, "ma"), P("gx", "gy", None, "ma")),
        check_vma=False,
    )
```

```python
import functools

import jax
import jax.numpy as jnp
from jax import lax
from jax.experimental import pallas as pl
from jax.experimental.pallas import tpu as pltpu
from jax.sharding import PartitionSpec as P

step_size = 0.02
lanes = 128
group = 2
pad = 8
vmem_bytes = 12 * 1024 * 1024
most_bytes = 60 * 1024 * 1024
f32 = jnp.float32
bf16 = jnp.bfloat16
whole = pl.BlockSpec(memory_space=pltpu.VMEM)
anywhere = pl.BlockSpec(memory_space=pl.ANY)


def call(body, out_shapes, scratch, work=1.0, vmem=vmem_bytes, in_specs=None, out_specs=None, aliases=None, name=None):
    return pl.pallas_call(
        body,
        out_shape=[jax.ShapeDtypeStruct(shape, kind) for shape, kind in out_shapes],
        in_specs=in_specs,
        out_specs=out_specs if out_specs is not None else [whole] * len(out_shapes),
        scratch_shapes=scratch,
        input_output_aliases=aliases or {},
        cost_estimate=pl.CostEstimate(flops=int(work * 1e6), bytes_accessed=int(work * 2e3), transcendentals=0),
        compiler_params=pltpu.CompilerParams(vmem_limit_bytes=vmem),
        name=name,
    )


def sent(array, axis, step, periodic):
    count = lax.axis_size(axis)
    pairs = [(i, (i + step) % count) for i in range(count) if periodic or 0 <= i + step < count]
    return lax.ppermute(array, axis, pairs)


def weights_body(couplings_ref, own_hi, own_lo, other_hi, other_lo, turned):
    half = lax.axis_index("ma")
    modes = own_hi.shape[1] // 2
    for field in range(3):
        mine = couplings_ref[field, pl.ds(pl.multiple_of(half * modes, modes), modes), :]
        theirs = couplings_ref[field, pl.ds(pl.multiple_of((1 - half) * modes, modes), modes), :]
        turned[:, :modes] = mine.T
        turned[:, modes:] = theirs.T
        own = turned[pl.ds(pl.multiple_of(half * modes, modes), modes), :]
        other = turned[pl.ds(pl.multiple_of((1 - half) * modes, modes), modes), :modes]
        rows = pl.ds(field * modes, modes)
        top = own.astype(bf16)
        own_hi[rows, :] = top
        own_lo[rows, :] = (own - top.astype(f32)).astype(bf16)
        top = other.astype(bf16)
        other_hi[rows, :] = top
        other_lo[rows, :] = (other - top.astype(f32)).astype(bf16)


def chosen_body(begin, field, *refs):
    out, held, sem = refs[-3:]
    count = out.shape[0]
    piece = 2
    inward, outward = [], []
    for number, at in enumerate(range(0, count, piece)):
        here = pl.ds(at, piece)
        inward.append(pltpu.make_async_copy(field.at[pl.ds(begin + at, piece)], held.at[here], sem.at[0, number]))
        outward.append(pltpu.make_async_copy(held.at[here], out.at[here], sem.at[1, number]))
        inward[-1].start()
    for first, then in zip(inward, outward):
        first.wait()
        then.start()
    for copy in outward:
        copy.wait()


def layers_body(depth, field, coef, first_x, last_x, first_y, last_y, held, sem):
    planes, rows = field.shape[0], field.shape[1]
    pieces = sem.shape[0]
    size = planes // pieces
    copies = []
    for number in range(pieces):
        here = pl.ds(number * size, size)
        copies.append(pltpu.make_async_copy(field.at[here], held.at[here], sem.at[number]))
        copies[-1].start()
    for out in (first_x, last_x, first_y, last_y):
        out[rows : rows + coef.shape[0]] = coef[...]
        out[rows + coef.shape[0] :] = jnp.zeros((out.shape[0] - rows - coef.shape[0], lanes), f32)
    for copy in copies:
        copy.wait()
    first_x[:rows] = held[0]
    last_x[:rows] = held[planes - 1]
    for plane in range(planes):
        first_y[plane * depth : (plane + 1) * depth] = held[plane, :depth]
        last_y[plane * depth : (plane + 1) * depth] = held[plane, rows - depth :]


def halves_body(coef, halves, square):
    count, rows = coef.shape[0], coef.shape[1]
    square[:count] = 0.5 * coef[...]
    square[count:] = jnp.zeros((lanes - count, rows), f32)
    columns = square[...].T
    planes = count // 3
    for plane in range(planes):
        for field in range(3):
            at = field * planes + plane
            halves[field, plane + 1, pad : pad + rows, :] = jnp.broadcast_to(columns[:, at : at + 1], (rows, lanes))


def around(ref, middle, row, size, depth):
    z = lax.broadcasted_iota(jnp.int32, (size, lanes), 0) % depth
    low = jnp.where(z != 0, ref[middle, row - 1 : row - 1 + size, :], 0.0)
    high = jnp.where(z != depth - 1, ref[middle, row + 1 : row + 1 + size, :], 0.0)
    beside = ref[middle, row - depth : row - depth + size, :] + ref[middle, row + depth : row + depth + size, :]
    return (ref[middle - 1, row : row + size, :] + ref[middle + 1, row : row + size, :]) + (beside + (low + high))


def diagonal_body(depth, low_x, high_x, low_y, high_y, halves_in, halves, diagonal):
    planes, rows = diagonal.shape[1], diagonal.shape[2]
    spread = lambda column, height: jnp.broadcast_to(column, (height, lanes))
    before = (0.5 * low_x[rows:]).T
    after = (0.5 * high_x[rows:]).T
    for field in range(3):
        at = field * planes + planes - 1
        halves[field, 0, pad : pad + rows, :] = spread(before[:, at : at + 1], rows)
        at = field * planes
        halves[field, planes + 1, pad : pad + rows, :] = spread(after[:, at : at + 1], rows)
    below = (0.5 * low_y[rows:]).T[rows - depth :]
    above = (0.5 * high_y[rows:]).T[:depth]
    for plane in range(planes):
        for field in range(3):
            at = field * planes + plane
            halves[field, plane + 1, pad - depth : pad, :] = spread(below[:, at : at + 1], depth)
            halves[field, plane + 1, pad + rows : pad + rows + depth, :] = spread(above[:, at : at + 1], depth)
    size = 32

    def one(plane, _):
        for start in range(0, rows, size):
            row = pad + start
            for field in range(3):
                here = halves[field, plane + 1, row : row + size, :]
                diagonal[field, plane, start : start + size, :] = 6.0 * here + around(halves.at[field], plane + 1, row, size, depth)
        return 0

    lax.fori_loop(0, planes, one, 0)


def weigh(padded, halves, weighed, local, first, count):
    size = (padded.shape[1]) // 3

    def one(i, _):
        for start in range(0, padded.shape[1], size):
            value = padded[local + i, start : start + size, :]
            for field in range(3):
                weighed[field, local + i, start : start + size, :] = halves[field, first + i, start : start + size, :] * value
        return 0

    lax.fori_loop(0, count, one, 0)


def stencil(padded, halves, diagonal, weighed, middle, plane, at, depth, upper, lower):
    size = 32
    rows = padded.shape[1] - 2 * pad
    for start in range(0, rows, size):
        row = pad + start
        here = padded[middle, row : row + size, :]
        total = around(padded, middle, row, size, depth)
        for field in range(3):
            value = diagonal[field, plane, start : start + size, :] * here - halves[field, plane + 1, row : row + size, :] * total
            value = value - around(weighed.at[field], middle, row, size, depth)
            where = slice(at + start, at + start + size), slice(field * lanes, (field + 1) * lanes)
            top = value.astype(bf16)
            upper[where] = top
            lower[where] = (value - top.astype(f32)).astype(bf16)


def operate(depth, count, place, scratch, halves, diagonal, hi, lo, emit):
    padded, weighed, upper_a, lower_a, upper_b, lower_b = scratch
    rows = padded.shape[1] - 2 * pad

    def fill(at, upper, lower):
        for j in range(group):
            middle, plane = place(at + j)
            stencil(padded, halves, diagonal, weighed, middle, plane, j * rows, depth, upper, lower)

    def flush(at, upper, lower):
        big, small = upper[...], lower[...]
        out = jnp.dot(big, hi[...], preferred_element_type=f32)
        out = out + jnp.dot(big, lo[...], preferred_element_type=f32)
        out = out + jnp.dot(small, hi[...], preferred_element_type=f32)
        for j in range(group):
            emit(at + j, out[j * rows : (j + 1) * rows])

    groups = -(-count // group)
    begin = lambda number: jnp.minimum(number * group, count - group)
    fill(0, upper_a, lower_a)

    def one(i, _):
        flush(begin(2 * i), upper_a, lower_a)
        fill(begin(2 * i + 1), upper_b, lower_b)
        flush(begin(2 * i + 1), upper_b, lower_b)
        fill(begin(2 * i + 2), upper_a, lower_a)
        return 0

    lax.fori_loop(0, (groups - 1) // 2, one, 0)
    if groups % 2:
        flush(count - group, upper_a, lower_a)
    else:
        flush((groups - 2) * group, upper_a, lower_a)
        fill(count - group, upper_b, lower_b)
        flush(count - group, upper_b, lower_b)


def strips(padded, local, count, depth, low, high, source, stacked):
    rows = padded.shape[1] - 2 * pad
    for i in range(count):
        at = slice((source + i) * depth, (source + i + 1) * depth) if stacked else source + i
        padded[local + i, pad - depth : pad, :] = low[at]
        padded[local + i, pad + rows : pad + rows + depth, :] = high[at]


def scratch_for(locals_, rows, width):
    padded = pltpu.VMEM((locals_, rows + 2 * pad, lanes), f32)
    weighed = pltpu.VMEM((3, locals_, rows + 2 * pad, lanes), f32)
    return [padded, weighed] + [pltpu.VMEM((group * rows, width), bf16)] * 4 + [pltpu.SemaphoreType.DMA((8,))]


class Run:
    def __init__(self, local, plane, count):
        self.local, self.plane, self.count = local, plane, count


def planes_body(depth, names, outs, pieces, edges, layers, runs, sends, emit, *refs):
    named = dict(zip(names + outs, refs))
    scratch = refs[len(names) + len(outs) :]
    padded, weighed, sem = scratch[0], scratch[1], scratch[-1]
    rows = padded.shape[1] - 2 * pad
    halves, diagonal = named["halves"], named["diagonal"]
    copies = []
    for number, (source, first, count, local) in enumerate(pieces):
        target = padded.at[pl.ds(local, count), pl.ds(pad, rows), :]
        copies.append(pltpu.make_async_copy(named[source].at[pl.ds(first, count)], target, sem.at[number]))
        copies[-1].start()
    for source, local in edges:
        padded[local, pad : pad + rows, :] = named[source][:rows]
    for low, high, first, count, local, stacked in layers:
        strips(padded, local, count, depth, named[low], named[high], first, stacked)
    for copy in copies:
        copy.wait()
    for run in runs:
        weigh(padded, halves, weighed, run.local - 1, run.plane, run.count + 2)
    total = sum(run.count for run in runs)

    def place(i):
        local, plane = i + runs[0].local, i + runs[0].plane
        if len(runs) > 1 and isinstance(i, int):
            run = runs[0] if i < runs[0].count else runs[1]
            return i - (0 if i < runs[0].count else runs[0].count) + run.local, i - (0 if i < runs[0].count else runs[0].count) + run.plane
        if len(runs) > 1:
            later = i >= runs[0].count
            local = jnp.where(later, i - runs[0].count + runs[1].local, local)
            plane = jnp.where(later, i - runs[0].count + runs[1].plane, plane)
        return local, plane

    def put(i, out):
        local, plane = place(i)
        emit(named, i, plane, out, padded, local, rows)

    used = pl.ds(0, 2 * lanes if sends else lanes)
    operate(depth, total, place, scratch[:-1], halves, diagonal, named["hi"].at[:, used], named["lo"].at[:, used], put)
    if "last" in named:
        named["last"][...] = named["residual"][0]
        named["first"][...] = named["residual"][1]


def own_emit(named, i, plane, out, padded, local, rows):
    named["rest"][i] = named["right"][plane] - out


def middle_emit(depth, named, i, plane, out, padded, local, rows):
    value = named["rest"][i] - out
    named["residual"][i] = value
    named["low"][i] = value[:depth]
    named["high"][i] = value[rows - depth :]


def second_emit(split, named, i, plane, out, padded, local, rows):
    here = padded[local, pad : pad + rows, :]
    later = here - step_size * out[:, :lanes]
    fields = named["start"][plane] + step_size * (here + later)
    values = (later, fields, out[:, lanes:])
    named["later"][i], named["fields"][i] = later, fields
    if split is not None and isinstance(i, int) and i >= split:
        named["part2"][i - split] = out[:, lanes:]
    else:
        named["part"][i] = out[:, lanes:]


def over_planes(name, depth, width, operands, outs, pieces, edges, layers, runs, sends, emit, work, ties=()):
    locals_ = max(run.local + run.count + 1 for run in runs)
    operands = dict(operands)
    copied = {piece[0] for piece in pieces} - {edge[0] for edge in edges}
    names = list(operands) + ["tie" + str(number) for number in range(len(ties))]
    rows = operands["diagonal"].shape[2]
    return call(
        functools.partial(planes_body, depth, tuple(names), tuple(outs), pieces, edges, layers, runs, sends, emit),
        [(shape, f32) for shape in outs.values()],
        scratch_for(locals_, rows, width),
        in_specs=[anywhere if key in copied or key.startswith("tie") else whole for key in names],
        work=work,
        name=name,
    )(*operands.values(), *ties)


def sides_body(depth, *refs):
    first, last = refs[-2:]
    planes = refs[0]
    rows = planes.shape[1]
    first[...] = planes[:, :depth, :]
    last[...] = planes[:, rows - depth :, :]


def handed_body(first, last, tie, first_out, last_out):
    first_out[...] = first[...]
    last_out[...] = last[...]


def sides_and_plane_body(depth, which, *refs):
    first, last, plane = refs[-3:]
    planes = refs[0]
    rows = planes.shape[1]
    first[...] = planes[:, :depth, :]
    last[...] = planes[:, rows - depth :, :]
    plane[...] = planes[which]


def last_body(first, skip, later_part, fields_part, came, *refs):
    later, fields, staged, sem = refs[-4:]
    count = came.shape[0]
    planes = later.shape[0]
    piece = 2
    copies = []
    for begin in range(0, count, piece):
        end = min(begin + piece, count)
        for at in range(begin, end):
            staged[0, at] = later_part[skip + at] - step_size * came[at]
            staged[1, at] = fields_part[skip + at] - (step_size * step_size) * came[at]
        wrap = max(begin, min(end, planes - first))
        for which, target in ((0, later), (1, fields)):
            for low, high in ((begin, wrap), (wrap, end)):
                if high > low:
                    goal = (first + low) % planes
                    copy = pltpu.make_async_copy(
                        staged.at[which, pl.ds(low, high - low)], target.at[pl.ds(goal, high - low)], sem.at[len(copies)]
                    )
                    copy.start()
                    copies.append(copy)
    for copy in copies:
        copy.wait()


def add_last(first, shape, later_part, fields_part, came, before, skip=0):
    count = came.shape[0]
    return call(
        functools.partial(last_body, first, skip),
        [(shape, f32)] * 2,
        [pltpu.VMEM((2,) + came.shape, f32), pltpu.SemaphoreType.DMA((2 * count + 4,))],
        in_specs=[whole] * 3 + [anywhere] * len(before),
        out_specs=[anywhere] * 2,
        aliases={3: 0, 4: 1} if before else {},
        work=0.2,
        name="last",
    )(later_part, fields_part, came, *before)


def shards(right_side, start_field, coefficients, couplings):
    nx, ny, depth, modes = start_field.shape
    rows = ny * depth
    plane = (rows, modes)
    flat = (nx,) + plane
    start = start_field.reshape(flat)
    right = right_side.reshape(flat)
    low, high = (3 * nx) // 16, (5 * nx) // 8
    width = 3 * modes
    strip = lambda count: ((count, depth, modes), f32)

    def chosen(begin, count, name, *ties):
        (out,) = call(
            functools.partial(chosen_body, begin),
            [((count,) + plane, f32)],
            [pltpu.VMEM((count,) + plane, f32), pltpu.SemaphoreType.DMA((2, count))],
            in_specs=[anywhere] * (1 + len(ties)),
            out_specs=[anywhere],
            vmem=vmem_bytes if ties else most_bytes,
            name=name,
        )(start, *ties)
        return sent(out, "ma", 1, True)

    raw_1 = chosen(low, high - low, "chosen_1")

    coef = coefficients.reshape(3 * nx, rows)
    layer = ((rows + lanes, lanes), f32)
    first_x, last_x, first_y, last_y = call(
        functools.partial(layers_body, depth),
        [layer] * 4,
        [pltpu.VMEM(flat, f32), pltpu.SemaphoreType.DMA((8,))],
        in_specs=[anywhere, whole],
        vmem=most_bytes,
        name="layers",
    )(start, coef)
    low_y = sent(last_y, "gy", 1, True)
    high_y = sent(first_y, "gy", -1, True)
    low_x = sent(last_x, "gx", 1, False)
    high_x = sent(first_x, "gx", -1, False)

    own_hi, own_lo, other_hi, other_lo = call(
        weights_body,
        [((width, 2 * modes), bf16)] * 2 + [((width, modes), bf16)] * 2,
        [pltpu.VMEM((2 * modes, 2 * modes), f32)],
        in_specs=[whole],
        name="weights",
    )(couplings)

    halves_shape = (3, nx + 2, rows + 2 * pad, lanes)
    (halves,) = call(halves_body, [(halves_shape, f32)], [pltpu.VMEM((lanes, rows), f32)], in_specs=[whole], name="halves")(coef)
    halves, diagonal = call(
        functools.partial(diagonal_body, depth),
        [(halves_shape, f32), ((3,) + flat, f32)],
        [],
        in_specs=[whole] * 5,
        aliases={4: 0},
        name="diagonal",
    )(low_x, high_x, low_y, high_y, halves)
    shared = {"halves": halves, "diagonal": diagonal}
    mine = {**shared, "hi": own_hi, "lo": own_lo}
    theirs = {**shared, "hi": other_hi, "lo": other_lo}
    raw_2 = chosen(high, nx - high, "chosen_2", own_hi, diagonal)

    n1, n2, n3 = high - low - 2, nx - high, low + 2
    ring = [Run(1, nx - 1, 1), Run(4, 0, low + 1)]

    def own(name, count, pieces, edges, layers, runs, ties=()):
        operands = {**mine, "start": start, "right": right, "low_y": low_y, "high_y": high_y, "low_x": low_x, "high_x": high_x}
        outs = {"rest": (count,) + plane}
        return over_planes(name, depth, width, operands, outs, pieces, edges, layers, runs, False, own_emit, count / 10, ties)[0]

    rest_1 = own(
        "own_1", n1, [("start", low, n1 + 2, 0)], [], [("low_y", "high_y", low + 1, n1, 1, True)], [Run(1, low + 1, n1)]
    )
    raw_3 = chosen(0, low, "chosen_3", rest_1)

    def sides(chunk, which, name, *ties):
        count = chunk.shape[0]
        body = functools.partial(sides_body, depth) if which is None else functools.partial(sides_and_plane_body, depth, which)
        return call(
            body,
            [strip(count)] * 2 + ([] if which is None else [(plane, f32)]),
            [],
            in_specs=[whole] + [anywhere] * len(ties),
            work=0.1,
            name=name,
        )(chunk, *ties)

    def exchanged(first, last):
        return sent(last, "gy", 1, True), sent(first, "gy", -1, True)

    def middle(name, count, operands, pieces, edges, layers, runs, with_edges, ties=()):
        outs = {"residual": (count,) + plane, "low": (count, depth, modes), "high": (count, depth, modes)}
        if with_edges:
            outs.update({"last": plane, "first": plane})
        emit = functools.partial(middle_emit, depth)
        return over_planes(name, depth, width, {**theirs, **operands}, outs, pieces, edges, layers, runs, False, emit, count / 10, ties)

    def second(name, counts, operands, pieces, edges, layers, runs, ties=(), work=1.0):
        outs = {key: (sum(counts),) + plane for key in ("later", "fields")}
        outs["part"] = (counts[0],) + plane
        if len(counts) > 1:
            outs["part2"] = (counts[1],) + plane
        emit = functools.partial(second_emit, counts[0] if len(counts) > 1 else None)
        operands = {**mine, "start": start, **operands}
        return over_planes(name, depth, width, operands, outs, pieces, edges, layers, runs, True, emit, work, ties)

    sides_1 = sides(raw_1, None, "sides_1", rest_1)
    raw_low_1, raw_high_1 = exchanged(*sides_1)
    rest_2 = own(
        "own_2",
        n2,
        [("start", high - 2, n2 + 2, 0)],
        [],
        [("low_y", "high_y", high - 1, n2, 1, True)],
        [Run(1, high - 1, n2)],
        (sides_1[0],),
    )
    residual_1, first_1, last_1 = middle(
        "middle_1",
        n1,
        {"rest": rest_1, "raw_1": raw_1, "low_1": raw_low_1, "high_1": raw_high_1},
        [("raw_1", 0, n1 + 2, 0)],
        [],
        [("low_1", "high_1", 1, n1, 1, False)],
        [Run(1, low + 1, n1)],
        False,
        (rest_2,),
    )
    low_1, high_1 = exchanged(first_1, last_1)
    rest_3 = own(
        "own_3",
        n3,
        [("start", nx - 2, 2, 0), ("start", 0, low + 2, 4)],
        [("high_x", 2), ("low_x", 3)],
        [("low_y", "high_y", nx - 1, 1, 1, True), ("low_y", "high_y", 0, low + 1, 4, True)],
        ring,
        (first_1,),
    )
    later_1, fields_1, part_1 = second(
        "second_1",
        [n1 - 2],
        {"residual_1": residual_1, "low_1": low_1, "high_1": high_1},
        [("residual_1", 0, n1, 0)],
        [],
        [("low_1", "high_1", 1, n1 - 2, 1, False)],
        [Run(1, low + 2, n1 - 2)],
        (rest_3,),
    )
    came_1 = sent(part_1, "ma", 1, True)

    sides_2 = sides(raw_2, nx - high - 1, "sides_2", part_1)
    raw_low_2, raw_high_2 = exchanged(sides_2[0], sides_2[1])
    raw_low_x = sent(sides_2[2], "gx", 1, False)
    residual_2, first_2, last_2 = middle(
        "middle_2",
        n2,
        {"rest": rest_2, "raw_1": raw_1, "raw_2": raw_2, "low_1": raw_low_1, "high_1": raw_high_1, "low_2": raw_low_2, "high_2": raw_high_2},
        [("raw_1", high - low - 2, 2, 0), ("raw_2", 0, n2, 2)],
        [],
        [("low_1", "high_1", high - low - 1, 1, 1, False), ("low_2", "high_2", 0, n2 - 1, 2, False)],
        [Run(1, high - 1, n2)],
        False,
    )
    low_2, high_2 = exchanged(first_2, last_2)

    sides_3 = sides(raw_3, 0, "sides_3", first_2)
    raw_low_3, raw_high_3 = exchanged(sides_3[0], sides_3[1])
    raw_high_x = sent(sides_3[2], "gx", -1, False)
    later_2, fields_2, part_2 = second(
        "second_2",
        [n2],
        {"residual_1": residual_1, "residual_2": residual_2, "low_1": low_1, "high_1": high_1, "low_2": low_2, "high_2": high_2},
        [("residual_1", n1 - 2, 2, 0), ("residual_2", 0, n2, 2)],
        [],
        [("low_1", "high_1", n1 - 1, 1, 1, False), ("low_2", "high_2", 0, n2 - 1, 2, False)],
        [Run(1, high - 2, n2)],
        (sides_3[0], raw_low_x),
    )
    came_2 = sent(part_2, "ma", 1, True)
    residual_3, first_3, last_3, edge_last, edge_first = middle(
        "middle_3",
        n3,
        {
            "rest": rest_3,
            "raw_1": raw_1,
            "raw_2": raw_2,
            "raw_3": raw_3,
            "low_x": raw_low_x,
            "high_x": raw_high_x,
            "low_1": raw_low_1,
            "high_1": raw_high_1,
            "low_2": raw_low_2,
            "high_2": raw_high_2,
            "low_3": raw_low_3,
            "high_3": raw_high_3,
        },
        [("raw_2", n2 - 2, 2, 0), ("raw_3", 0, low, 4), ("raw_1", 0, 2, 4 + low)],
        [("high_x", 2), ("low_x", 3)],
        [("low_2", "high_2", n2 - 1, 1, 1, False), ("low_3", "high_3", 0, low, 4, False), ("low_1", "high_1", 0, 1, 4 + low, False)],
        ring,
        True,
        (part_2,),
    )
    next_low_x = sent(edge_last, "gx", 1, False)
    next_high_x = sent(edge_first, "gx", -1, False)
    low_3, high_3 = exchanged(
        *call(
            handed_body,
            [strip(n3)] * 2,
            [],
            in_specs=[whole] * 2 + [anywhere],
            work=0.1,
            name="handed",
        )(first_3, last_3, came_1)
    )
    final = 2 * group if -(-(low + 4) // group) % 2 == 0 else group
    count = low + 4
    later_3, fields_3, part_3, part_4 = second(
        "second_3",
        [count - final, final],
        {
            "residual_1": residual_1,
            "residual_2": residual_2,
            "residual_3": residual_3,
            "low_x": next_low_x,
            "high_x": next_high_x,
            "low_1": low_1,
            "high_1": high_1,
            "low_2": low_2,
            "high_2": high_2,
            "low_3": low_3,
            "high_3": high_3,
        },
        [("residual_2", n2 - 2, 2, 0), ("residual_3", 0, 1, 2), ("residual_3", 1, low + 1, 5), ("residual_1", 0, 2, 6 + low)],
        [("high_x", 3), ("low_x", 4)],
        [
            ("low_2", "high_2", n2 - 1, 1, 1, False),
            ("low_3", "high_3", 0, 1, 2, False),
            ("low_3", "high_3", 1, low + 1, 5, False),
            ("low_1", "high_1", 0, 1, 6 + low, False),
        ],
        [Run(1, nx - 2, 2), Run(5, 0, low + 2)],
        (came_1,),
        1.0,
    )
    came_3 = sent(part_3, "ma", 1, True)
    came_4 = sent(part_4, "ma", 1, True)

    outs = add_last(low + 2, flat, later_1, fields_1, came_1, ())
    outs = add_last(high - 2, flat, later_2, fields_2, came_2, outs)
    outs = add_last(nx - 2, flat, later_3, fields_3, came_3, outs)
    later, fields = add_last(low + 2 - final, flat, later_3, fields_3, came_4, outs, count - final)
    return (fields.reshape(start_field.shape), later.reshape(start_field.shape))


def solution(mesh):
    placed = (P("gx", "gy", None, "ma"), P("gx", "gy", None, "ma"), P(None, "gx", "gy", None), P())
    return jax.shard_map(
        shards,
        mesh=mesh,
        in_specs=placed,
        out_specs=(P("gx", "gy", None, "ma"), P("gx", "gy", None, "ma")),
        check_vma=False,
    )
```

```python
import functools

import jax
import jax.numpy as jnp
from jax import lax
from jax.experimental import pallas as pl
from jax.experimental.pallas import tpu as pltpu
from jax.sharding import PartitionSpec as P

step_size = 0.02
lanes = 128
group = 2
pad = 8
vmem_bytes = 12 * 1024 * 1024
most_bytes = 60 * 1024 * 1024
f32 = jnp.float32
bf16 = jnp.bfloat16
whole = pl.BlockSpec(memory_space=pltpu.VMEM)
anywhere = pl.BlockSpec(memory_space=pl.ANY)


def call(body, out_shapes, scratch, work=1.0, vmem=vmem_bytes, in_specs=None, out_specs=None, aliases=None, name=None):
    return pl.pallas_call(
        body,
        out_shape=[jax.ShapeDtypeStruct(shape, kind) for shape, kind in out_shapes],
        in_specs=in_specs,
        out_specs=out_specs if out_specs is not None else [whole] * len(out_shapes),
        scratch_shapes=scratch,
        input_output_aliases=aliases or {},
        cost_estimate=pl.CostEstimate(flops=int(work * 1e9), bytes_accessed=int(work * 2e6), transcendentals=0),
        compiler_params=pltpu.CompilerParams(vmem_limit_bytes=vmem),
        name=name,
    )


def sent(array, axis, step, periodic):
    count = lax.axis_size(axis)
    pairs = [(i, (i + step) % count) for i in range(count) if periodic or 0 <= i + step < count]
    return lax.ppermute(array, axis, pairs)


def weights_body(couplings_ref, own_hi, own_lo, other_hi, other_lo, turned):
    half = lax.axis_index("ma")
    modes = own_hi.shape[1] // 2
    for field in range(3):
        mine = couplings_ref[field, pl.ds(pl.multiple_of(half * modes, modes), modes), :]
        theirs = couplings_ref[field, pl.ds(pl.multiple_of((1 - half) * modes, modes), modes), :]
        turned[:, :modes] = mine.T
        turned[:, modes:] = theirs.T
        own = turned[pl.ds(pl.multiple_of(half * modes, modes), modes), :]
        other = turned[pl.ds(pl.multiple_of((1 - half) * modes, modes), modes), :modes]
        rows = pl.ds(field * modes, modes)
        top = own.astype(bf16)
        own_hi[rows, :] = top
        own_lo[rows, :] = (own - top.astype(f32)).astype(bf16)
        top = other.astype(bf16)
        other_hi[rows, :] = top
        other_lo[rows, :] = (other - top.astype(f32)).astype(bf16)


def chosen_body(begin, field, *refs):
    out, sem = refs[-2:]
    copy = pltpu.make_async_copy(field.at[pl.ds(begin, out.shape[0])], out, sem)
    copy.start()
    copy.wait()


def layers_body(depth, field, coef, first_x, last_x, first_y, last_y, held, sem):
    planes, rows = field.shape[0], field.shape[1]
    pieces = sem.shape[0]
    size = planes // pieces
    copies = []
    for number in range(pieces):
        here = pl.ds(number * size, size)
        copies.append(pltpu.make_async_copy(field.at[here], held.at[here], sem.at[number]))
        copies[-1].start()
    for out in (first_x, last_x, first_y, last_y):
        out[rows : rows + coef.shape[0]] = coef[...]
        out[rows + coef.shape[0] :] = jnp.zeros((out.shape[0] - rows - coef.shape[0], lanes), f32)
    for copy in copies:
        copy.wait()
    first_x[:rows] = held[0]
    last_x[:rows] = held[planes - 1]
    for plane in range(planes):
        first_y[plane * depth : (plane + 1) * depth] = held[plane, :depth]
        last_y[plane * depth : (plane + 1) * depth] = held[plane, rows - depth :]


def halves_body(coef, halves, square):
    count, rows = coef.shape[0], coef.shape[1]
    square[:count] = 0.5 * coef[...]
    square[count:] = jnp.zeros((lanes - count, rows), f32)
    columns = square[...].T
    planes = count // 3
    for plane in range(planes):
        for field in range(3):
            at = field * planes + plane
            halves[field, plane + 1, pad : pad + rows, :] = jnp.broadcast_to(columns[:, at : at + 1], (rows, lanes))


def around(ref, middle, row, size, depth):
    z = lax.broadcasted_iota(jnp.int32, (size, lanes), 0) % depth
    low = jnp.where(z != 0, ref[middle, row - 1 : row - 1 + size, :], 0.0)
    high = jnp.where(z != depth - 1, ref[middle, row + 1 : row + 1 + size, :], 0.0)
    beside = ref[middle, row - depth : row - depth + size, :] + ref[middle, row + depth : row + depth + size, :]
    return (ref[middle - 1, row : row + size, :] + ref[middle + 1, row : row + size, :]) + (beside + (low + high))


def diagonal_body(depth, low_x, high_x, low_y, high_y, halves_in, halves, diagonal):
    planes, rows = diagonal.shape[1], diagonal.shape[2]
    spread = lambda column, height: jnp.broadcast_to(column, (height, lanes))
    before = (0.5 * low_x[rows:]).T
    after = (0.5 * high_x[rows:]).T
    for field in range(3):
        at = field * planes + planes - 1
        halves[field, 0, pad : pad + rows, :] = spread(before[:, at : at + 1], rows)
        at = field * planes
        halves[field, planes + 1, pad : pad + rows, :] = spread(after[:, at : at + 1], rows)
    below = (0.5 * low_y[rows:]).T[rows - depth :]
    above = (0.5 * high_y[rows:]).T[:depth]
    for plane in range(planes):
        for field in range(3):
            at = field * planes + plane
            halves[field, plane + 1, pad - depth : pad, :] = spread(below[:, at : at + 1], depth)
            halves[field, plane + 1, pad + rows : pad + rows + depth, :] = spread(above[:, at : at + 1], depth)
    size = 32

    def one(plane, _):
        for start in range(0, rows, size):
            row = pad + start
            for field in range(3):
                here = halves[field, plane + 1, row : row + size, :]
                diagonal[field, plane, start : start + size, :] = 6.0 * here + around(halves.at[field], plane + 1, row, size, depth)
        return 0

    lax.fori_loop(0, planes, one, 0)


def weigh(padded, halves, weighed, local, first, count):
    size = (padded.shape[1]) // 3

    def one(i, _):
        for start in range(0, padded.shape[1], size):
            value = padded[local + i, start : start + size, :]
            for field in range(3):
                weighed[field, local + i, start : start + size, :] = halves[field, first + i, start : start + size, :] * value
        return 0

    lax.fori_loop(0, count, one, 0)


def stencil(padded, halves, diagonal, weighed, middle, plane, at, depth, upper, lower):
    size = 32
    rows = padded.shape[1] - 2 * pad
    for start in range(0, rows, size):
        row = pad + start
        here = padded[middle, row : row + size, :]
        total = around(padded, middle, row, size, depth)
        for field in range(3):
            value = diagonal[field, plane, start : start + size, :] * here - halves[field, plane + 1, row : row + size, :] * total
            value = value - around(weighed.at[field], middle, row, size, depth)
            where = slice(at + start, at + start + size), slice(field * lanes, (field + 1) * lanes)
            top = value.astype(bf16)
            upper[where] = top
            lower[where] = (value - top.astype(f32)).astype(bf16)


def operate(depth, count, place, scratch, halves, diagonal, hi, lo, emit):
    padded, weighed, upper_a, lower_a, upper_b, lower_b = scratch
    rows = padded.shape[1] - 2 * pad

    def fill(at, upper, lower):
        for j in range(group):
            middle, plane = place(at + j)
            stencil(padded, halves, diagonal, weighed, middle, plane, j * rows, depth, upper, lower)

    def flush(at, upper, lower):
        big, small = upper[...], lower[...]
        out = jnp.dot(big, hi[...], preferred_element_type=f32)
        out = out + jnp.dot(big, lo[...], preferred_element_type=f32)
        out = out + jnp.dot(small, hi[...], preferred_element_type=f32)
        for j in range(group):
            emit(at + j, out[j * rows : (j + 1) * rows])

    groups = -(-count // group)
    begin = lambda number: jnp.minimum(number * group, count - group)
    fill(0, upper_a, lower_a)

    def one(i, _):
        flush(begin(2 * i), upper_a, lower_a)
        fill(begin(2 * i + 1), upper_b, lower_b)
        flush(begin(2 * i + 1), upper_b, lower_b)
        fill(begin(2 * i + 2), upper_a, lower_a)
        return 0

    lax.fori_loop(0, (groups - 1) // 2, one, 0)
    if groups % 2:
        flush(count - group, upper_a, lower_a)
    else:
        flush((groups - 2) * group, upper_a, lower_a)
        fill(count - group, upper_b, lower_b)
        flush(count - group, upper_b, lower_b)


def strips(padded, local, count, depth, low, high, source, stacked):
    rows = padded.shape[1] - 2 * pad
    for i in range(count):
        at = slice((source + i) * depth, (source + i + 1) * depth) if stacked else source + i
        padded[local + i, pad - depth : pad, :] = low[at]
        padded[local + i, pad + rows : pad + rows + depth, :] = high[at]


def scratch_for(locals_, rows, width):
    padded = pltpu.VMEM((locals_, rows + 2 * pad, lanes), f32)
    weighed = pltpu.VMEM((3, locals_, rows + 2 * pad, lanes), f32)
    return [padded, weighed] + [pltpu.VMEM((group * rows, width), bf16)] * 4 + [pltpu.SemaphoreType.DMA((8,))]


class Run:
    def __init__(self, local, plane, count):
        self.local, self.plane, self.count = local, plane, count


def planes_body(depth, names, outs, pieces, edges, layers, runs, sends, emit, *refs):
    named = dict(zip(names + outs, refs))
    scratch = refs[len(names) + len(outs) :]
    padded, weighed, sem = scratch[0], scratch[1], scratch[-1]
    rows = padded.shape[1] - 2 * pad
    halves, diagonal = named["halves"], named["diagonal"]
    copies = []
    for number, (source, first, count, local) in enumerate(pieces):
        target = padded.at[pl.ds(local, count), pl.ds(pad, rows), :]
        copies.append(pltpu.make_async_copy(named[source].at[pl.ds(first, count)], target, sem.at[number]))
        copies[-1].start()
    for source, local in edges:
        padded[local, pad : pad + rows, :] = named[source][:rows]
    for low, high, first, count, local, stacked in layers:
        strips(padded, local, count, depth, named[low], named[high], first, stacked)
    for copy in copies:
        copy.wait()
    for run in runs:
        weigh(padded, halves, weighed, run.local - 1, run.plane, run.count + 2)
    total = sum(run.count for run in runs)

    def place(i):
        local, plane = i + runs[0].local, i + runs[0].plane
        if len(runs) > 1 and isinstance(i, int):
            run = runs[0] if i < runs[0].count else runs[1]
            return i - (0 if i < runs[0].count else runs[0].count) + run.local, i - (0 if i < runs[0].count else runs[0].count) + run.plane
        if len(runs) > 1:
            later = i >= runs[0].count
            local = jnp.where(later, i - runs[0].count + runs[1].local, local)
            plane = jnp.where(later, i - runs[0].count + runs[1].plane, plane)
        return local, plane

    def put(i, out):
        local, plane = place(i)
        emit(named, i, plane, out, padded, local, rows)

    used = pl.ds(0, 2 * lanes if sends else lanes)
    operate(depth, total, place, scratch[:-1], halves, diagonal, named["hi"].at[:, used], named["lo"].at[:, used], put)
    if "last" in named:
        named["last"][...] = named["residual"][0]
        named["first"][...] = named["residual"][1]


def own_emit(named, i, plane, out, padded, local, rows):
    named["rest"][i] = named["right"][plane] - out


def middle_emit(depth, named, i, plane, out, padded, local, rows):
    value = named["rest"][i] - out
    named["residual"][i] = value
    named["low"][i] = value[:depth]
    named["high"][i] = value[rows - depth :]


def second_emit(split, named, i, plane, out, padded, local, rows):
    here = padded[local, pad : pad + rows, :]
    later = here - step_size * out[:, :lanes]
    fields = named["start"][plane] + step_size * (here + later)
    values = (later, fields, out[:, lanes:])
    named["later"][i], named["fields"][i] = later, fields
    if split is not None and isinstance(i, int) and i >= split:
        named["part2"][i - split] = out[:, lanes:]
    else:
        named["part"][i] = out[:, lanes:]


def over_planes(name, depth, width, operands, outs, pieces, edges, layers, runs, sends, emit, work, ties=()):
    locals_ = max(run.local + run.count + 1 for run in runs)
    operands = dict(operands)
    copied = {piece[0] for piece in pieces} - {edge[0] for edge in edges}
    names = list(operands) + ["tie" + str(number) for number in range(len(ties))]
    rows = operands["diagonal"].shape[2]
    return call(
        functools.partial(planes_body, depth, tuple(names), tuple(outs), pieces, edges, layers, runs, sends, emit),
        [(shape, f32) for shape in outs.values()],
        scratch_for(locals_, rows, width),
        in_specs=[anywhere if key in copied or key.startswith("tie") else whole for key in names],
        work=work,
        name=name,
    )(*operands.values(), *ties)


def sides_body(depth, *refs):
    first, last = refs[-2:]
    planes = refs[0]
    rows = planes.shape[1]
    first[...] = planes[:, :depth, :]
    last[...] = planes[:, rows - depth :, :]


def handed_body(first, last, tie, first_out, last_out):
    first_out[...] = first[...]
    last_out[...] = last[...]


def sides_and_plane_body(depth, which, *refs):
    first, last, plane = refs[-3:]
    planes = refs[0]
    rows = planes.shape[1]
    first[...] = planes[:, :depth, :]
    last[...] = planes[:, rows - depth :, :]
    plane[...] = planes[which]


def last_body(first, skip, later_part, fields_part, came, *refs):
    later, fields, staged, sem = refs[-4:]
    count = came.shape[0]
    planes = later.shape[0]
    piece = 2
    copies = []
    for begin in range(0, count, piece):
        end = min(begin + piece, count)
        for at in range(begin, end):
            staged[0, at] = later_part[skip + at] - step_size * came[at]
            staged[1, at] = fields_part[skip + at] - (step_size * step_size) * came[at]
        wrap = max(begin, min(end, planes - first))
        for which, target in ((0, later), (1, fields)):
            for low, high in ((begin, wrap), (wrap, end)):
                if high > low:
                    goal = (first + low) % planes
                    copy = pltpu.make_async_copy(
                        staged.at[which, pl.ds(low, high - low)], target.at[pl.ds(goal, high - low)], sem.at[len(copies)]
                    )
                    copy.start()
                    copies.append(copy)
    for copy in copies:
        copy.wait()


def add_last(first, shape, later_part, fields_part, came, before, skip=0):
    count = came.shape[0]
    return call(
        functools.partial(last_body, first, skip),
        [(shape, f32)] * 2,
        [pltpu.VMEM((2,) + came.shape, f32), pltpu.SemaphoreType.DMA((2 * count + 4,))],
        in_specs=[whole] * 3 + [anywhere] * len(before),
        out_specs=[anywhere] * 2,
        aliases={3: 0, 4: 1} if before else {},
        work=0.2,
        name="last",
    )(later_part, fields_part, came, *before)


def shards(right_side, start_field, coefficients, couplings):
    nx, ny, depth, modes = start_field.shape
    rows = ny * depth
    plane = (rows, modes)
    flat = (nx,) + plane
    start = start_field.reshape(flat)
    right = right_side.reshape(flat)
    low, high = (3 * nx) // 16, (5 * nx) // 8
    width = 3 * modes
    strip = lambda count: ((count, depth, modes), f32)

    def chosen(begin, count, name, *ties):
        (out,) = call(
            functools.partial(chosen_body, begin),
            [((count,) + plane, f32)],
            [pltpu.SemaphoreType.DMA],
            in_specs=[anywhere] * (1 + len(ties)),
            vmem=vmem_bytes,
            name=name,
        )(start, *ties)
        return sent(out, "ma", 1, True)

    raw_1 = chosen(low, high - low, "chosen_1")

    coef = coefficients.reshape(3 * nx, rows)
    layer = ((rows + lanes, lanes), f32)
    first_x, last_x, first_y, last_y = call(
        functools.partial(layers_body, depth),
        [layer] * 4,
        [pltpu.VMEM(flat, f32), pltpu.SemaphoreType.DMA((8,))],
        in_specs=[anywhere, whole],
        name="layers",
    )(start, coef)
    low_y = sent(last_y, "gy", 1, True)
    high_y = sent(first_y, "gy", -1, True)
    low_x = sent(last_x, "gx", 1, False)
    high_x = sent(first_x, "gx", -1, False)

    own_hi, own_lo, other_hi, other_lo = call(
        weights_body,
        [((width, 2 * modes), bf16)] * 2 + [((width, modes), bf16)] * 2,
        [pltpu.VMEM((2 * modes, 2 * modes), f32)],
        in_specs=[whole],
        name="weights",
    )(couplings)

    halves_shape = (3, nx + 2, rows + 2 * pad, lanes)
    (halves,) = call(halves_body, [(halves_shape, f32)], [pltpu.VMEM((lanes, rows), f32)], in_specs=[whole], name="halves")(coef)
    halves, diagonal = call(
        functools.partial(diagonal_body, depth),
        [(halves_shape, f32), ((3,) + flat, f32)],
        [],
        in_specs=[whole] * 5,
        aliases={4: 0},
        name="diagonal",
    )(low_x, high_x, low_y, high_y, halves)
    shared = {"halves": halves, "diagonal": diagonal}
    mine = {**shared, "hi": own_hi, "lo": own_lo}
    theirs = {**shared, "hi": other_hi, "lo": other_lo}
    raw_2 = chosen(high, nx - high, "chosen_2", own_hi, diagonal)

    n1, n2, n3 = high - low - 2, nx - high, low + 2
    ring = [Run(1, nx - 1, 1), Run(4, 0, low + 1)]

    def own(name, count, pieces, edges, layers, runs, ties=()):
        operands = {**mine, "start": start, "right": right, "low_y": low_y, "high_y": high_y, "low_x": low_x, "high_x": high_x}
        outs = {"rest": (count,) + plane}
        return over_planes(name, depth, width, operands, outs, pieces, edges, layers, runs, False, own_emit, count / 10, ties)[0]

    rest_1 = own(
        "own_1", n1, [("start", low, n1 + 2, 0)], [], [("low_y", "high_y", low + 1, n1, 1, True)], [Run(1, low + 1, n1)]
    )
    raw_3 = chosen(0, low, "chosen_3", rest_1)

    def sides(chunk, which, name, *ties):
        count = chunk.shape[0]
        body = functools.partial(sides_body, depth) if which is None else functools.partial(sides_and_plane_body, depth, which)
        return call(
            body,
            [strip(count)] * 2 + ([] if which is None else [(plane, f32)]),
            [],
            in_specs=[whole] + [anywhere] * len(ties),
            work=0.1,
            name=name,
        )(chunk, *ties)

    def exchanged(first, last):
        return sent(last, "gy", 1, True), sent(first, "gy", -1, True)

    def middle(name, count, operands, pieces, edges, layers, runs, with_edges, ties=()):
        outs = {"residual": (count,) + plane, "low": (count, depth, modes), "high": (count, depth, modes)}
        if with_edges:
            outs.update({"last": plane, "first": plane})
        emit = functools.partial(middle_emit, depth)
        return over_planes(name, depth, width, {**theirs, **operands}, outs, pieces, edges, layers, runs, False, emit, count / 10, ties)

    def second(name, counts, operands, pieces, edges, layers, runs, ties=(), work=1.0):
        outs = {key: (sum(counts),) + plane for key in ("later", "fields")}
        outs["part"] = (counts[0],) + plane
        if len(counts) > 1:
            outs["part2"] = (counts[1],) + plane
        emit = functools.partial(second_emit, counts[0] if len(counts) > 1 else None)
        operands = {**mine, "start": start, **operands}
        return over_planes(name, depth, width, operands, outs, pieces, edges, layers, runs, True, emit, work, ties)

    sides_1 = sides(raw_1, None, "sides_1", rest_1)
    raw_low_1, raw_high_1 = exchanged(*sides_1)
    rest_2 = own(
        "own_2",
        n2,
        [("start", high - 2, n2 + 2, 0)],
        [],
        [("low_y", "high_y", high - 1, n2, 1, True)],
        [Run(1, high - 1, n2)],
        (sides_1[0],),
    )
    residual_1, first_1, last_1 = middle(
        "middle_1",
        n1,
        {"rest": rest_1, "raw_1": raw_1, "low_1": raw_low_1, "high_1": raw_high_1},
        [("raw_1", 0, n1 + 2, 0)],
        [],
        [("low_1", "high_1", 1, n1, 1, False)],
        [Run(1, low + 1, n1)],
        False,
        (rest_2,),
    )
    low_1, high_1 = exchanged(first_1, last_1)
    rest_3 = own(
        "own_3",
        n3,
        [("start", nx - 2, 2, 0), ("start", 0, low + 2, 4)],
        [("high_x", 2), ("low_x", 3)],
        [("low_y", "high_y", nx - 1, 1, 1, True), ("low_y", "high_y", 0, low + 1, 4, True)],
        ring,
        (first_1,),
    )
    later_1, fields_1, part_1 = second(
        "second_1",
        [n1 - 2],
        {"residual_1": residual_1, "low_1": low_1, "high_1": high_1},
        [("residual_1", 0, n1, 0)],
        [],
        [("low_1", "high_1", 1, n1 - 2, 1, False)],
        [Run(1, low + 2, n1 - 2)],
        (rest_3,),
    )
    came_1 = sent(part_1, "ma", 1, True)

    sides_2 = sides(raw_2, nx - high - 1, "sides_2", part_1)
    raw_low_2, raw_high_2 = exchanged(sides_2[0], sides_2[1])
    raw_low_x = sent(sides_2[2], "gx", 1, False)
    residual_2, first_2, last_2 = middle(
        "middle_2",
        n2,
        {"rest": rest_2, "raw_1": raw_1, "raw_2": raw_2, "low_1": raw_low_1, "high_1": raw_high_1, "low_2": raw_low_2, "high_2": raw_high_2},
        [("raw_1", high - low - 2, 2, 0), ("raw_2", 0, n2, 2)],
        [],
        [("low_1", "high_1", high - low - 1, 1, 1, False), ("low_2", "high_2", 0, n2 - 1, 2, False)],
        [Run(1, high - 1, n2)],
        False,
    )
    low_2, high_2 = exchanged(first_2, last_2)

    sides_3 = sides(raw_3, 0, "sides_3", first_2)
    raw_low_3, raw_high_3 = exchanged(sides_3[0], sides_3[1])
    raw_high_x = sent(sides_3[2], "gx", -1, False)
    later_2, fields_2, part_2 = second(
        "second_2",
        [n2],
        {"residual_1": residual_1, "residual_2": residual_2, "low_1": low_1, "high_1": high_1, "low_2": low_2, "high_2": high_2},
        [("residual_1", n1 - 2, 2, 0), ("residual_2", 0, n2, 2)],
        [],
        [("low_1", "high_1", n1 - 1, 1, 1, False), ("low_2", "high_2", 0, n2 - 1, 2, False)],
        [Run(1, high - 2, n2)],
        (sides_3[0], raw_low_x),
    )
    came_2 = sent(part_2, "ma", 1, True)
    residual_3, first_3, last_3, edge_last, edge_first = middle(
        "middle_3",
        n3,
        {
            "rest": rest_3,
            "raw_1": raw_1,
            "raw_2": raw_2,
            "raw_3": raw_3,
            "low_x": raw_low_x,
            "high_x": raw_high_x,
            "low_1": raw_low_1,
            "high_1": raw_high_1,
            "low_2": raw_low_2,
            "high_2": raw_high_2,
            "low_3": raw_low_3,
            "high_3": raw_high_3,
        },
        [("raw_2", n2 - 2, 2, 0), ("raw_3", 0, low, 4), ("raw_1", 0, 2, 4 + low)],
        [("high_x", 2), ("low_x", 3)],
        [("low_2", "high_2", n2 - 1, 1, 1, False), ("low_3", "high_3", 0, low, 4, False), ("low_1", "high_1", 0, 1, 4 + low, False)],
        ring,
        True,
        (part_2,),
    )
    next_low_x = sent(edge_last, "gx", 1, False)
    next_high_x = sent(edge_first, "gx", -1, False)
    low_3, high_3 = exchanged(
        *call(
            handed_body,
            [strip(n3)] * 2,
            [],
            in_specs=[whole] * 2 + [anywhere],
            work=0.1,
            name="handed",
        )(first_3, last_3, came_1)
    )
    final = 2 * group if -(-(low + 4) // group) % 2 == 0 else group
    count = low + 4
    later_3, fields_3, part_3, part_4 = second(
        "second_3",
        [count - final, final],
        {
            "residual_1": residual_1,
            "residual_2": residual_2,
            "residual_3": residual_3,
            "low_x": next_low_x,
            "high_x": next_high_x,
            "low_1": low_1,
            "high_1": high_1,
            "low_2": low_2,
            "high_2": high_2,
            "low_3": low_3,
            "high_3": high_3,
        },
        [("residual_2", n2 - 2, 2, 0), ("residual_3", 0, 1, 2), ("residual_3", 1, low + 1, 5), ("residual_1", 0, 2, 6 + low)],
        [("high_x", 3), ("low_x", 4)],
        [
            ("low_2", "high_2", n2 - 1, 1, 1, False),
            ("low_3", "high_3", 0, 1, 2, False),
            ("low_3", "high_3", 1, low + 1, 5, False),
            ("low_1", "high_1", 0, 1, 6 + low, False),
        ],
        [Run(1, nx - 2, 2), Run(5, 0, low + 2)],
        (came_1,),
        1.0,
    )
    came_3 = sent(part_3, "ma", 1, True)
    came_4 = sent(part_4, "ma", 1, True)

    outs = add_last(low + 2, flat, later_1, fields_1, came_1, ())
    outs = add_last(high - 2, flat, later_2, fields_2, came_2, outs)
    outs = add_last(nx - 2, flat, later_3, fields_3, came_3, outs)
    later, fields = add_last(low + 2 - final, flat, later_3, fields_3, came_4, outs, count - final)
    return (fields.reshape(start_field.shape), later.reshape(start_field.shape))


def solution(mesh):
    placed = (P("gx", "gy", None, "ma"), P("gx", "gy", None, "ma"), P(None, "gx", "gy", None), P())
    return jax.shard_map(
        shards,
        mesh=mesh,
        in_specs=placed,
        out_specs=(P("gx", "gy", None, "ma"), P("gx", "gy", None, "ma")),
        check_vma=False,
    )
```

```python
import functools

import jax
import jax.numpy as jnp
from jax import lax
from jax.experimental import pallas as pl
from jax.experimental.pallas import tpu as pltpu
from jax.sharding import PartitionSpec as P

step_size = 0.02
lanes = 128
group = 2
pad = 8
vmem_bytes = 12 * 1024 * 1024
first_bytes = 60 * 1024 * 1024
f32 = jnp.float32
bf16 = jnp.bfloat16
whole = pl.BlockSpec(memory_space=pltpu.VMEM)
anywhere = pl.BlockSpec(memory_space=pl.ANY)


def call(body, out_shapes, scratch, work=1.0, vmem=vmem_bytes, in_specs=None, out_specs=None, aliases=None, name=None):
    return pl.pallas_call(
        body,
        out_shape=[jax.ShapeDtypeStruct(shape, kind) for shape, kind in out_shapes],
        in_specs=in_specs,
        out_specs=out_specs if out_specs is not None else [whole] * len(out_shapes),
        scratch_shapes=scratch,
        input_output_aliases=aliases or {},
        cost_estimate=pl.CostEstimate(flops=int(work * 1e9), bytes_accessed=int(work * 2e6), transcendentals=0),
        compiler_params=pltpu.CompilerParams(vmem_limit_bytes=vmem),
        name=name,
    )


def sent(array, axis, step, periodic):
    count = lax.axis_size(axis)
    pairs = [(i, (i + step) % count) for i in range(count) if periodic or 0 <= i + step < count]
    return lax.ppermute(array, axis, pairs)


def weights_body(couplings_ref, own_hi, own_lo, other_hi, other_lo, turned):
    half = lax.axis_index("ma")
    modes = own_hi.shape[1] // 2
    for field in range(3):
        mine = couplings_ref[field, pl.ds(pl.multiple_of(half * modes, modes), modes), :]
        theirs = couplings_ref[field, pl.ds(pl.multiple_of((1 - half) * modes, modes), modes), :]
        turned[:, :modes] = mine.T
        turned[:, modes:] = theirs.T
        own = turned[pl.ds(pl.multiple_of(half * modes, modes), modes), :]
        other = turned[pl.ds(pl.multiple_of((1 - half) * modes, modes), modes), :modes]
        rows = pl.ds(field * modes, modes)
        top = own.astype(bf16)
        own_hi[rows, :] = top
        own_lo[rows, :] = (own - top.astype(f32)).astype(bf16)
        top = other.astype(bf16)
        other_hi[rows, :] = top
        other_lo[rows, :] = (other - top.astype(f32)).astype(bf16)


def chosen_body(begin, field, *refs):
    out, sem = refs[-2:]
    copy = pltpu.make_async_copy(field.at[pl.ds(begin, out.shape[0])], out, sem)
    copy.start()
    copy.wait()


def layers_body(depth, field, coef, first_x, last_x, first_y, last_y, held, sem):
    planes, rows = field.shape[0], field.shape[1]
    pieces = sem.shape[0]
    size = planes // pieces
    copies = []
    for number in range(pieces):
        here = pl.ds(number * size, size)
        copies.append(pltpu.make_async_copy(field.at[here], held.at[here], sem.at[number]))
        copies[-1].start()
    for out in (first_x, last_x, first_y, last_y):
        out[rows : rows + coef.shape[0]] = coef[...]
        out[rows + coef.shape[0] :] = jnp.zeros((out.shape[0] - rows - coef.shape[0], lanes), f32)
    for copy in copies:
        copy.wait()
    first_x[:rows] = held[0]
    last_x[:rows] = held[planes - 1]
    for plane in range(planes):
        first_y[plane * depth : (plane + 1) * depth] = held[plane, :depth]
        last_y[plane * depth : (plane + 1) * depth] = held[plane, rows - depth :]


def halves_body(coef, halves, square):
    count, rows = coef.shape[0], coef.shape[1]
    square[:count] = 0.5 * coef[...]
    square[count:] = jnp.zeros((lanes - count, rows), f32)
    columns = square[...].T
    planes = count // 3
    for plane in range(planes):
        for field in range(3):
            at = field * planes + plane
            halves[field, plane + 1, pad : pad + rows, :] = jnp.broadcast_to(columns[:, at : at + 1], (rows, lanes))


def around(ref, middle, row, size, depth):
    z = lax.broadcasted_iota(jnp.int32, (size, lanes), 0) % depth
    low = jnp.where(z != 0, ref[middle, row - 1 : row - 1 + size, :], 0.0)
    high = jnp.where(z != depth - 1, ref[middle, row + 1 : row + 1 + size, :], 0.0)
    beside = ref[middle, row - depth : row - depth + size, :] + ref[middle, row + depth : row + depth + size, :]
    return (ref[middle - 1, row : row + size, :] + ref[middle + 1, row : row + size, :]) + (beside + (low + high))


def diagonal_body(depth, low_x, high_x, low_y, high_y, halves_in, halves, diagonal):
    planes, rows = diagonal.shape[1], diagonal.shape[2]
    spread = lambda column, height: jnp.broadcast_to(column, (height, lanes))
    before = (0.5 * low_x[rows:]).T
    after = (0.5 * high_x[rows:]).T
    for field in range(3):
        at = field * planes + planes - 1
        halves[field, 0, pad : pad + rows, :] = spread(before[:, at : at + 1], rows)
        at = field * planes
        halves[field, planes + 1, pad : pad + rows, :] = spread(after[:, at : at + 1], rows)
    below = (0.5 * low_y[rows:]).T[rows - depth :]
    above = (0.5 * high_y[rows:]).T[:depth]
    for plane in range(planes):
        for field in range(3):
            at = field * planes + plane
            halves[field, plane + 1, pad - depth : pad, :] = spread(below[:, at : at + 1], depth)
            halves[field, plane + 1, pad + rows : pad + rows + depth, :] = spread(above[:, at : at + 1], depth)
    size = 32

    def one(plane, _):
        for start in range(0, rows, size):
            row = pad + start
            for field in range(3):
                here = halves[field, plane + 1, row : row + size, :]
                diagonal[field, plane, start : start + size, :] = 6.0 * here + around(halves.at[field], plane + 1, row, size, depth)
        return 0

    lax.fori_loop(0, planes, one, 0)


def weigh(padded, halves, weighed, local, first, count):
    size = (padded.shape[1]) // 3

    def one(i, _):
        for start in range(0, padded.shape[1], size):
            value = padded[local + i, start : start + size, :]
            for field in range(3):
                weighed[field, local + i, start : start + size, :] = halves[field, first + i, start : start + size, :] * value
        return 0

    lax.fori_loop(0, count, one, 0)


def stencil(padded, halves, diagonal, weighed, middle, plane, at, depth, upper, lower):
    size = 32
    rows = padded.shape[1] - 2 * pad
    for start in range(0, rows, size):
        row = pad + start
        here = padded[middle, row : row + size, :]
        total = around(padded, middle, row, size, depth)
        for field in range(3):
            value = diagonal[field, plane, start : start + size, :] * here - halves[field, plane + 1, row : row + size, :] * total
            value = value - around(weighed.at[field], middle, row, size, depth)
            where = slice(at + start, at + start + size), slice(field * lanes, (field + 1) * lanes)
            top = value.astype(bf16)
            upper[where] = top
            lower[where] = (value - top.astype(f32)).astype(bf16)


def operate(depth, count, place, scratch, halves, diagonal, hi, lo, emit):
    padded, weighed, upper_a, lower_a, upper_b, lower_b = scratch
    rows = padded.shape[1] - 2 * pad

    def fill(at, upper, lower):
        for j in range(group):
            middle, plane = place(at + j)
            stencil(padded, halves, diagonal, weighed, middle, plane, j * rows, depth, upper, lower)

    def flush(at, upper, lower):
        big, small = upper[...], lower[...]
        out = jnp.dot(big, hi[...], preferred_element_type=f32)
        out = out + jnp.dot(big, lo[...], preferred_element_type=f32)
        out = out + jnp.dot(small, hi[...], preferred_element_type=f32)
        for j in range(group):
            emit(at + j, out[j * rows : (j + 1) * rows])

    groups = -(-count // group)
    begin = lambda number: jnp.minimum(number * group, count - group)
    fill(0, upper_a, lower_a)

    def one(i, _):
        flush(begin(2 * i), upper_a, lower_a)
        fill(begin(2 * i + 1), upper_b, lower_b)
        flush(begin(2 * i + 1), upper_b, lower_b)
        fill(begin(2 * i + 2), upper_a, lower_a)
        return 0

    lax.fori_loop(0, (groups - 1) // 2, one, 0)
    if groups % 2:
        flush(count - group, upper_a, lower_a)
    else:
        flush((groups - 2) * group, upper_a, lower_a)
        fill(count - group, upper_b, lower_b)
        flush(count - group, upper_b, lower_b)


def strips(padded, local, count, depth, low, high, source, stacked):
    rows = padded.shape[1] - 2 * pad
    for i in range(count):
        at = slice((source + i) * depth, (source + i + 1) * depth) if stacked else source + i
        padded[local + i, pad - depth : pad, :] = low[at]
        padded[local + i, pad + rows : pad + rows + depth, :] = high[at]


def scratch_for(locals_, rows, width):
    padded = pltpu.VMEM((locals_, rows + 2 * pad, lanes), f32)
    weighed = pltpu.VMEM((3, locals_, rows + 2 * pad, lanes), f32)
    return [padded, weighed] + [pltpu.VMEM((group * rows, width), bf16)] * 4 + [pltpu.SemaphoreType.DMA((8,))]


class Run:
    def __init__(self, local, plane, count):
        self.local, self.plane, self.count = local, plane, count


def planes_body(depth, names, outs, pieces, edges, layers, runs, sends, emit, *refs):
    named = dict(zip(names + outs, refs))
    scratch = refs[len(names) + len(outs) :]
    padded, weighed, sem = scratch[0], scratch[1], scratch[-1]
    rows = padded.shape[1] - 2 * pad
    halves, diagonal = named["halves"], named["diagonal"]
    copies = []
    for number, (source, first, count, local) in enumerate(pieces):
        target = padded.at[pl.ds(local, count), pl.ds(pad, rows), :]
        copies.append(pltpu.make_async_copy(named[source].at[pl.ds(first, count)], target, sem.at[number]))
        copies[-1].start()
    for source, local in edges:
        padded[local, pad : pad + rows, :] = named[source][:rows]
    for low, high, first, count, local, stacked in layers:
        strips(padded, local, count, depth, named[low], named[high], first, stacked)
    for copy in copies:
        copy.wait()
    for run in runs:
        weigh(padded, halves, weighed, run.local - 1, run.plane, run.count + 2)
    total = sum(run.count for run in runs)

    def place(i):
        local, plane = i + runs[0].local, i + runs[0].plane
        if len(runs) > 1 and isinstance(i, int):
            run = runs[0] if i < runs[0].count else runs[1]
            return i - (0 if i < runs[0].count else runs[0].count) + run.local, i - (0 if i < runs[0].count else runs[0].count) + run.plane
        if len(runs) > 1:
            later = i >= runs[0].count
            local = jnp.where(later, i - runs[0].count + runs[1].local, local)
            plane = jnp.where(later, i - runs[0].count + runs[1].plane, plane)
        return local, plane

    def put(i, out):
        local, plane = place(i)
        emit(named, i, plane, out, padded, local, rows)

    used = pl.ds(0, 2 * lanes if sends else lanes)
    operate(depth, total, place, scratch[:-1], halves, diagonal, named["hi"].at[:, used], named["lo"].at[:, used], put)
    if "last" in named:
        named["last"][...] = named["residual"][0]
        named["first"][...] = named["residual"][1]


def own_emit(named, i, plane, out, padded, local, rows):
    named["rest"][i] = named["right"][plane] - out


def middle_emit(depth, named, i, plane, out, padded, local, rows):
    value = named["rest"][i] - out
    named["residual"][i] = value
    named["low"][i] = value[:depth]
    named["high"][i] = value[rows - depth :]


def second_emit(split, named, i, plane, out, padded, local, rows):
    here = padded[local, pad : pad + rows, :]
    later = here - step_size * out[:, :lanes]
    fields = named["start"][plane] + step_size * (here + later)
    values = (later, fields, out[:, lanes:])
    named["later"][i], named["fields"][i] = later, fields
    if split is not None and isinstance(i, int) and i >= split:
        named["part2"][i - split] = out[:, lanes:]
    else:
        named["part"][i] = out[:, lanes:]


def over_planes(name, depth, width, operands, outs, pieces, edges, layers, runs, sends, emit, work, ties=()):
    locals_ = max(run.local + run.count + 1 for run in runs)
    operands = dict(operands)
    copied = {piece[0] for piece in pieces} - {edge[0] for edge in edges}
    names = list(operands) + ["tie" + str(number) for number in range(len(ties))]
    rows = operands["diagonal"].shape[2]
    return call(
        functools.partial(planes_body, depth, tuple(names), tuple(outs), pieces, edges, layers, runs, sends, emit),
        [(shape, f32) for shape in outs.values()],
        scratch_for(locals_, rows, width),
        in_specs=[anywhere if key in copied or key.startswith("tie") else whole for key in names],
        work=work,
        name=name,
    )(*operands.values(), *ties)


def sides_body(depth, *refs):
    first, last = refs[-2:]
    planes = refs[0]
    rows = planes.shape[1]
    first[...] = planes[:, :depth, :]
    last[...] = planes[:, rows - depth :, :]


def handed_body(first, last, tie, first_out, last_out):
    first_out[...] = first[...]
    last_out[...] = last[...]


def sides_and_plane_body(depth, which, *refs):
    first, last, plane = refs[-3:]
    planes = refs[0]
    rows = planes.shape[1]
    first[...] = planes[:, :depth, :]
    last[...] = planes[:, rows - depth :, :]
    plane[...] = planes[which]


def last_body(first, skip, later_part, fields_part, came, *refs):
    later, fields, staged, sem = refs[-4:]
    count = came.shape[0]
    planes = later.shape[0]
    piece = 2
    copies = []
    for begin in range(0, count, piece):
        end = min(begin + piece, count)
        for at in range(begin, end):
            staged[0, at] = later_part[skip + at] - step_size * came[at]
            staged[1, at] = fields_part[skip + at] - (step_size * step_size) * came[at]
        wrap = max(begin, min(end, planes - first))
        for which, target in ((0, later), (1, fields)):
            for low, high in ((begin, wrap), (wrap, end)):
                if high > low:
                    goal = (first + low) % planes
                    copy = pltpu.make_async_copy(
                        staged.at[which, pl.ds(low, high - low)], target.at[pl.ds(goal, high - low)], sem.at[len(copies)]
                    )
                    copy.start()
                    copies.append(copy)
    for copy in copies:
        copy.wait()


def add_last(first, shape, later_part, fields_part, came, before, skip=0):
    count = came.shape[0]
    return call(
        functools.partial(last_body, first, skip),
        [(shape, f32)] * 2,
        [pltpu.VMEM((2,) + came.shape, f32), pltpu.SemaphoreType.DMA((2 * count + 4,))],
        in_specs=[whole] * 3 + [anywhere] * len(before),
        out_specs=[anywhere] * 2,
        aliases={3: 0, 4: 1} if before else {},
        work=0.2,
        name="last",
    )(later_part, fields_part, came, *before)


def shards(right_side, start_field, coefficients, couplings):
    nx, ny, depth, modes = start_field.shape
    rows = ny * depth
    plane = (rows, modes)
    flat = (nx,) + plane
    start = start_field.reshape(flat)
    right = right_side.reshape(flat)
    low, high = (3 * nx) // 16, (5 * nx) // 8
    width = 3 * modes
    strip = lambda count: ((count, depth, modes), f32)

    def chosen(begin, count, name, *ties):
        (out,) = call(
            functools.partial(chosen_body, begin),
            [((count,) + plane, f32)],
            [pltpu.SemaphoreType.DMA],
            in_specs=[anywhere] * (1 + len(ties)),
            vmem=vmem_bytes if ties else first_bytes,
            name=name,
        )(start, *ties)
        return sent(out, "ma", 1, True)

    raw_1 = chosen(low, high - low, "chosen_1")

    coef = coefficients.reshape(3 * nx, rows)
    layer = ((rows + lanes, lanes), f32)
    first_x, last_x, first_y, last_y = call(
        functools.partial(layers_body, depth),
        [layer] * 4,
        [pltpu.VMEM(flat, f32), pltpu.SemaphoreType.DMA((8,))],
        in_specs=[anywhere, whole],
        name="layers",
    )(start, coef)
    low_y = sent(last_y, "gy", 1, True)
    high_y = sent(first_y, "gy", -1, True)
    low_x = sent(last_x, "gx", 1, False)
    high_x = sent(first_x, "gx", -1, False)

    own_hi, own_lo, other_hi, other_lo = call(
        weights_body,
        [((width, 2 * modes), bf16)] * 2 + [((width, modes), bf16)] * 2,
        [pltpu.VMEM((2 * modes, 2 * modes), f32)],
        in_specs=[whole],
        name="weights",
    )(couplings)

    halves_shape = (3, nx + 2, rows + 2 * pad, lanes)
    (halves,) = call(halves_body, [(halves_shape, f32)], [pltpu.VMEM((lanes, rows), f32)], in_specs=[whole], name="halves")(coef)
    halves, diagonal = call(
        functools.partial(diagonal_body, depth),
        [(halves_shape, f32), ((3,) + flat, f32)],
        [],
        in_specs=[whole] * 5,
        aliases={4: 0},
        name="diagonal",
    )(low_x, high_x, low_y, high_y, halves)
    shared = {"halves": halves, "diagonal": diagonal}
    mine = {**shared, "hi": own_hi, "lo": own_lo}
    theirs = {**shared, "hi": other_hi, "lo": other_lo}
    raw_2 = chosen(high, nx - high, "chosen_2", own_hi, diagonal)

    n1, n2, n3 = high - low - 2, nx - high, low + 2
    ring = [Run(1, nx - 1, 1), Run(4, 0, low + 1)]

    def own(name, count, pieces, edges, layers, runs, ties=()):
        operands = {**mine, "start": start, "right": right, "low_y": low_y, "high_y": high_y, "low_x": low_x, "high_x": high_x}
        outs = {"rest": (count,) + plane}
        return over_planes(name, depth, width, operands, outs, pieces, edges, layers, runs, False, own_emit, count / 10, ties)[0]

    rest_1 = own(
        "own_1", n1, [("start", low, n1 + 2, 0)], [], [("low_y", "high_y", low + 1, n1, 1, True)], [Run(1, low + 1, n1)]
    )
    raw_3 = chosen(0, low, "chosen_3", rest_1)

    def sides(chunk, which, name, *ties):
        count = chunk.shape[0]
        body = functools.partial(sides_body, depth) if which is None else functools.partial(sides_and_plane_body, depth, which)
        return call(
            body,
            [strip(count)] * 2 + ([] if which is None else [(plane, f32)]),
            [],
            in_specs=[whole] + [anywhere] * len(ties),
            work=0.1,
            name=name,
        )(chunk, *ties)

    def exchanged(first, last):
        return sent(last, "gy", 1, True), sent(first, "gy", -1, True)

    def middle(name, count, operands, pieces, edges, layers, runs, with_edges, ties=()):
        outs = {"residual": (count,) + plane, "low": (count, depth, modes), "high": (count, depth, modes)}
        if with_edges:
            outs.update({"last": plane, "first": plane})
        emit = functools.partial(middle_emit, depth)
        return over_planes(name, depth, width, {**theirs, **operands}, outs, pieces, edges, layers, runs, False, emit, count / 10, ties)

    def second(name, counts, operands, pieces, edges, layers, runs, ties=(), work=1.0):
        outs = {key: (sum(counts),) + plane for key in ("later", "fields")}
        outs["part"] = (counts[0],) + plane
        if len(counts) > 1:
            outs["part2"] = (counts[1],) + plane
        emit = functools.partial(second_emit, counts[0] if len(counts) > 1 else None)
        operands = {**mine, "start": start, **operands}
        return over_planes(name, depth, width, operands, outs, pieces, edges, layers, runs, True, emit, work, ties)

    sides_1 = sides(raw_1, None, "sides_1", rest_1)
    raw_low_1, raw_high_1 = exchanged(*sides_1)
    rest_2 = own(
        "own_2",
        n2,
        [("start", high - 2, n2 + 2, 0)],
        [],
        [("low_y", "high_y", high - 1, n2, 1, True)],
        [Run(1, high - 1, n2)],
        (sides_1[0],),
    )
    residual_1, first_1, last_1 = middle(
        "middle_1",
        n1,
        {"rest": rest_1, "raw_1": raw_1, "low_1": raw_low_1, "high_1": raw_high_1},
        [("raw_1", 0, n1 + 2, 0)],
        [],
        [("low_1", "high_1", 1, n1, 1, False)],
        [Run(1, low + 1, n1)],
        False,
        (rest_2,),
    )
    low_1, high_1 = exchanged(first_1, last_1)
    rest_3 = own(
        "own_3",
        n3,
        [("start", nx - 2, 2, 0), ("start", 0, low + 2, 4)],
        [("high_x", 2), ("low_x", 3)],
        [("low_y", "high_y", nx - 1, 1, 1, True), ("low_y", "high_y", 0, low + 1, 4, True)],
        ring,
        (first_1,),
    )
    later_1, fields_1, part_1 = second(
        "second_1",
        [n1 - 2],
        {"residual_1": residual_1, "low_1": low_1, "high_1": high_1},
        [("residual_1", 0, n1, 0)],
        [],
        [("low_1", "high_1", 1, n1 - 2, 1, False)],
        [Run(1, low + 2, n1 - 2)],
        (rest_3,),
    )
    came_1 = sent(part_1, "ma", 1, True)

    sides_2 = sides(raw_2, nx - high - 1, "sides_2", part_1)
    raw_low_2, raw_high_2 = exchanged(sides_2[0], sides_2[1])
    raw_low_x = sent(sides_2[2], "gx", 1, False)
    residual_2, first_2, last_2 = middle(
        "middle_2",
        n2,
        {"rest": rest_2, "raw_1": raw_1, "raw_2": raw_2, "low_1": raw_low_1, "high_1": raw_high_1, "low_2": raw_low_2, "high_2": raw_high_2},
        [("raw_1", high - low - 2, 2, 0), ("raw_2", 0, n2, 2)],
        [],
        [("low_1", "high_1", high - low - 1, 1, 1, False), ("low_2", "high_2", 0, n2 - 1, 2, False)],
        [Run(1, high - 1, n2)],
        False,
    )
    low_2, high_2 = exchanged(first_2, last_2)

    sides_3 = sides(raw_3, 0, "sides_3", first_2)
    raw_low_3, raw_high_3 = exchanged(sides_3[0], sides_3[1])
    raw_high_x = sent(sides_3[2], "gx", -1, False)
    later_2, fields_2, part_2 = second(
        "second_2",
        [n2],
        {"residual_1": residual_1, "residual_2": residual_2, "low_1": low_1, "high_1": high_1, "low_2": low_2, "high_2": high_2},
        [("residual_1", n1 - 2, 2, 0), ("residual_2", 0, n2, 2)],
        [],
        [("low_1", "high_1", n1 - 1, 1, 1, False), ("low_2", "high_2", 0, n2 - 1, 2, False)],
        [Run(1, high - 2, n2)],
        (sides_3[0], raw_low_x),
        4.0,
    )
    came_2 = sent(part_2, "ma", 1, True)
    residual_3, first_3, last_3, edge_last, edge_first = middle(
        "middle_3",
        n3,
        {
            "rest": rest_3,
            "raw_1": raw_1,
            "raw_2": raw_2,
            "raw_3": raw_3,
            "low_x": raw_low_x,
            "high_x": raw_high_x,
            "low_1": raw_low_1,
            "high_1": raw_high_1,
            "low_2": raw_low_2,
            "high_2": raw_high_2,
            "low_3": raw_low_3,
            "high_3": raw_high_3,
        },
        [("raw_2", n2 - 2, 2, 0), ("raw_3", 0, low, 4), ("raw_1", 0, 2, 4 + low)],
        [("high_x", 2), ("low_x", 3)],
        [("low_2", "high_2", n2 - 1, 1, 1, False), ("low_3", "high_3", 0, low, 4, False), ("low_1", "high_1", 0, 1, 4 + low, False)],
        ring,
        True,
        (part_2,),
    )
    next_low_x = sent(edge_last, "gx", 1, False)
    next_high_x = sent(edge_first, "gx", -1, False)
    low_3, high_3 = exchanged(
        *call(
            handed_body,
            [strip(n3)] * 2,
            [],
            in_specs=[whole] * 2 + [anywhere],
            work=0.1,
            name="handed",
        )(first_3, last_3, came_1)
    )
    final = 2 * group if -(-(low + 4) // group) % 2 == 0 else group
    count = low + 4
    later_3, fields_3, part_3, part_4 = second(
        "second_3",
        [count - final, final],
        {
            "residual_1": residual_1,
            "residual_2": residual_2,
            "residual_3": residual_3,
            "low_x": next_low_x,
            "high_x": next_high_x,
            "low_1": low_1,
            "high_1": high_1,
            "low_2": low_2,
            "high_2": high_2,
            "low_3": low_3,
            "high_3": high_3,
        },
        [("residual_2", n2 - 2, 2, 0), ("residual_3", 0, 1, 2), ("residual_3", 1, low + 1, 5), ("residual_1", 0, 2, 6 + low)],
        [("high_x", 3), ("low_x", 4)],
        [
            ("low_2", "high_2", n2 - 1, 1, 1, False),
            ("low_3", "high_3", 0, 1, 2, False),
            ("low_3", "high_3", 1, low + 1, 5, False),
            ("low_1", "high_1", 0, 1, 6 + low, False),
        ],
        [Run(1, nx - 2, 2), Run(5, 0, low + 2)],
        (came_1,),
        2.0,
    )
    came_3 = sent(part_3, "ma", 1, True)
    came_4 = sent(part_4, "ma", 1, True)

    outs = add_last(low + 2, flat, later_1, fields_1, came_1, ())
    outs = add_last(high - 2, flat, later_2, fields_2, came_2, outs)
    outs = add_last(nx - 2, flat, later_3, fields_3, came_3, outs)
    later, fields = add_last(low + 2 - final, flat, later_3, fields_3, came_4, outs, count - final)
    return (fields.reshape(start_field.shape), later.reshape(start_field.shape))


def solution(mesh):
    placed = (P("gx", "gy", None, "ma"), P("gx", "gy", None, "ma"), P(None, "gx", "gy", None), P())
    return jax.shard_map(
        shards,
        mesh=mesh,
        in_specs=placed,
        out_specs=(P("gx", "gy", None, "ma"), P("gx", "gy", None, "ma")),
        check_vma=False,
    )
```

```python
import functools

import jax
import jax.numpy as jnp
from jax import lax
from jax.experimental import pallas as pl
from jax.experimental.pallas import tpu as pltpu
from jax.sharding import PartitionSpec as P

step_size = 0.02
lanes = 128
group = 2
pad = 8
vmem_bytes = 12 * 1024 * 1024
first_bytes = 60 * 1024 * 1024
f32 = jnp.float32
bf16 = jnp.bfloat16
whole = pl.BlockSpec(memory_space=pltpu.VMEM)
anywhere = pl.BlockSpec(memory_space=pl.ANY)


def call(body, out_shapes, scratch, work=1.0, vmem=vmem_bytes, in_specs=None, out_specs=None, aliases=None, name=None):
    return pl.pallas_call(
        body,
        out_shape=[jax.ShapeDtypeStruct(shape, kind) for shape, kind in out_shapes],
        in_specs=in_specs,
        out_specs=out_specs if out_specs is not None else [whole] * len(out_shapes),
        scratch_shapes=scratch,
        input_output_aliases=aliases or {},
        cost_estimate=pl.CostEstimate(flops=int(work * 1e9), bytes_accessed=int(work * 2e6), transcendentals=0),
        compiler_params=pltpu.CompilerParams(vmem_limit_bytes=vmem),
        name=name,
    )


def sent(array, axis, step, periodic):
    count = lax.axis_size(axis)
    pairs = [(i, (i + step) % count) for i in range(count) if periodic or 0 <= i + step < count]
    return lax.ppermute(array, axis, pairs)


def weights_body(couplings_ref, own_hi, own_lo, other_hi, other_lo, turned):
    half = lax.axis_index("ma")
    modes = own_hi.shape[1] // 2
    for field in range(3):
        mine = couplings_ref[field, pl.ds(pl.multiple_of(half * modes, modes), modes), :]
        theirs = couplings_ref[field, pl.ds(pl.multiple_of((1 - half) * modes, modes), modes), :]
        turned[:, :modes] = mine.T
        turned[:, modes:] = theirs.T
        own = turned[pl.ds(pl.multiple_of(half * modes, modes), modes), :]
        other = turned[pl.ds(pl.multiple_of((1 - half) * modes, modes), modes), :modes]
        rows = pl.ds(field * modes, modes)
        top = own.astype(bf16)
        own_hi[rows, :] = top
        own_lo[rows, :] = (own - top.astype(f32)).astype(bf16)
        top = other.astype(bf16)
        other_hi[rows, :] = top
        other_lo[rows, :] = (other - top.astype(f32)).astype(bf16)


def chosen_body(begin, field, *refs):
    out, sem = refs[-2:]
    copy = pltpu.make_async_copy(field.at[pl.ds(begin, out.shape[0])], out, sem)
    copy.start()
    copy.wait()


def layers_body(depth, field, coef, first_x, last_x, first_y, last_y, near, far, sem):
    planes, rows = field.shape[0], field.shape[1]
    copies = [
        pltpu.make_async_copy(field.at[:, pl.ds(0, pad), :], near, sem.at[0]),
        pltpu.make_async_copy(field.at[:, pl.ds(rows - pad, pad), :], far, sem.at[1]),
        pltpu.make_async_copy(field.at[0], first_x.at[pl.ds(0, rows)], sem.at[2]),
        pltpu.make_async_copy(field.at[planes - 1], last_x.at[pl.ds(0, rows)], sem.at[3]),
    ]
    for copy in copies:
        copy.start()
    for out in (first_x, last_x, first_y, last_y):
        out[rows : rows + coef.shape[0]] = coef[...]
        out[rows + coef.shape[0] :] = jnp.zeros((out.shape[0] - rows - coef.shape[0], lanes), f32)
    for copy in copies:
        copy.wait()
    for plane in range(planes):
        first_y[plane * depth : (plane + 1) * depth] = near[plane, :depth]
        last_y[plane * depth : (plane + 1) * depth] = far[plane, pad - depth :]


def halves_body(coef, halves, square):
    count, rows = coef.shape[0], coef.shape[1]
    square[:count] = 0.5 * coef[...]
    square[count:] = jnp.zeros((lanes - count, rows), f32)
    columns = square[...].T
    planes = count // 3
    for plane in range(planes):
        for field in range(3):
            at = field * planes + plane
            halves[field, plane + 1, pad : pad + rows, :] = jnp.broadcast_to(columns[:, at : at + 1], (rows, lanes))


def around(ref, middle, row, size, depth):
    z = lax.broadcasted_iota(jnp.int32, (size, lanes), 0) % depth
    low = jnp.where(z != 0, ref[middle, row - 1 : row - 1 + size, :], 0.0)
    high = jnp.where(z != depth - 1, ref[middle, row + 1 : row + 1 + size, :], 0.0)
    beside = ref[middle, row - depth : row - depth + size, :] + ref[middle, row + depth : row + depth + size, :]
    return (ref[middle - 1, row : row + size, :] + ref[middle + 1, row : row + size, :]) + (beside + (low + high))


def diagonal_body(depth, low_x, high_x, low_y, high_y, halves_in, halves, diagonal):
    planes, rows = diagonal.shape[1], diagonal.shape[2]
    spread = lambda column, height: jnp.broadcast_to(column, (height, lanes))
    before = (0.5 * low_x[rows:]).T
    after = (0.5 * high_x[rows:]).T
    for field in range(3):
        at = field * planes + planes - 1
        halves[field, 0, pad : pad + rows, :] = spread(before[:, at : at + 1], rows)
        at = field * planes
        halves[field, planes + 1, pad : pad + rows, :] = spread(after[:, at : at + 1], rows)
    below = (0.5 * low_y[rows:]).T[rows - depth :]
    above = (0.5 * high_y[rows:]).T[:depth]
    for plane in range(planes):
        for field in range(3):
            at = field * planes + plane
            halves[field, plane + 1, pad - depth : pad, :] = spread(below[:, at : at + 1], depth)
            halves[field, plane + 1, pad + rows : pad + rows + depth, :] = spread(above[:, at : at + 1], depth)
    size = 32

    def one(plane, _):
        for start in range(0, rows, size):
            row = pad + start
            for field in range(3):
                here = halves[field, plane + 1, row : row + size, :]
                diagonal[field, plane, start : start + size, :] = 6.0 * here + around(halves.at[field], plane + 1, row, size, depth)
        return 0

    lax.fori_loop(0, planes, one, 0)


def weigh(padded, halves, weighed, local, first, count):
    size = (padded.shape[1]) // 3

    def one(i, _):
        for start in range(0, padded.shape[1], size):
            value = padded[local + i, start : start + size, :]
            for field in range(3):
                weighed[field, local + i, start : start + size, :] = halves[field, first + i, start : start + size, :] * value
        return 0

    lax.fori_loop(0, count, one, 0)


def stencil(padded, halves, diagonal, weighed, middle, plane, at, depth, upper, lower):
    size = 32
    rows = padded.shape[1] - 2 * pad
    for start in range(0, rows, size):
        row = pad + start
        here = padded[middle, row : row + size, :]
        total = around(padded, middle, row, size, depth)
        for field in range(3):
            value = diagonal[field, plane, start : start + size, :] * here - halves[field, plane + 1, row : row + size, :] * total
            value = value - around(weighed.at[field], middle, row, size, depth)
            where = slice(at + start, at + start + size), slice(field * lanes, (field + 1) * lanes)
            top = value.astype(bf16)
            upper[where] = top
            lower[where] = (value - top.astype(f32)).astype(bf16)


def operate(depth, count, place, scratch, halves, diagonal, hi, lo, emit):
    padded, weighed, upper_a, lower_a, upper_b, lower_b = scratch
    rows = padded.shape[1] - 2 * pad

    def fill(at, upper, lower):
        for j in range(group):
            middle, plane = place(at + j)
            stencil(padded, halves, diagonal, weighed, middle, plane, j * rows, depth, upper, lower)

    def flush(at, upper, lower):
        big, small = upper[...], lower[...]
        out = jnp.dot(big, hi[...], preferred_element_type=f32)
        out = out + jnp.dot(big, lo[...], preferred_element_type=f32)
        out = out + jnp.dot(small, hi[...], preferred_element_type=f32)
        for j in range(group):
            emit(at + j, out[j * rows : (j + 1) * rows])

    groups = -(-count // group)
    begin = lambda number: jnp.minimum(number * group, count - group)
    fill(0, upper_a, lower_a)

    def one(i, _):
        flush(begin(2 * i), upper_a, lower_a)
        fill(begin(2 * i + 1), upper_b, lower_b)
        flush(begin(2 * i + 1), upper_b, lower_b)
        fill(begin(2 * i + 2), upper_a, lower_a)
        return 0

    lax.fori_loop(0, (groups - 1) // 2, one, 0)
    if groups % 2:
        flush(count - group, upper_a, lower_a)
    else:
        flush((groups - 2) * group, upper_a, lower_a)
        fill(count - group, upper_b, lower_b)
        flush(count - group, upper_b, lower_b)


def strips(padded, local, count, depth, low, high, source, stacked):
    rows = padded.shape[1] - 2 * pad
    for i in range(count):
        at = slice((source + i) * depth, (source + i + 1) * depth) if stacked else source + i
        padded[local + i, pad - depth : pad, :] = low[at]
        padded[local + i, pad + rows : pad + rows + depth, :] = high[at]


def scratch_for(locals_, rows, width):
    padded = pltpu.VMEM((locals_, rows + 2 * pad, lanes), f32)
    weighed = pltpu.VMEM((3, locals_, rows + 2 * pad, lanes), f32)
    return [padded, weighed] + [pltpu.VMEM((group * rows, width), bf16)] * 4 + [pltpu.SemaphoreType.DMA((8,))]


class Run:
    def __init__(self, local, plane, count):
        self.local, self.plane, self.count = local, plane, count


def planes_body(depth, names, outs, pieces, edges, layers, runs, sends, emit, *refs):
    named = dict(zip(names + outs, refs))
    scratch = refs[len(names) + len(outs) :]
    padded, weighed, sem = scratch[0], scratch[1], scratch[-1]
    rows = padded.shape[1] - 2 * pad
    halves, diagonal = named["halves"], named["diagonal"]
    copies = []
    for number, (source, first, count, local) in enumerate(pieces):
        target = padded.at[pl.ds(local, count), pl.ds(pad, rows), :]
        copies.append(pltpu.make_async_copy(named[source].at[pl.ds(first, count)], target, sem.at[number]))
        copies[-1].start()
    for source, local in edges:
        padded[local, pad : pad + rows, :] = named[source][:rows]
    for low, high, first, count, local, stacked in layers:
        strips(padded, local, count, depth, named[low], named[high], first, stacked)
    for copy in copies:
        copy.wait()
    for run in runs:
        weigh(padded, halves, weighed, run.local - 1, run.plane, run.count + 2)
    total = sum(run.count for run in runs)

    def place(i):
        local, plane = i + runs[0].local, i + runs[0].plane
        if len(runs) > 1 and isinstance(i, int):
            run = runs[0] if i < runs[0].count else runs[1]
            return i - (0 if i < runs[0].count else runs[0].count) + run.local, i - (0 if i < runs[0].count else runs[0].count) + run.plane
        if len(runs) > 1:
            later = i >= runs[0].count
            local = jnp.where(later, i - runs[0].count + runs[1].local, local)
            plane = jnp.where(later, i - runs[0].count + runs[1].plane, plane)
        return local, plane

    def put(i, out):
        local, plane = place(i)
        emit(named, i, plane, out, padded, local, rows)

    used = pl.ds(0, 2 * lanes if sends else lanes)
    operate(depth, total, place, scratch[:-1], halves, diagonal, named["hi"].at[:, used], named["lo"].at[:, used], put)
    if "last" in named:
        named["last"][...] = named["residual"][0]
        named["first"][...] = named["residual"][1]


def own_emit(named, i, plane, out, padded, local, rows):
    named["rest"][i] = named["right"][plane] - out


def middle_emit(depth, named, i, plane, out, padded, local, rows):
    value = named["rest"][i] - out
    named["residual"][i] = value
    named["low"][i] = value[:depth]
    named["high"][i] = value[rows - depth :]


def second_emit(split, named, i, plane, out, padded, local, rows):
    here = padded[local, pad : pad + rows, :]
    later = here - step_size * out[:, :lanes]
    fields = named["start"][plane] + step_size * (here + later)
    values = (later, fields, out[:, lanes:])
    named["later"][i], named["fields"][i] = later, fields
    if split is not None and isinstance(i, int) and i >= split:
        named["part2"][i - split] = out[:, lanes:]
    else:
        named["part"][i] = out[:, lanes:]


def over_planes(name, depth, width, operands, outs, pieces, edges, layers, runs, sends, emit, work, ties=()):
    locals_ = max(run.local + run.count + 1 for run in runs)
    operands = dict(operands)
    copied = {piece[0] for piece in pieces} - {edge[0] for edge in edges}
    names = list(operands) + ["tie" + str(number) for number in range(len(ties))]
    rows = operands["diagonal"].shape[2]
    return call(
        functools.partial(planes_body, depth, tuple(names), tuple(outs), pieces, edges, layers, runs, sends, emit),
        [(shape, f32) for shape in outs.values()],
        scratch_for(locals_, rows, width),
        in_specs=[anywhere if key in copied or key.startswith("tie") else whole for key in names],
        work=work,
        name=name,
    )(*operands.values(), *ties)


def sides_body(depth, *refs):
    first, last = refs[-2:]
    planes = refs[0]
    rows = planes.shape[1]
    first[...] = planes[:, :depth, :]
    last[...] = planes[:, rows - depth :, :]


def handed_body(first, last, tie, first_out, last_out):
    first_out[...] = first[...]
    last_out[...] = last[...]


def sides_and_plane_body(depth, which, *refs):
    first, last, plane = refs[-3:]
    planes = refs[0]
    rows = planes.shape[1]
    first[...] = planes[:, :depth, :]
    last[...] = planes[:, rows - depth :, :]
    plane[...] = planes[which]


def last_body(first, skip, later_part, fields_part, came, *refs):
    later, fields, staged, sem = refs[-4:]
    count = came.shape[0]
    planes = later.shape[0]
    piece = 2
    copies = []
    for begin in range(0, count, piece):
        end = min(begin + piece, count)
        for at in range(begin, end):
            staged[0, at] = later_part[skip + at] - step_size * came[at]
            staged[1, at] = fields_part[skip + at] - (step_size * step_size) * came[at]
        wrap = max(begin, min(end, planes - first))
        for which, target in ((0, later), (1, fields)):
            for low, high in ((begin, wrap), (wrap, end)):
                if high > low:
                    goal = (first + low) % planes
                    copy = pltpu.make_async_copy(
                        staged.at[which, pl.ds(low, high - low)], target.at[pl.ds(goal, high - low)], sem.at[len(copies)]
                    )
                    copy.start()
                    copies.append(copy)
    for copy in copies:
        copy.wait()


def add_last(first, shape, later_part, fields_part, came, before, skip=0):
    count = came.shape[0]
    return call(
        functools.partial(last_body, first, skip),
        [(shape, f32)] * 2,
        [pltpu.VMEM((2,) + came.shape, f32), pltpu.SemaphoreType.DMA((2 * count + 4,))],
        in_specs=[whole] * 3 + [anywhere] * len(before),
        out_specs=[anywhere] * 2,
        aliases={3: 0, 4: 1} if before else {},
        work=0.2,
        name="last",
    )(later_part, fields_part, came, *before)


def shards(right_side, start_field, coefficients, couplings):
    nx, ny, depth, modes = start_field.shape
    rows = ny * depth
    plane = (rows, modes)
    flat = (nx,) + plane
    start = start_field.reshape(flat)
    right = right_side.reshape(flat)
    low, high = (3 * nx) // 16, (5 * nx) // 8
    width = 3 * modes
    strip = lambda count: ((count, depth, modes), f32)

    def chosen(begin, count, name, *ties):
        (out,) = call(
            functools.partial(chosen_body, begin),
            [((count,) + plane, f32)],
            [pltpu.SemaphoreType.DMA],
            in_specs=[anywhere] * (1 + len(ties)),
            name=name,
        )(start, *ties)
        return sent(out, "ma", 1, True)

    raw_1 = sent(lax.slice_in_dim(start, low, high, axis=0), "ma", 1, True)

    coef = coefficients.reshape(3 * nx, rows)
    layer = ((rows + lanes, lanes), f32)
    first_x, last_x, first_y, last_y = call(
        functools.partial(layers_body, depth),
        [layer] * 4,
        [pltpu.VMEM((nx, pad, lanes), f32)] * 2 + [pltpu.SemaphoreType.DMA((4,))],
        in_specs=[anywhere, whole],
        vmem=first_bytes,
        name="layers",
    )(start, coef)
    low_y = sent(last_y, "gy", 1, True)
    high_y = sent(first_y, "gy", -1, True)
    low_x = sent(last_x, "gx", 1, False)
    high_x = sent(first_x, "gx", -1, False)

    own_hi, own_lo, other_hi, other_lo = call(
        weights_body,
        [((width, 2 * modes), bf16)] * 2 + [((width, modes), bf16)] * 2,
        [pltpu.VMEM((2 * modes, 2 * modes), f32)],
        in_specs=[whole],
        name="weights",
    )(couplings)

    halves_shape = (3, nx + 2, rows + 2 * pad, lanes)
    (halves,) = call(halves_body, [(halves_shape, f32)], [pltpu.VMEM((lanes, rows), f32)], in_specs=[whole], name="halves")(coef)
    halves, diagonal = call(
        functools.partial(diagonal_body, depth),
        [(halves_shape, f32), ((3,) + flat, f32)],
        [],
        in_specs=[whole] * 5,
        aliases={4: 0},
        name="diagonal",
    )(low_x, high_x, low_y, high_y, halves)
    shared = {"halves": halves, "diagonal": diagonal}
    mine = {**shared, "hi": own_hi, "lo": own_lo}
    theirs = {**shared, "hi": other_hi, "lo": other_lo}
    raw_2 = chosen(high, nx - high, "chosen_2", own_hi, diagonal)

    n1, n2, n3 = high - low - 2, nx - high, low + 2
    ring = [Run(1, nx - 1, 1), Run(4, 0, low + 1)]

    def own(name, count, pieces, edges, layers, runs, ties=()):
        operands = {**mine, "start": start, "right": right, "low_y": low_y, "high_y": high_y, "low_x": low_x, "high_x": high_x}
        outs = {"rest": (count,) + plane}
        return over_planes(name, depth, width, operands, outs, pieces, edges, layers, runs, False, own_emit, count / 10, ties)[0]

    rest_1 = own(
        "own_1", n1, [("start", low, n1 + 2, 0)], [], [("low_y", "high_y", low + 1, n1, 1, True)], [Run(1, low + 1, n1)]
    )
    raw_3 = chosen(0, low, "chosen_3", rest_1)

    def sides(chunk, which, name, *ties):
        count = chunk.shape[0]
        body = functools.partial(sides_body, depth) if which is None else functools.partial(sides_and_plane_body, depth, which)
        return call(
            body,
            [strip(count)] * 2 + ([] if which is None else [(plane, f32)]),
            [],
            in_specs=[whole] + [anywhere] * len(ties),
            work=0.1,
            name=name,
        )(chunk, *ties)

    def exchanged(first, last):
        return sent(last, "gy", 1, True), sent(first, "gy", -1, True)

    def middle(name, count, operands, pieces, edges, layers, runs, with_edges, ties=()):
        outs = {"residual": (count,) + plane, "low": (count, depth, modes), "high": (count, depth, modes)}
        if with_edges:
            outs.update({"last": plane, "first": plane})
        emit = functools.partial(middle_emit, depth)
        return over_planes(name, depth, width, {**theirs, **operands}, outs, pieces, edges, layers, runs, False, emit, count / 10, ties)

    def second(name, counts, operands, pieces, edges, layers, runs, ties=(), work=1.0):
        outs = {key: (sum(counts),) + plane for key in ("later", "fields")}
        outs["part"] = (counts[0],) + plane
        if len(counts) > 1:
            outs["part2"] = (counts[1],) + plane
        emit = functools.partial(second_emit, counts[0] if len(counts) > 1 else None)
        operands = {**mine, "start": start, **operands}
        return over_planes(name, depth, width, operands, outs, pieces, edges, layers, runs, True, emit, work, ties)

    sides_1 = sides(raw_1, None, "sides_1", rest_1)
    raw_low_1, raw_high_1 = exchanged(*sides_1)
    rest_2 = own(
        "own_2",
        n2,
        [("start", high - 2, n2 + 2, 0)],
        [],
        [("low_y", "high_y", high - 1, n2, 1, True)],
        [Run(1, high - 1, n2)],
        (sides_1[0],),
    )
    residual_1, first_1, last_1 = middle(
        "middle_1",
        n1,
        {"rest": rest_1, "raw_1": raw_1, "low_1": raw_low_1, "high_1": raw_high_1},
        [("raw_1", 0, n1 + 2, 0)],
        [],
        [("low_1", "high_1", 1, n1, 1, False)],
        [Run(1, low + 1, n1)],
        False,
        (rest_2,),
    )
    low_1, high_1 = exchanged(first_1, last_1)
    rest_3 = own(
        "own_3",
        n3,
        [("start", nx - 2, 2, 0), ("start", 0, low + 2, 4)],
        [("high_x", 2), ("low_x", 3)],
        [("low_y", "high_y", nx - 1, 1, 1, True), ("low_y", "high_y", 0, low + 1, 4, True)],
        ring,
        (first_1,),
    )
    later_1, fields_1, part_1 = second(
        "second_1",
        [n1 - 2],
        {"residual_1": residual_1, "low_1": low_1, "high_1": high_1},
        [("residual_1", 0, n1, 0)],
        [],
        [("low_1", "high_1", 1, n1 - 2, 1, False)],
        [Run(1, low + 2, n1 - 2)],
        (rest_3,),
    )
    came_1 = sent(part_1, "ma", 1, True)

    sides_2 = sides(raw_2, nx - high - 1, "sides_2", part_1)
    raw_low_2, raw_high_2 = exchanged(sides_2[0], sides_2[1])
    raw_low_x = sent(sides_2[2], "gx", 1, False)
    residual_2, first_2, last_2 = middle(
        "middle_2",
        n2,
        {"rest": rest_2, "raw_1": raw_1, "raw_2": raw_2, "low_1": raw_low_1, "high_1": raw_high_1, "low_2": raw_low_2, "high_2": raw_high_2},
        [("raw_1", high - low - 2, 2, 0), ("raw_2", 0, n2, 2)],
        [],
        [("low_1", "high_1", high - low - 1, 1, 1, False), ("low_2", "high_2", 0, n2 - 1, 2, False)],
        [Run(1, high - 1, n2)],
        False,
    )
    low_2, high_2 = exchanged(first_2, last_2)

    sides_3 = sides(raw_3, 0, "sides_3", first_2)
    raw_low_3, raw_high_3 = exchanged(sides_3[0], sides_3[1])
    raw_high_x = sent(sides_3[2], "gx", -1, False)
    later_2, fields_2, part_2 = second(
        "second_2",
        [n2],
        {"residual_1": residual_1, "residual_2": residual_2, "low_1": low_1, "high_1": high_1, "low_2": low_2, "high_2": high_2},
        [("residual_1", n1 - 2, 2, 0), ("residual_2", 0, n2, 2)],
        [],
        [("low_1", "high_1", n1 - 1, 1, 1, False), ("low_2", "high_2", 0, n2 - 1, 2, False)],
        [Run(1, high - 2, n2)],
        (sides_3[0], raw_low_x),
        4.0,
    )
    came_2 = sent(part_2, "ma", 1, True)
    residual_3, first_3, last_3, edge_last, edge_first = middle(
        "middle_3",
        n3,
        {
            "rest": rest_3,
            "raw_1": raw_1,
            "raw_2": raw_2,
            "raw_3": raw_3,
            "low_x": raw_low_x,
            "high_x": raw_high_x,
            "low_1": raw_low_1,
            "high_1": raw_high_1,
            "low_2": raw_low_2,
            "high_2": raw_high_2,
            "low_3": raw_low_3,
            "high_3": raw_high_3,
        },
        [("raw_2", n2 - 2, 2, 0), ("raw_3", 0, low, 4), ("raw_1", 0, 2, 4 + low)],
        [("high_x", 2), ("low_x", 3)],
        [("low_2", "high_2", n2 - 1, 1, 1, False), ("low_3", "high_3", 0, low, 4, False), ("low_1", "high_1", 0, 1, 4 + low, False)],
        ring,
        True,
        (part_2,),
    )
    next_low_x = sent(edge_last, "gx", 1, False)
    next_high_x = sent(edge_first, "gx", -1, False)
    low_3, high_3 = exchanged(
        *call(
            handed_body,
            [strip(n3)] * 2,
            [],
            in_specs=[whole] * 2 + [anywhere],
            work=0.1,
            name="handed",
        )(first_3, last_3, came_1)
    )
    final = 2 * group if -(-(low + 4) // group) % 2 == 0 else group
    count = low + 4
    later_3, fields_3, part_3, part_4 = second(
        "second_3",
        [count - final, final],
        {
            "residual_1": residual_1,
            "residual_2": residual_2,
            "residual_3": residual_3,
            "low_x": next_low_x,
            "high_x": next_high_x,
            "low_1": low_1,
            "high_1": high_1,
            "low_2": low_2,
            "high_2": high_2,
            "low_3": low_3,
            "high_3": high_3,
        },
        [("residual_2", n2 - 2, 2, 0), ("residual_3", 0, 1, 2), ("residual_3", 1, low + 1, 5), ("residual_1", 0, 2, 6 + low)],
        [("high_x", 3), ("low_x", 4)],
        [
            ("low_2", "high_2", n2 - 1, 1, 1, False),
            ("low_3", "high_3", 0, 1, 2, False),
            ("low_3", "high_3", 1, low + 1, 5, False),
            ("low_1", "high_1", 0, 1, 6 + low, False),
        ],
        [Run(1, nx - 2, 2), Run(5, 0, low + 2)],
        (came_1,),
        2.0,
    )
    came_3 = sent(part_3, "ma", 1, True)
    came_4 = sent(part_4, "ma", 1, True)

    outs = add_last(low + 2, flat, later_1, fields_1, came_1, ())
    outs = add_last(high - 2, flat, later_2, fields_2, came_2, outs)
    outs = add_last(nx - 2, flat, later_3, fields_3, came_3, outs)
    later, fields = add_last(low + 2 - final, flat, later_3, fields_3, came_4, outs, count - final)
    return (fields.reshape(start_field.shape), later.reshape(start_field.shape))


def solution(mesh):
    placed = (P("gx", "gy", None, "ma"), P("gx", "gy", None, "ma"), P(None, "gx", "gy", None), P())
    return jax.shard_map(
        shards,
        mesh=mesh,
        in_specs=placed,
        out_specs=(P("gx", "gy", None, "ma"), P("gx", "gy", None, "ma")),
        check_vma=False,
    )
```
